32 devices in a mesh: dp: 4 (over y, core), tensor: 8 (over z, x).
Axes of the slice: x: 2, y: 2, z: 4, core: 2. Of those that a mesh axis runs over, the one named last changes fastest.
Arguments:
- tokens: bfloat16 [1024, 8, 1024], P('tensor', 'dp'), may hold values from -6 to 6
- conditioning: bfloat16 [8, 1024], P('dp'), may hold values from -6 to 6
- cotangent: bfloat16 [1024, 8, 1024], P('tensor', 'dp'), may hold values from -6 to 6
- w_qkv: bfloat16 [1024, 16, 192], P('dp', 'tensor'), may hold values from -0.1875 to 0.1875
- b_qkv: bfloat16 [2, 1024], P(None, 'dp'), may hold values from -3 to 3
- w_proj: bfloat16 [1024, 1024], P('tensor', 'dp'), may hold values from -1.5 to 1.5
- b_proj: bfloat16 [1024], P('dp'), may hold values from -3 to 3
- w_fc1: bfloat16 [1024, 4096], P('dp', 'tensor'), may hold values from -0.1875 to 0.1875
- b_fc1: bfloat16 [4096], P('dp'), may hold values from -3 to 3
- w_fc2: bfloat16 [4096, 1024], P('tensor', 'dp'), may hold values from -0.09375 to 0.09375
- b_fc2: bfloat16 [1024], P('dp'), may hold values from -3 to 3
- w_ada: bfloat16 [1024, 6144], P('dp'), may hold values from -0.1875 to 0.1875
- b_ada: bfloat16 [6144], P('dp'), may hold values from -3 to 3
Outputs:
- output: bfloat16 [1024, 8, 1024], P('tensor', 'dp')
- d_tokens: float32 [1024, 8, 1024], P('tensor', 'dp')
- d_conditioning: float32 [8, 1024], P('dp')
- grad_w_qkv: float32 [1024, 16, 192], P('dp', 'tensor')
- grad_b_qkv: float32 [2, 1024], P(None, 'dp')
- grad_w_proj: float32 [1024, 1024], P('tensor', 'dp')
- grad_b_proj: float32 [1024], P('dp')
- grad_w_fc1: float32 [1024, 4096], P('dp', 'tensor')
- grad_b_fc1: float32 [4096], P('dp')
- grad_w_fc2: float32 [4096, 1024], P('tensor', 'dp')
- grad_b_fc2: float32 [1024], P('dp')
- grad_w_ada: float32 [1024, 6144], P('dp', 'tensor')
- grad_b_ada: float32 [6144], P('dp')
The draws below stay inside these ranges and needn't reach their ends.
All inputs are finite; a program needn't handle non-finite values.
Results may differ from the reference program's by a relative error of at most 0.012.
The reference program's roundings to bfloat16 on the way count: a program that leaves them out, or rounds other values in their place, can miss the bound.
Values may be sent and summed in bfloat16 or wider, within the bound.
No kernel may reach another device: no remote copies, remote signals or barrier semaphores. Data moves between devices by JAX's collectives and lax.ppermute only.
A program may use at most 192 MiB of HBM per device.

```python
import jax
import jax.numpy as jnp
from jax import lax

D = 1024
H = 16
HD = 64
FF = 4096
SEQ = 1024
SEQS = 1
SAMPLES = 8


def level_of(rng, shape, pieces, least, largest):
    def one(dim, blocks):
        draws = jax.random.uniform(jax.random.fold_in(jax.random.fold_in(rng, 6), dim), (blocks,), jnp.float32, least / len(pieces), largest / len(pieces))
        return jnp.repeat(jnp.exp(draws), shape[dim] // blocks).reshape((-1,) + (1,) * (len(shape) - dim - 1))

    factor_of = one(*pieces[0])
    for cut in pieces[1:]:
        factor_of = factor_of * one(*cut)
    return factor_of


def gaussian(rng, extent, deviation, reach, cuts=(), held_as=jnp.bfloat16):
    drawn = jax.random.normal(rng, extent, jnp.float32) * deviation
    if len(cuts) > 0:
        drawn = level_of(rng, extent, cuts, -0.22, 0.18) * drawn
    return jnp.clip(drawn, min=-reach, max=reach).astype(held_as)


def setup_inputs(seed: int = 0) -> dict:
    key_of = jax.random.split(jax.random.key(seed), 14)
    return {
        "tokens": gaussian(key_of[0], (SEQ, SAMPLES, D), 1.0, 6.0, ((0, 8), (1, 4))),
        "conditioning": gaussian(key_of[1], (SAMPLES, D), 1.0, 6.0, ((0, 4),)),
        "cotangent": gaussian(key_of[2], (SEQ, SAMPLES, D), 1.0, 6.0, ((0, 8), (1, 4))),
        "w_qkv": gaussian(key_of[3], (D, H, 3 * HD), D ** -0.5, 0.1875, ((0, 4), (1, 8))),
        "b_qkv": gaussian(key_of[4], (2, D), 0.5, 3.0, ((1, 4),)),
        "w_proj": gaussian(key_of[5], (D, D), (D * 16 // SEQ) ** -0.5, 1.5, ((0, 8), (1, 4))),
        "b_proj": gaussian(key_of[6], (D,), 0.5, 3.0, ((0, 4),)),
        "w_fc1": gaussian(key_of[7], (D, FF), D ** -0.5, 0.1875, ((0, 4), (1, 8))),
        "b_fc1": gaussian(key_of[8], (FF,), 0.5, 3.0, ((0, 4),)),
        "w_fc2": gaussian(key_of[9], (FF, D), FF ** -0.5, 0.09375, ((0, 8), (1, 4))),
        "b_fc2": gaussian(key_of[10], (D,), 0.5, 3.0, ((0, 4),)),
        "w_ada": gaussian(key_of[11], (D, 6 * D), D ** -0.5, 0.1875, ((0, 4),)),
        "b_ada": gaussian(key_of[12], (6 * D,), 0.5, 3.0, ((0, 4),)),
    }


@jax.custom_vjp
def low(v):
    return lax.optimization_barrier(v.astype(jnp.bfloat16)).astype(jnp.float32)

@jax.custom_vjp
def low_back(v):
    return v

def low_keep(v):
    return (low(v), None)

def low_pass(kept, grad):
    return (grad,)

def back_keep(v):
    return (v, None)

def back_low(kept, grad):
    return (low(grad),)
low.defvjp(low_keep, low_pass)
low_back.defvjp(back_keep, back_low)
highest = lax.Precision.HIGHEST
norm_eps = 1e-06

def round_both(block_inputs):
    return low(low_back(block_inputs))

def norm_rows(block_inputs):
    center = block_inputs - lax.optimization_barrier(jnp.mean(block_inputs, axis=-1, keepdims=True))
    return center * lax.rsqrt(lax.optimization_barrier(jnp.mean(center * center, axis=-1, keepdims=True)) + norm_eps)

def attend(queries, key_heads, val_heads):
    block_rows = min(512, SEQ)
    block_count = SEQ // block_rows
    blocks = queries.reshape((block_count, block_rows) + queries.shape[1:])
    factor = HD ** (-0.5)

    def one_block(qblock):
        scores = low_back(jnp.einsum('qghe,kghe->ghqk', qblock, key_heads, precision=highest) * factor)
        attn_probs = low(jax.nn.softmax(scores, axis=-1))
        return jnp.einsum('ghqk,kghe->qghe', attn_probs, val_heads, precision=highest)
    return lax.map(jax.checkpoint(one_block), blocks).reshape(queries.shape)

def diffusion_transformer_block(block_parameters, block_inputs, condition_rows):
    w_qkv, b_qkv, w_proj, b_proj, w_fc1, b_fc1, w_fc2, b_fc2, w_ada, b_ada = block_parameters
    samples = block_inputs.shape[1]
    act_cond = low(jax.nn.silu(condition_rows))
    modulation = (jnp.dot(act_cond, w_ada, precision=highest) + b_ada).reshape(samples, 6, D)
    shift_attn, scale_attn, gate_attn = (modulation[:, 0], modulation[:, 1], modulation[:, 2])
    shift_mlp, scale_mlp, gate_mlp = (modulation[:, 3], modulation[:, 4], modulation[:, 5])
    normed = low(norm_rows(block_inputs) * (1.0 + scale_attn) + shift_attn)
    packed = jnp.einsum('sgd,dhe->sghe', normed, w_qkv, precision=highest)
    queries = round_both(packed[..., :HD] + b_qkv[0].reshape(H, HD))
    key_heads = round_both(packed[..., HD:2 * HD])
    val_heads = round_both(packed[..., 2 * HD:] + b_qkv[1].reshape(H, HD))
    attn_mixed = round_both(attend(queries, key_heads, val_heads)).reshape(block_inputs.shape)
    branch = low_back(jnp.einsum('sgd,de->sge', attn_mixed, w_proj, precision=highest) + b_proj)
    middle = block_inputs + gate_attn * branch
    normed_mlp = low(norm_rows(middle) * (1.0 + scale_mlp) + shift_mlp)
    hidden = low_back(jnp.einsum('sgd,df->sgf', normed_mlp, w_fc1, precision=highest) + b_fc1)
    activated = low(jax.nn.gelu(hidden, approximate=True))
    branch_mlp = low_back(jnp.einsum('sgf,fd->sgd', activated, w_fc2, precision=highest) + b_fc2)
    return middle + gate_mlp * branch_mlp

def reference(tokens, conditioning, cotangent, w_qkv, b_qkv, w_proj, b_proj, w_fc1, b_fc1, w_fc2, b_fc2, w_ada, b_ada):
    block_parameters = tuple((weight_arg.astype(jnp.float32) for weight_arg in (w_qkv, b_qkv, w_proj, b_proj, w_fc1, b_fc1, w_fc2, b_fc2, w_ada, b_ada)))
    groups = tokens.shape[1] // SEQS

    def regroup(array):
        return array.astype(jnp.float32).reshape(SEQ, groups, SEQS, D).transpose(1, 0, 2, 3)

    def unsplit(array):
        return array.transpose(1, 0, 2, 3).reshape(SEQ, groups * SEQS, D)
    stacked = (regroup(tokens), conditioning.astype(jnp.float32).reshape(groups, SEQS, D), regroup(cotangent))

    def scan_step(totals, group_items):
        block_inputs, condition_rows, grad_rows = group_items
        block_result, backward_function = jax.vjp(diffusion_transformer_block, block_parameters, block_inputs, condition_rows)
        dparams, dinputs, cond_grad = backward_function(grad_rows)
        return (jax.tree.map(jnp.add, totals, dparams), (block_result, dinputs, cond_grad))
    zero_grads = jax.tree.map(jnp.zeros_like, block_parameters)
    totals, (results, dinputs, cond_grads) = lax.scan(scan_step, zero_grads, stacked)
    g_qkv, g_bqkv, g_proj, g_bproj, g_fc1, g_bfc1, g_fc2, g_bfc2, g_ada, g_bada = totals
    return (unsplit(results).astype(jnp.bfloat16), unsplit(dinputs), cond_grads.reshape(groups * SEQS, D), g_qkv, g_bqkv, g_proj, g_bproj, g_fc1, g_bfc1, g_fc2, g_bfc2, g_ada, g_bada)
```

```python
import jax
import jax.numpy as jnp
from jax import lax
from jax.sharding import Mesh, PartitionSpec as P

HD = 64
NZ = 4
NC = 2
norm_eps = 1e-06
f32 = jnp.float32
bf16 = jnp.bfloat16


def flip_bits(array, axis, count, index):
    bit = 1
    while bit < count:
        shape = array.shape
        view = array.reshape(
            shape[:axis] + (count // (2 * bit), 2, bit) + shape[axis + 1 :]
        )
        swapped = jnp.flip(view, axis=axis + 1)
        on = ((index // bit) % 2) == 1
        array = jnp.where(on, swapped, view).reshape(shape)
        bit *= 2
    return array


def swap_with(array, axis_name, count, offset):
    return lax.ppermute(array, axis_name, [(i, i ^ offset) for i in range(count)])


def layer_stats(rows):
    center = rows - jnp.mean(rows, axis=-1, keepdims=True)
    scale = lax.rsqrt(jnp.mean(center * center, axis=-1, keepdims=True) + norm_eps)
    return center * scale, scale


def layer_back(grad, unit, scale):
    return scale * (
        grad
        - jnp.mean(grad, axis=-1, keepdims=True)
        - unit * jnp.mean(grad * unit, axis=-1, keepdims=True)
    )


def split_three(values):
    high = lax.reduce_precision(values, 8, 7)
    rest = values - high
    middle = lax.reduce_precision(rest, 8, 7)
    return [part.astype(bf16) for part in (high, middle, rest - middle)]


def dot(a, b, dims):
    return lax.dot_general(a, b, (dims, ((), ())), preferred_element_type=f32)


def attn_forward(queries, keys, values, factor):
    samples, rows, width = queries.shape
    heads = width // HD
    qh = queries.reshape(samples, rows, heads, HD)
    kh = keys.reshape(samples, keys.shape[1], heads, HD)
    vh = values.reshape(samples, keys.shape[1], heads, HD)
    scores = jnp.einsum("sqhe,skhe->shqk", qh, kh, preferred_element_type=f32) * factor
    top = jnp.max(scores, axis=-1, keepdims=True)
    exps = jnp.exp(scores - top)
    total = jnp.sum(exps, axis=-1, keepdims=True)
    probs = (exps / total).astype(bf16)
    mixed = jnp.einsum("shqk,skhe->sqhe", probs, vh, preferred_element_type=f32)
    return mixed.reshape(queries.shape).astype(bf16), (top + jnp.log(total))


def attn_backward(queries, keys, values, grads, log_norm, factor):
    samples, rows, width = queries.shape
    heads = width // HD
    qh = queries.reshape(samples, rows, heads, HD)
    gh = grads.reshape(samples, rows, heads, HD)
    kh = keys.reshape(samples, keys.shape[1], heads, HD)
    vh = values.reshape(samples, keys.shape[1], heads, HD)
    scores = jnp.einsum("sqhe,skhe->shqk", qh, kh, preferred_element_type=f32) * factor
    probs = jnp.exp(scores - log_norm)
    dprobs = jnp.einsum("sqhe,skhe->shqk", gh, vh, preferred_element_type=f32)
    delta = jnp.sum(probs * dprobs, axis=-1, keepdims=True)
    dscores = (probs * (dprobs - delta)).astype(bf16)
    dq = jnp.einsum("shqk,skhe->sqhe", dscores, kh, preferred_element_type=f32) * factor
    dk = jnp.einsum("shqk,sqhe->skhe", dscores, qh, preferred_element_type=f32) * factor
    dv = jnp.einsum("shqk,sqhe->skhe", probs.astype(bf16), gh, preferred_element_type=f32)
    return dq.reshape(queries.shape), dk.reshape(keys.shape), dv.reshape(keys.shape)


def make_body(ny, nx):
    def to_cores(k):
        return [
            (c * NZ + z, (z // 2) * NZ + c * 2 + ((z % 2) ^ k))
            for c in range(NC)
            for z in range(NZ)
        ]

    def body(
        tokens,
        conditioning,
        cotangent,
        w_qkv,
        b_qkv,
        w_proj,
        b_proj,
        w_fc1,
        b_fc1,
        w_fc2,
        b_fc2,
        w_ada,
        b_ada,
    ):
        y, c = lax.axis_index("y"), lax.axis_index("c")
        z, x = lax.axis_index("z"), lax.axis_index("x")
        z0, z1 = z % 2, z // 2
        place, ns, D = tokens.shape
        q = ns // 2
        L = 2 * place
        dp = ny * NC
        B = D // dp
        own = y * NC + c
        hpt = w_qkv.shape[1]
        HW = hpt * HD
        F = w_fc1.shape[1]
        FF = F * NZ * nx
        factor = HD ** (-0.5)

        def rel(array):
            shape = array.shape
            view = array.reshape(shape[:-1] + (ny, NC, B))
            view = flip_bits(view, len(shape) - 1, ny, y)
            view = flip_bits(view, len(shape), NC, c)
            return view.reshape(shape)

        def spread(array):
            view = array.reshape(place, 2, q, D)
            first = jnp.where(z0 == 0, view[:, 0], view[:, 1])
            second = jnp.where(z0 == 0, view[:, 1], view[:, 0])
            got = [
                lax.ppermute(piece, ("c", "z"), to_cores(k))
                for k, piece in enumerate((first, second))
            ]
            return jnp.concatenate([g.transpose(1, 0, 2) for g in got], axis=1)

        def collect(array):
            pieces = [
                array[:, k * place : (k + 1) * place].transpose(1, 0, 2) for k in range(2)
            ]
            got = [
                lax.ppermute(piece, ("c", "z"), [(b, a) for a, b in to_cores(k)])
                for k, piece in enumerate(pieces)
            ]
            first = jnp.where(z0 == 0, got[0], got[1])
            second = jnp.where(z0 == 0, got[1], got[0])
            return jnp.stack([first, second], axis=1).reshape(place, ns, D)

        def gather_x(array):
            return jnp.stack(
                [array] + [swap_with(array, "x", nx, k) for k in range(1, nx)]
            )

        def reduce_x(parts):
            total = parts[0]
            for k in range(1, nx):
                total = total + swap_with(parts[k].astype(bf16), "x", nx, k).astype(f32)
            return total

        def gather_w(shard, by_rows):
            along = 1 if by_rows else 0
            over_z = jnp.concatenate(
                [shard] + [swap_with(shard, "z", NZ, k) for k in range(1, NZ)], axis=along
            )
            over_y = jnp.stack(
                [over_z] + [swap_with(over_z, "y", ny, k) for k in range(1, ny)]
            )
            other = swap_with(over_y, "c", NC, 1)
            if by_rows:
                return jnp.stack([over_y, other], axis=1).reshape(D, shard.shape[1] * NZ)
            pieces = [p for k in range(ny) for p in (over_y[k], other[k])]
            return jnp.concatenate(pieces, axis=1)

        def reduce_w(grad, by_rows):
            if by_rows:
                view = grad.reshape(ny, NC, B, NZ, grad.shape[1] // NZ)
                part = lambda ky, kc, kz: view[ky, kc, :, kz]
            else:
                view = grad.reshape(NZ, grad.shape[0] // NZ, ny, NC, B)
                part = lambda ky, kc, kz: view[kz, :, ky, kc]
            pick = lambda kc: jnp.stack(
                [jnp.stack([part(ky, kc, kz) for kz in range(NZ)]) for ky in range(ny)]
            )
            got = swap_with(pick(1).astype(bf16), "c", NC, 1)
            over_c = pick(0) + got.astype(f32)
            over_y = over_c[0]
            for k in range(1, ny):
                over_y = over_y + swap_with(over_c[k].astype(bf16), "y", ny, k).astype(f32)
            over_z = over_y[0]
            for k in range(1, NZ):
                over_z = over_z + swap_with(over_y[k].astype(bf16), "z", NZ, k).astype(f32)
            return over_z

        cond_c = jnp.stack([conditioning, swap_with(conditioning, "c", NC, 1)])
        cond_c = flip_bits(cond_c, 0, NC, c)
        cond_all = jnp.stack([cond_c] + [swap_with(cond_c, "y", ny, k) for k in range(1, ny)])
        cond_all = flip_bits(cond_all.reshape(ny, NZ, q, D), 1, NZ, z)
        act_all = jax.nn.silu(cond_all.astype(f32)).astype(bf16)
        act_rows = lax.dynamic_slice_in_dim(act_all, own * B, B, 3)

        partial_mod = dot(act_rows[:, 0].reshape(ny * q, B), w_ada, ((1,), (0,)))
        pad = lambda v, n: lax.dynamic_update_slice_in_dim(
            jnp.zeros((n,), f32), v.astype(f32), own * v.shape[0], 0
        )
        partial_mod = partial_mod + pad(b_ada, 6 * D)
        bias_vec = jnp.concatenate(
            [pad(b_qkv[0], D), pad(b_qkv[1], D), pad(b_proj, D), pad(b_fc1, FF), pad(b_fc2, D)]
        )
        partial_mod = partial_mod.reshape(ny, q * 6 * D)
        packed_mod = jnp.concatenate(
            [partial_mod, jnp.broadcast_to(bias_vec, (ny,) + bias_vec.shape)], axis=1
        )
        total_mod = packed_mod[0]
        for k in range(1, ny):
            total_mod = total_mod + swap_with(packed_mod[k], "y", ny, k)
        total_mod = total_mod + swap_with(total_mod, "c", NC, 1)
        modulation = rel(total_mod[: q * 6 * D].reshape(q, 6, 1, D))
        biases = total_mod[q * 6 * D :]
        bias_heads = biases[: 2 * D].reshape(2, NZ, nx, HW)
        bias_heads = lax.dynamic_index_in_dim(bias_heads, x, 2, keepdims=False)
        bias_heads = flip_bits(bias_heads, 1, NZ, z).reshape(2, NZ * HW)
        bias_proj = rel(biases[2 * D : 3 * D])
        bias_fc1 = biases[3 * D : 3 * D + FF].reshape(NZ, nx, F)
        bias_fc1 = lax.dynamic_index_in_dim(bias_fc1, x, 1, keepdims=False)
        bias_fc1 = flip_bits(bias_fc1, 0, NZ, z).reshape(NZ * F)
        bias_fc2 = rel(biases[3 * D + FF :])
        shift_attn, scale_attn, gate_attn, shift_mlp, scale_mlp, gate_mlp = (
            modulation[:, i] for i in range(6)
        )

        block_in = rel(spread(tokens)).astype(f32)
        w_heads = w_qkv.reshape(B, hpt, 3, HD).transpose(0, 2, 1, 3).reshape(B, 3 * HW)
        full_qkv = gather_w(w_heads, True)
        full_proj = gather_w(w_proj, False)
        full_fc1 = gather_w(w_fc1, True)
        full_fc2 = gather_w(w_fc2, False)
        grad_top = rel(spread(cotangent)).astype(f32)

        unit_in, rstd_in = layer_stats(block_in)
        normed = (unit_in * (1.0 + scale_attn) + shift_attn).astype(bf16)
        normed_all = gather_x(normed).reshape(nx * q * L, D)
        T = nx * q * L
        packed = dot(normed_all, full_qkv, ((1,), (0,))).reshape(T, NZ, 3, HW)
        queries = (packed[:, :, 0].reshape(T, NZ * HW) + bias_heads[0]).astype(bf16)
        keys = packed[:, :, 1].reshape(T, NZ * HW).astype(bf16)
        vals = (packed[:, :, 2].reshape(T, NZ * HW) + bias_heads[1]).astype(bf16)

        def by_sample(array):
            return array.reshape(nx, q, L, -1).transpose(1, 0, 2, 3).reshape(q, nx * L, -1)

        def by_rank(array):
            return array.reshape(q, nx, L, -1).transpose(1, 0, 2, 3).reshape(T, -1)

        queries, keys, vals = by_sample(queries), by_sample(keys), by_sample(vals)
        key_vals = jnp.stack([keys, vals])
        other_kv = swap_with(key_vals, "c", NC, 1)
        keys_all = jnp.concatenate([keys, other_kv[0]], axis=1)
        vals_all = jnp.concatenate([vals, other_kv[1]], axis=1)
        mixed, log_norm = attn_forward(queries, keys_all, vals_all, factor)
        mixed_rows = by_rank(mixed)
        branch_part = dot(mixed_rows, full_proj, ((1,), (0,))).reshape(nx, q, L, D)
        branch = reduce_x(branch_part) + bias_proj
        middle = block_in + gate_attn * branch
        unit_mid, rstd_mid = layer_stats(middle)
        normed_mlp = (unit_mid * (1.0 + scale_mlp) + shift_mlp).astype(bf16)
        mlp_all = gather_x(normed_mlp).reshape(T, D)
        hidden = dot(mlp_all, full_fc1, ((1,), (0,))) + bias_fc1
        activated, gelu_pull = jax.vjp(lambda h: jax.nn.gelu(h, approximate=True), hidden)
        act_low = activated.astype(bf16)
        mlp_part = dot(act_low, full_fc2, ((1,), (0,))).reshape(nx, q, L, D)
        branch_mlp = reduce_x(mlp_part) + bias_fc2
        block_out = (middle + gate_mlp * branch_mlp).astype(bf16)
        out = collect(rel(block_out))

        dgate_mlp = jnp.sum(grad_top * branch_mlp, axis=1)
        dbranch_mlp = (gate_mlp * grad_top).astype(bf16)
        g_bfc2 = jnp.sum(dbranch_mlp, axis=(0, 1), dtype=f32)
        dmlp_all = gather_x(dbranch_mlp).reshape(T, D)
        g_fc2 = reduce_w(dot(act_low, dmlp_all, ((0,), (0,))), False)
        dactiv = dot(dmlp_all, full_fc2, ((1,), (1,)))
        dhidden = gelu_pull(dactiv)[0].astype(bf16)
        g_bfc1 = jnp.sum(dhidden, axis=0, dtype=f32)
        g_fc1 = reduce_w(dot(mlp_all, dhidden, ((0,), (0,))), True)
        dnormed_mlp = reduce_x(dot(dhidden, full_fc1, ((1,), (1,))).reshape(nx, q, L, D))
        dshift_mlp = jnp.sum(dnormed_mlp, axis=1)
        dscale_mlp = jnp.sum(dnormed_mlp * unit_mid, axis=1)
        dmiddle = grad_top + layer_back(dnormed_mlp * (1.0 + scale_mlp), unit_mid, rstd_mid)
        dgate_attn = jnp.sum(dmiddle * branch, axis=1)
        dbranch = (gate_attn * dmiddle).astype(bf16)
        g_bproj = jnp.sum(dbranch, axis=(0, 1), dtype=f32)
        dattn_all = gather_x(dbranch).reshape(T, D)
        g_proj = reduce_w(dot(mixed_rows, dattn_all, ((0,), (0,))), False)
        dmixed = by_sample(dot(dattn_all, full_proj, ((1,), (1,))).astype(bf16))
        dq, dk, dv = attn_backward(queries, keys_all, vals_all, dmixed, log_norm, factor)
        half = nx * L
        dkv = jnp.stack([dk, dv])
        got_dkv = swap_with(dkv[:, :, half:].astype(bf16), "c", NC, 1)
        dkv = (dkv[:, :, :half] + got_dkv.astype(f32)).astype(bf16)
        dq = dq.astype(bf16)
        g_bq = jnp.sum(dq, axis=(0, 1), dtype=f32)
        g_bv = jnp.sum(dkv[1], axis=(0, 1), dtype=f32)
        dpacked = jnp.stack(
            [by_rank(v).reshape(T, NZ, HW) for v in (dq, dkv[0], dkv[1])], axis=2
        ).reshape(T, NZ * 3 * HW)
        g_qkv = reduce_w(dot(normed_all, dpacked, ((0,), (0,))), True)
        g_qkv = g_qkv.reshape(B, 3, hpt, HD).transpose(0, 2, 1, 3).reshape(B, hpt, 3 * HD)
        dnormed = reduce_x(dot(dpacked, full_qkv, ((1,), (1,))).reshape(nx, q, L, D))
        dshift_attn = jnp.sum(dnormed, axis=1)
        dscale_attn = jnp.sum(dnormed * unit_in, axis=1)
        dblock = dmiddle + layer_back(dnormed * (1.0 + scale_attn), unit_in, rstd_in)
        d_tokens = collect(rel(dblock.astype(bf16))).astype(f32)

        dmod = jnp.stack(
            [dshift_attn, dscale_attn, dgate_attn, dshift_mlp, dscale_mlp, dgate_mlp], axis=1
        )
        here = (jnp.arange(nx) == x).astype(f32)[:, None]

        def head_bias(vec, width):
            vec = flip_bits(vec.reshape(NZ, 1, width), 0, NZ, z)
            return (vec * here).reshape(NZ * nx * width)

        small = jnp.concatenate(
            [
                rel(dmod).reshape(q * 6 * D),
                head_bias(g_bq, HW),
                head_bias(g_bv, HW),
                rel(g_bproj),
                head_bias(g_bfc1, F),
                rel(g_bfc2),
            ]
        )
        for k in range(1, nx):
            small_k = swap_with(small, "x", nx, k)
            total = small_k if k == 1 else total + small_k
        small = small + total
        small = small + swap_with(small, "c", NC, 1)
        cut = q * 6 * D
        over_z = [small] + [swap_with(small, "z", NZ, k) for k in range(1, NZ)]
        bias_sum = sum(v[cut:] for v in over_z)
        flat = jnp.concatenate([v[:cut] for v in over_z] + [bias_sum])
        over_y = [flat] + [swap_with(flat, "y", ny, k) for k in range(1, ny)]
        bias_sum = sum(v[NZ * cut :] for v in over_y)
        dmod_all = jnp.stack([v[: NZ * cut] for v in over_y]).reshape(ny * NZ * q, 6 * D)

        take = lambda v, n: lax.dynamic_slice_in_dim(v, own * n, n, 0)
        out_bqkv = jnp.stack([take(bias_sum[:D], B), take(bias_sum[D : 2 * D], B)])
        out_bproj = take(bias_sum[2 * D : 3 * D], B)
        out_bfc1 = take(bias_sum[3 * D : 3 * D + FF], FF // dp)
        out_bfc2 = take(bias_sum[3 * D + FF :], B)
        out_bada = take(jnp.sum(dmod_all, axis=0), 6 * D // dp)
        cols = 6 * D // (NZ * nx)
        dmod_cols = lax.dynamic_slice_in_dim(dmod_all, (z * nx + x) * cols, cols, 1)
        act_mine = act_rows.reshape(ny * NZ * q, B)
        out_ada = dot(
            jnp.concatenate([act_mine] * 3),
            jnp.concatenate(split_three(dmod_cols)),
            ((0,), (0,)),
        )
        dact = sum(
            dot(part, w_ada, ((1,), (1,))) for part in split_three(dmod_all)
        ).reshape(ny, NZ, q, B)
        over_y = jnp.stack([dact[0]] + [swap_with(dact[k], "y", ny, k) for k in range(1, ny)])
        over_y = flip_bits(over_y, 1, NZ, z)
        over_y = flip_bits(over_y.reshape(ny, NC, 2 * q, B), 1, NC, c)
        other = swap_with(over_y[:, 1], "c", NC, 1)
        dact_rows = jnp.stack([over_y[:, 0], other], axis=1)
        dact_rows = rel(dact_rows.transpose(2, 0, 1, 3).reshape(ns, D))
        silu_pull = jax.vjp(jax.nn.silu, conditioning.astype(f32))[1]
        d_cond = silu_pull(dact_rows)[0]
        return (
            out,
            d_tokens,
            d_cond,
            g_qkv,
            out_bqkv,
            g_proj,
            out_bproj,
            g_fc1,
            out_bfc1,
            g_fc2,
            out_bfc2,
            out_ada,
            out_bada,
        )

    return body


def solution(mesh):
    dp, tensor = mesh.shape["dp"], mesh.shape["tensor"]
    ny, nx = dp // NC, tensor // NZ
    fine = Mesh(mesh.devices.reshape(ny, NC, NZ, nx), ("y", "c", "z", "x"))
    rows, cols = ("y", "c"), ("z", "x")
    placed = (
        P(cols, rows, None),
        P(rows, None),
        P(cols, rows, None),
        P(rows, cols, None),
        P(None, rows),
        P(cols, rows),
        P(rows),
        P(rows, cols),
        P(rows),
        P(cols, rows),
        P(rows),
        P(rows, None),
        P(rows),
    )
    out_placed = (
        P(cols, rows, None),
        P(cols, rows, None),
        P(rows, None),
        P(rows, cols, None),
        P(None, rows),
        P(cols, rows),
        P(rows),
        P(rows, cols),
        P(rows),
        P(cols, rows),
        P(rows),
        P(rows, cols),
        P(rows),
    )
    return jax.shard_map(
        make_body(ny, nx), mesh=fine, in_specs=placed, out_specs=out_placed, check_vma=False
    )
```

```python
import functools
import math

import jax
import jax.numpy as jnp
from jax import lax
from jax.experimental import pallas as pl
from jax.experimental.pallas import tpu as pltpu
from jax.sharding import Mesh, PartitionSpec as P

HD = 64
NZ = 4
NC = 2
norm_eps = 1e-06
f32 = jnp.float32
bf16 = jnp.bfloat16


def flip_bits(array, axis, count, index):
    bit = 1
    while bit < count:
        shape = array.shape
        view = array.reshape(
            shape[:axis] + (count // (2 * bit), 2, bit) + shape[axis + 1 :]
        )
        swapped = jnp.flip(view, axis=axis + 1)
        on = ((index // bit) % 2) == 1
        array = jnp.where(on, swapped, view).reshape(shape)
        bit *= 2
    return array


def swap_with(array, axis_name, count, offset):
    return lax.ppermute(array, axis_name, [(i, i ^ offset) for i in range(count)])


def layer_stats(rows):
    center = rows - jnp.mean(rows, axis=-1, keepdims=True)
    scale = lax.rsqrt(jnp.mean(center * center, axis=-1, keepdims=True) + norm_eps)
    return center * scale, scale


def layer_back(grad, unit, scale):
    return scale * (
        grad
        - jnp.mean(grad, axis=-1, keepdims=True)
        - unit * jnp.mean(grad * unit, axis=-1, keepdims=True)
    )


def split_three(values):
    high = lax.reduce_precision(values, 8, 7)
    rest = values - high
    middle = lax.reduce_precision(rest, 8, 7)
    return [part.astype(bf16) for part in (high, middle, rest - middle)]


def dot(a, b, dims):
    return lax.dot_general(a, b, (dims, ((), ())), preferred_element_type=f32)


def attn_forward(queries, keys, values, factor):
    samples, rows, width = queries.shape
    heads = width // HD
    qh = queries.reshape(samples, rows, heads, HD)
    kh = keys.reshape(samples, keys.shape[1], heads, HD)
    vh = values.reshape(samples, keys.shape[1], heads, HD)
    scores = jnp.einsum("sqhe,skhe->shqk", qh, kh, preferred_element_type=f32) * factor
    top = jnp.max(scores, axis=-1, keepdims=True)
    exps = jnp.exp(scores - top)
    total = jnp.sum(exps, axis=-1, keepdims=True)
    probs = (exps / total).astype(bf16)
    mixed = jnp.einsum("shqk,skhe->sqhe", probs, vh, preferred_element_type=f32)
    return mixed.reshape(queries.shape).astype(bf16), (top + jnp.log(total))


def attn_backward(queries, keys, values, grads, log_norm, factor):
    samples, rows, width = queries.shape
    heads = width // HD
    qh = queries.reshape(samples, rows, heads, HD)
    gh = grads.reshape(samples, rows, heads, HD)
    kh = keys.reshape(samples, keys.shape[1], heads, HD)
    vh = values.reshape(samples, keys.shape[1], heads, HD)
    scores = jnp.einsum("sqhe,skhe->shqk", qh, kh, preferred_element_type=f32) * factor
    probs = jnp.exp(scores - log_norm)
    dprobs = jnp.einsum("sqhe,skhe->shqk", gh, vh, preferred_element_type=f32)
    delta = jnp.sum(probs * dprobs, axis=-1, keepdims=True)
    dscores = (probs * (dprobs - delta)).astype(bf16)
    dq = jnp.einsum("shqk,skhe->sqhe", dscores, kh, preferred_element_type=f32) * factor
    dk = jnp.einsum("shqk,sqhe->skhe", dscores, qh, preferred_element_type=f32) * factor
    dv = jnp.einsum("shqk,sqhe->skhe", probs.astype(bf16), gh, preferred_element_type=f32)
    return dq.reshape(queries.shape), dk.reshape(keys.shape), dv.reshape(keys.shape)


def make_body(ny, nx):
    def to_cores(k):
        return [
            (c * NZ + z, (z // 2) * NZ + c * 2 + ((z % 2) ^ k))
            for c in range(NC)
            for z in range(NZ)
        ]

    def body(
        tokens,
        conditioning,
        cotangent,
        w_qkv,
        b_qkv,
        w_proj,
        b_proj,
        w_fc1,
        b_fc1,
        w_fc2,
        b_fc2,
        w_ada,
        b_ada,
    ):
        y, c = lax.axis_index("y"), lax.axis_index("c")
        z, x = lax.axis_index("z"), lax.axis_index("x")
        z0, z1 = z % 2, z // 2
        place, ns, D = tokens.shape
        q = ns // 2
        L = 2 * place
        dp = ny * NC
        B = D // dp
        own = y * NC + c
        hpt = w_qkv.shape[1]
        HW = hpt * HD
        F = w_fc1.shape[1]
        FF = F * NZ * nx
        factor = HD ** (-0.5)

        def rel(array):
            shape = array.shape
            view = array.reshape(shape[:-1] + (ny, NC, B))
            view = flip_bits(view, len(shape) - 1, ny, y)
            view = flip_bits(view, len(shape), NC, c)
            return view.reshape(shape)

        def spread(array):
            view = array.reshape(place, 2, q, D)
            first = jnp.where(z0 == 0, view[:, 0], view[:, 1])
            second = jnp.where(z0 == 0, view[:, 1], view[:, 0])
            got = [
                lax.ppermute(piece, ("c", "z"), to_cores(k))
                for k, piece in enumerate((first, second))
            ]
            return jnp.concatenate([g.transpose(1, 0, 2) for g in got], axis=1)

        def collect(array):
            pieces = [
                array[:, k * place : (k + 1) * place].transpose(1, 0, 2) for k in range(2)
            ]
            got = [
                lax.ppermute(piece, ("c", "z"), [(b, a) for a, b in to_cores(k)])
                for k, piece in enumerate(pieces)
            ]
            first = jnp.where(z0 == 0, got[0], got[1])
            second = jnp.where(z0 == 0, got[1], got[0])
            return jnp.stack([first, second], axis=1).reshape(place, ns, D)

        def gather_x(array):
            return jnp.stack(
                [array] + [swap_with(array, "x", nx, k) for k in range(1, nx)]
            )

        def reduce_x(parts):
            total = parts[0]
            for k in range(1, nx):
                total = total + swap_with(parts[k].astype(bf16), "x", nx, k).astype(f32)
            return total

        def gather_w(shard, by_rows):
            along = 1 if by_rows else 0
            over_z = jnp.concatenate(
                [shard] + [swap_with(shard, "z", NZ, k) for k in range(1, NZ)], axis=along
            )
            over_y = jnp.stack(
                [over_z] + [swap_with(over_z, "y", ny, k) for k in range(1, ny)]
            )
            other = swap_with(over_y, "c", NC, 1)
            if by_rows:
                return jnp.stack([over_y, other], axis=1).reshape(D, shard.shape[1] * NZ)
            pieces = [p for k in range(ny) for p in (over_y[k], other[k])]
            return jnp.concatenate(pieces, axis=1)

        def reduce_w(grad, by_rows):
            if by_rows:
                view = grad.reshape(ny, NC, B, NZ, grad.shape[1] // NZ)
                part = lambda ky, kc, kz: view[ky, kc, :, kz]
            else:
                view = grad.reshape(NZ, grad.shape[0] // NZ, ny, NC, B)
                part = lambda ky, kc, kz: view[kz, :, ky, kc]
            pick = lambda kc: jnp.stack(
                [jnp.stack([part(ky, kc, kz) for kz in range(NZ)]) for ky in range(ny)]
            )
            got = swap_with(pick(1).astype(bf16), "c", NC, 1)
            over_c = pick(0) + got.astype(f32)
            over_y = over_c[0]
            for k in range(1, ny):
                over_y = over_y + swap_with(over_c[k].astype(bf16), "y", ny, k).astype(f32)
            over_z = over_y[0]
            for k in range(1, NZ):
                over_z = over_z + swap_with(over_y[k].astype(bf16), "z", NZ, k).astype(f32)
            return over_z

        cond_c = jnp.stack([conditioning, swap_with(conditioning, "c", NC, 1)])
        cond_c = flip_bits(cond_c, 0, NC, c)
        cond_all = jnp.stack([cond_c] + [swap_with(cond_c, "y", ny, k) for k in range(1, ny)])
        cond_all = flip_bits(cond_all.reshape(ny, NZ, q, D), 1, NZ, z)
        act_all = jax.nn.silu(cond_all.astype(f32)).astype(bf16)
        act_rows = lax.dynamic_slice_in_dim(act_all, own * B, B, 3)

        partial_mod = dot(act_rows[:, 0].reshape(ny * q, B), w_ada, ((1,), (0,)))
        pad = lambda v, n: lax.dynamic_update_slice_in_dim(
            jnp.zeros((n,), f32), v.astype(f32), own * v.shape[0], 0
        )
        partial_mod = partial_mod + pad(b_ada, 6 * D)
        bias_vec = jnp.concatenate(
            [pad(b_qkv[0], D), pad(b_qkv[1], D), pad(b_proj, D), pad(b_fc1, FF), pad(b_fc2, D)]
        )
        partial_mod = partial_mod.reshape(ny, q * 6 * D)
        packed_mod = jnp.concatenate(
            [partial_mod, jnp.broadcast_to(bias_vec, (ny,) + bias_vec.shape)], axis=1
        )
        total_mod = packed_mod[0]
        for k in range(1, ny):
            total_mod = total_mod + swap_with(packed_mod[k], "y", ny, k)
        total_mod = total_mod + swap_with(total_mod, "c", NC, 1)
        modulation = rel(total_mod[: q * 6 * D].reshape(q, 6, 1, D))
        biases = total_mod[q * 6 * D :]
        bias_heads = biases[: 2 * D].reshape(2, NZ, nx, HW)
        bias_heads = lax.dynamic_index_in_dim(bias_heads, x, 2, keepdims=False)
        bias_heads = flip_bits(bias_heads, 1, NZ, z).reshape(2, NZ * HW)
        bias_proj = rel(biases[2 * D : 3 * D])
        bias_fc1 = biases[3 * D : 3 * D + FF].reshape(NZ, nx, F)
        bias_fc1 = lax.dynamic_index_in_dim(bias_fc1, x, 1, keepdims=False)
        bias_fc1 = flip_bits(bias_fc1, 0, NZ, z).reshape(NZ * F)
        bias_fc2 = rel(biases[3 * D + FF :])
        shift_attn, scale_attn, gate_attn, shift_mlp, scale_mlp, gate_mlp = (
            modulation[:, i] for i in range(6)
        )

        block_in = rel(spread(tokens)).astype(f32)
        w_heads = w_qkv.reshape(B, hpt, 3, HD).transpose(0, 2, 1, 3).reshape(B, 3 * HW)
        full_qkv = gather_w(w_heads, True)
        full_proj = gather_w(w_proj, False)
        full_fc1 = gather_w(w_fc1, True)
        full_fc2 = gather_w(w_fc2, False)
        grad_top = rel(spread(cotangent)).astype(f32)

        unit_in, rstd_in = layer_stats(block_in)
        normed = (unit_in * (1.0 + scale_attn) + shift_attn).astype(bf16)
        normed_all = gather_x(normed).reshape(nx * q * L, D)
        T = nx * q * L
        packed = dot(normed_all, full_qkv, ((1,), (0,))).reshape(T, NZ, 3, HW)
        queries = (packed[:, :, 0].reshape(T, NZ * HW) + bias_heads[0]).astype(bf16)
        keys = packed[:, :, 1].reshape(T, NZ * HW).astype(bf16)
        vals = (packed[:, :, 2].reshape(T, NZ * HW) + bias_heads[1]).astype(bf16)

        def by_sample(array):
            return array.reshape(nx, q, L, -1).transpose(1, 0, 2, 3).reshape(q, nx * L, -1)

        def by_rank(array):
            return array.reshape(q, nx, L, -1).transpose(1, 0, 2, 3).reshape(T, -1)

        queries, keys, vals = by_sample(queries), by_sample(keys), by_sample(vals)
        key_vals = jnp.stack([keys, vals])
        other_kv = swap_with(key_vals, "c", NC, 1)
        keys_all = jnp.concatenate([keys, other_kv[0]], axis=1)
        vals_all = jnp.concatenate([vals, other_kv[1]], axis=1)
        mixed, log_norm = attn_forward(queries, keys_all, vals_all, factor)
        mixed_rows = by_rank(mixed)
        branch_part = dot(mixed_rows, full_proj, ((1,), (0,))).reshape(nx, q, L, D)
        branch = reduce_x(branch_part) + bias_proj
        middle = block_in + gate_attn * branch
        unit_mid, rstd_mid = layer_stats(middle)
        normed_mlp = (unit_mid * (1.0 + scale_mlp) + shift_mlp).astype(bf16)
        mlp_all = gather_x(normed_mlp).reshape(T, D)
        hidden = dot(mlp_all, full_fc1, ((1,), (0,))) + bias_fc1
        activated, gelu_pull = jax.vjp(lambda h: jax.nn.gelu(h, approximate=True), hidden)
        act_low = activated.astype(bf16)
        mlp_part = dot(act_low, full_fc2, ((1,), (0,))).reshape(nx, q, L, D)
        branch_mlp = reduce_x(mlp_part) + bias_fc2
        block_out = (middle + gate_mlp * branch_mlp).astype(bf16)
        out = collect(rel(block_out))

        dgate_mlp = jnp.sum(grad_top * branch_mlp, axis=1)
        dbranch_mlp = (gate_mlp * grad_top).astype(bf16)
        g_bfc2 = jnp.sum(dbranch_mlp, axis=(0, 1), dtype=f32)
        dmlp_all = gather_x(dbranch_mlp).reshape(T, D)
        g_fc2 = reduce_w(dot(act_low, dmlp_all, ((0,), (0,))), False)
        dactiv = dot(dmlp_all, full_fc2, ((1,), (1,)))
        dhidden = gelu_pull(dactiv)[0].astype(bf16)
        g_bfc1 = jnp.sum(dhidden, axis=0, dtype=f32)
        g_fc1 = reduce_w(dot(mlp_all, dhidden, ((0,), (0,))), True)
        dnormed_mlp = reduce_x(dot(dhidden, full_fc1, ((1,), (1,))).reshape(nx, q, L, D))
        dshift_mlp = jnp.sum(dnormed_mlp, axis=1)
        dscale_mlp = jnp.sum(dnormed_mlp * unit_mid, axis=1)
        dmiddle = grad_top + layer_back(dnormed_mlp * (1.0 + scale_mlp), unit_mid, rstd_mid)
        dgate_attn = jnp.sum(dmiddle * branch, axis=1)
        dbranch = (gate_attn * dmiddle).astype(bf16)
        g_bproj = jnp.sum(dbranch, axis=(0, 1), dtype=f32)
        dattn_all = gather_x(dbranch).reshape(T, D)
        g_proj = reduce_w(dot(mixed_rows, dattn_all, ((0,), (0,))), False)
        dmixed = by_sample(dot(dattn_all, full_proj, ((1,), (1,))).astype(bf16))
        dq, dk, dv = attn_backward(queries, keys_all, vals_all, dmixed, log_norm, factor)
        half = nx * L
        dkv = jnp.stack([dk, dv])
        got_dkv = swap_with(dkv[:, :, half:].astype(bf16), "c", NC, 1)
        dkv = (dkv[:, :, :half] + got_dkv.astype(f32)).astype(bf16)
        dq = dq.astype(bf16)
        g_bq = jnp.sum(dq, axis=(0, 1), dtype=f32)
        g_bv = jnp.sum(dkv[1], axis=(0, 1), dtype=f32)
        dpacked = jnp.stack(
            [by_rank(v).reshape(T, NZ, HW) for v in (dq, dkv[0], dkv[1])], axis=2
        ).reshape(T, NZ * 3 * HW)
        g_qkv = reduce_w(dot(normed_all, dpacked, ((0,), (0,))), True)
        g_qkv = g_qkv.reshape(B, 3, hpt, HD).transpose(0, 2, 1, 3).reshape(B, hpt, 3 * HD)
        dnormed = reduce_x(dot(dpacked, full_qkv, ((1,), (1,))).reshape(nx, q, L, D))
        dshift_attn = jnp.sum(dnormed, axis=1)
        dscale_attn = jnp.sum(dnormed * unit_in, axis=1)
        dblock = dmiddle + layer_back(dnormed * (1.0 + scale_attn), unit_in, rstd_in)
        d_tokens = collect(rel(dblock.astype(bf16))).astype(f32)

        dmod = jnp.stack(
            [dshift_attn, dscale_attn, dgate_attn, dshift_mlp, dscale_mlp, dgate_mlp], axis=1
        )
        here = (jnp.arange(nx) == x).astype(f32)[:, None]

        def head_bias(vec, width):
            vec = flip_bits(vec.reshape(NZ, 1, width), 0, NZ, z)
            return (vec * here).reshape(NZ * nx * width)

        small = jnp.concatenate(
            [
                rel(dmod).reshape(q * 6 * D),
                head_bias(g_bq, HW),
                head_bias(g_bv, HW),
                rel(g_bproj),
                head_bias(g_bfc1, F),
                rel(g_bfc2),
            ]
        )
        for k in range(1, nx):
            small_k = swap_with(small, "x", nx, k)
            total = small_k if k == 1 else total + small_k
        small = small + total
        small = small + swap_with(small, "c", NC, 1)
        cut = q * 6 * D
        over_z = [small] + [swap_with(small, "z", NZ, k) for k in range(1, NZ)]
        bias_sum = sum(v[cut:] for v in over_z)
        flat = jnp.concatenate([v[:cut] for v in over_z] + [bias_sum])
        over_y = [flat] + [swap_with(flat, "y", ny, k) for k in range(1, ny)]
        bias_sum = sum(v[NZ * cut :] for v in over_y)
        dmod_all = jnp.stack([v[: NZ * cut] for v in over_y]).reshape(ny * NZ * q, 6 * D)

        take = lambda v, n: lax.dynamic_slice_in_dim(v, own * n, n, 0)
        out_bqkv = jnp.stack([take(bias_sum[:D], B), take(bias_sum[D : 2 * D], B)])
        out_bproj = take(bias_sum[2 * D : 3 * D], B)
        out_bfc1 = take(bias_sum[3 * D : 3 * D + FF], FF // dp)
        out_bfc2 = take(bias_sum[3 * D + FF :], B)
        out_bada = take(jnp.sum(dmod_all, axis=0), 6 * D // dp)
        cols = 6 * D // (NZ * nx)
        dmod_cols = lax.dynamic_slice_in_dim(dmod_all, (z * nx + x) * cols, cols, 1)
        act_mine = act_rows.reshape(ny * NZ * q, B)
        out_ada = dot(
            jnp.concatenate([act_mine] * 3),
            jnp.concatenate(split_three(dmod_cols)),
            ((0,), (0,)),
        )
        dact = sum(
            dot(part, w_ada, ((1,), (1,))) for part in split_three(dmod_all)
        ).reshape(ny, NZ, q, B)
        over_y = jnp.stack([dact[0]] + [swap_with(dact[k], "y", ny, k) for k in range(1, ny)])
        over_y = flip_bits(over_y, 1, NZ, z)
        over_y = flip_bits(over_y.reshape(ny, NC, 2 * q, B), 1, NC, c)
        other = swap_with(over_y[:, 1], "c", NC, 1)
        dact_rows = jnp.stack([over_y[:, 0], other], axis=1)
        dact_rows = rel(dact_rows.transpose(2, 0, 1, 3).reshape(ns, D))
        silu_pull = jax.vjp(jax.nn.silu, conditioning.astype(f32))[1]
        d_cond = silu_pull(dact_rows)[0]
        return (
            out,
            d_tokens,
            d_cond,
            g_qkv,
            out_bqkv,
            g_proj,
            out_bproj,
            g_fc1,
            out_bfc1,
            g_fc2,
            out_bfc2,
            out_ada,
            out_bada,
        )

    return body


LOG2E = 1.4426950408889634


def nn(a, b):
    return lax.dot_general(a, b, (((1,), (0,)), ((), ())), preferred_element_type=f32)


def nt(a, b):
    return lax.dot_general(a, b, (((1,), (1,)), ((), ())), preferred_element_type=f32)


def lanes(ref, block, width=256):
    return ref[:, pl.ds(pl.multiple_of(block * width, width), width)]


def total_rows(array):
    return jnp.sum(array, axis=0, keepdims=True)


def whole(shape):
    zeros = (0,) * len(shape)
    return pl.BlockSpec(shape, lambda *_: zeros)


def kernel_call(body, table, operands, in_specs, out_specs, outs, steps=1, scratch=(), flops=0, name=None):
    moved = sum(o.size * o.dtype.itemsize for o in operands)
    listed = outs if isinstance(outs, list) else [outs]
    moved += sum(math.prod(o.shape) * jnp.dtype(o.dtype).itemsize for o in listed)
    return pl.pallas_call(
        body,
        grid_spec=pltpu.PrefetchScalarGridSpec(
            num_scalar_prefetch=1,
            grid=(steps,),
            in_specs=in_specs,
            out_specs=out_specs,
            scratch_shapes=list(scratch),
        ),
        out_shape=outs,
        cost_estimate=pl.CostEstimate(flops=flops, bytes_accessed=moved, transcendentals=0),
        name=name,
    )(table, *operands)


def shaped(shape, dtype):
    return jax.ShapeDtypeStruct(shape, dtype)


COLS = 512


def weight_specs():
    spec = pl.BlockSpec((2, 1, 256, COLS), lambda j, t: (0, j, 0, 0))
    return [spec, spec]


def column_spec(width, rows=256):
    return pl.BlockSpec((rows, width), lambda j, t: (0, j))


PAIRS = [(kc, ky) for kc in range(2) for ky in range(2)]


def mod_kernel(t, act, w_ada, b_ada, b_qkv, b_proj, b_fc1, b_fc2, out):
    own = t[13]

    def placed(vec, count):
        tiled = jnp.concatenate([vec.astype(f32)] * count, axis=1)
        width = vec.shape[1]
        lane = lax.broadcasted_iota(jnp.int32, tiled.shape, 1)
        here = (lane >= own * width) & (lane < own * width + width)
        return jnp.where(here, tiled, 0.0)

    bias_ada = placed(b_ada[...], 4)
    rows = []
    for i in range(6):
        part = slice(i * 1024, (i + 1) * 1024)
        rows.append(nn(act[...], w_ada[:, part]) + bias_ada[:, part])
    tail = [placed(b_proj[...], 4), placed(b_fc2[...], 4), placed(b_qkv[0:1], 4), placed(b_qkv[1:2], 4)]
    fc1 = b_fc1[...].astype(f32)
    tail += [jnp.where(own == r, fc1, 0.0) for r in range(4)]
    tail += [jnp.zeros((1, 1024), f32)] * 2
    for ky in range(2):
        out[ky] = jnp.concatenate([r[ky : ky + 1] for r in rows] + tail, axis=0)


def norm(rows):
    center = rows - jnp.mean(rows, axis=-1, keepdims=True)
    scale = lax.rsqrt(jnp.mean(center * center, axis=-1, keepdims=True) + norm_eps)
    return center * scale, scale


def ln_kernel(t, first, second, mod, out):
    for i, ref in enumerate((first, second)):
        unit, _ = norm(ref[...].astype(f32))
        out[i * 128 : (i + 1) * 128] = (unit * (1.0 + mod[1:2]) + mod[0:1]).astype(bf16)


def dmlp_kernel(t, first, second, mod, out, sums):
    total = jnp.zeros((1, 1024), f32)
    for i, ref in enumerate((first, second)):
        grad = (mod[5:6] * ref[...].astype(f32)).astype(bf16)
        out[i * 128 : (i + 1) * 128] = grad
        total = total + total_rows(grad.astype(f32))
    sums[...] = total


def qkv_kernel(t, x, wo, wt, bias, q, kv):
    acc = jnp.zeros((256, 384), f32)
    for kc, ky in PAIRS:
        acc = acc + nn(lanes(x, t[kc * 2 + ky]), (wo, wt)[kc][ky, 0, :, :384])
    q[...] = (acc[:, :128] + bias[8:9]).astype(bf16)
    kv[0] = acc[:, 128:256].astype(bf16)
    kv[1] = (acc[:, 256:] + bias[9:10]).astype(bf16)


def attn_kernel(t, q, a, b, c, d, mixed, lse):
    scale = HD**-0.5 * LOG2E
    chunks = (a, b, c, d)
    keys = jnp.concatenate([r[0] for r in chunks], axis=0)
    vals_t = jnp.concatenate([r[1] for r in chunks], axis=0).T
    lane = lax.broadcasted_iota(jnp.int32, (256, 128), 1)
    queries = q[...]
    parts = []
    for h in range(2):
        qm = jnp.where((lane // HD) == h, queries, jnp.zeros_like(queries))
        s = nt(keys, qm)
        top = jnp.max(s, axis=0, keepdims=True)
        p = jnp.exp2((s - top) * scale)
        total = jnp.sum(p, axis=0, keepdims=True)
        o = nn(vals_t, p.astype(bf16)) / total
        parts.append(o[h * HD : (h + 1) * HD])
        lse[0, h : h + 1] = top * scale + jnp.log2(total)
    mixed[...] = jnp.concatenate(parts, axis=0).T.astype(bf16)


def attn_back_kernel(t, q, do, mixed, lse, a, b, c, d, dq, near, far):
    factor = HD**-0.5
    scale = factor * LOG2E
    lane = lax.broadcasted_iota(jnp.int32, (256, 128), 1)
    queries, grads = q[...], do[...]
    product_t = (grads.astype(f32) * mixed[...].astype(f32)).T
    zero = jnp.zeros_like(queries)
    qms = [jnp.where((lane // HD) == h, queries, zero) for h in range(2)]
    gms = [jnp.where((lane // HD) == h, grads, zero) for h in range(2)]
    deltas = [total_rows(product_t[h * HD : (h + 1) * HD]) for h in range(2)]
    dq_t = [jnp.zeros((128, 256), f32) for _ in range(2)]
    for i, ref in enumerate((a, b, c, d)):
        key, val = ref[0], ref[1]
        key_t = key.T
        dk = jnp.zeros((256, 128), f32)
        dv = jnp.zeros((256, 128), f32)
        for h in range(2):
            p = jnp.exp2(nt(key, qms[h]) * scale - lse[0, h : h + 1])
            ds = (p * (nt(val, gms[h]) - deltas[h])).astype(bf16)
            dv = dv + nn(p.astype(bf16), gms[h])
            dk = dk + nn(ds, qms[h])
            dq_t[h] = dq_t[h] + nn(key_t, ds)
        out = (near, far)[i // 2]
        rows = slice((i % 2) * 256, (i % 2) * 256 + 256)
        out[0, rows] = (dk * factor).astype(bf16)
        out[1, rows] = dv.astype(bf16)
    both = jnp.concatenate([dq_t[h][h * HD : (h + 1) * HD] for h in range(2)], axis=0)
    dq[...] = (both * factor).T.astype(bf16)


def unpack_proj(block):
    return jnp.concatenate([block[:128, 384:], block[128:, 384:]], axis=1)


def proj_kernel(t, mixed, wo, wt, out, acc):
    j = pl.program_id(0)

    @pl.when(j == 0)
    def _():
        acc[...] = jnp.zeros_like(acc)

    for i, (kc, ky) in enumerate(PAIRS):
        acc[i] += nn(mixed[...], unpack_proj((wo, wt)[kc][ky, 0]))

    @pl.when(j == 3)
    def _():
        for i in range(4):
            out[:, pl.ds(pl.multiple_of(t[i] * 256, 256), 256)] = acc[i].astype(out.dtype)


def proj_back_kernel(t, grad, wo, wt, out):
    acc = jnp.zeros((256, 128), f32)
    for kc, ky in PAIRS:
        acc = acc + nt(lanes(grad, t[kc * 2 + ky]), unpack_proj((wo, wt)[kc][ky, 0]))
    out[...] = acc.astype(bf16)


def mid_kernel(t, first, second, part, got, mod, branch, middle, out):
    for i, ref in enumerate((first, second)):
        rows = slice(i * 128, (i + 1) * 128)
        br = part[rows] + got[rows].astype(f32) + mod[6:7]
        mid = ref[...].astype(f32) + mod[2:3] * br
        unit, _ = norm(mid)
        branch[rows] = br
        middle[rows] = mid
        out[rows] = (unit * (1.0 + mod[4:5]) + mod[3:4]).astype(bf16)


def fc1_kernel(t, x, wo, wt, bias, act, slope):
    j = pl.program_id(0)
    h = jnp.zeros((256, COLS), f32)
    for kc, ky in PAIRS:
        h = h + nn(lanes(x, t[kc * 2 + ky]), (wo, wt)[kc][ky, 0])
    h = h + bias[pl.ds(10 + t[8 + j], 1), :]
    root = 0.7978845608028654
    inner = jnp.tanh(root * h * (1.0 + 0.044715 * h * h))
    half = 0.5 * (1.0 + inner)
    act[...] = (h * half).astype(bf16)
    slope[...] = (half + (0.5 * root) * h * (1.0 - inner * inner) * (1.0 + 3 * 0.044715 * h * h)).astype(bf16)


def fc2_kernel(t, act, wo, wt, out, acc):
    j = pl.program_id(0)

    @pl.when(j == 0)
    def _():
        acc[...] = jnp.zeros_like(acc)

    for i, (kc, ky) in enumerate(PAIRS):
        w = (wo, wt)[kc]
        acc[i] += nn(act[:, :256], w[ky, 0, :, :256]) + nn(act[:, 256:], w[ky, 0, :, 256:])

    @pl.when(j == 3)
    def _():
        for i in range(4):
            out[:, pl.ds(pl.multiple_of(t[i] * 256, 256), 256)] = acc[i].astype(out.dtype)


def mlp_back_kernel(t, grad, slope, w2o, w2t, w1o, w1t, dh, sums, out, acc):
    j = pl.program_id(0)

    @pl.when(j == 0)
    def _():
        acc[...] = jnp.zeros_like(acc)

    left = jnp.zeros((256, 256), f32)
    right = jnp.zeros((256, 256), f32)
    for kc, ky in PAIRS:
        w, g = (w2o, w2t)[kc], lanes(grad, t[kc * 2 + ky])
        left = left + nt(g, w[ky, 0, :, :256])
        right = right + nt(g, w[ky, 0, :, 256:])
    dhidden = (jnp.concatenate([left, right], axis=1) * slope[...].astype(f32)).astype(bf16)
    dh[...] = dhidden
    sums[...] = total_rows(dhidden.astype(f32))
    for i, (kc, ky) in enumerate(PAIRS):
        acc[i] += nt(dhidden, (w1o, w1t)[kc][ky, 0])

    @pl.when(j == 3)
    def _():
        for i in range(4):
            out[:, pl.ds(pl.multiple_of(t[i] * 256, 256), 256)] = acc[i].astype(out.dtype)


def mlp_grads_kernel(t, xo, xt, dho, dht, acto, actt, go, gt, keep, send):
    dh = jnp.concatenate([dho[...], dht[...]], axis=0)
    act_t = jnp.concatenate([acto[...], actt[...]], axis=0).T
    for i, (kc, ky) in enumerate(PAIRS):
        x_t = jnp.concatenate([lanes(xo, t[i]), lanes(xt, t[i])], axis=0).T
        grad = jnp.concatenate([lanes(go, t[i]), lanes(gt, t[i])], axis=0)
        out = (keep, send)[kc]
        out[ky, 0, 0] = nn(x_t, dh).astype(bf16)
        fc2 = nn(act_t, grad).astype(bf16)
        out[ky, 0, 1] = jnp.concatenate([fc2[:256], fc2[256:]], axis=1)


def attn_grads_kernel(t, xo, xt, dpo, dpt, mo, mt, go, gt, keep, send):
    dpacked = jnp.concatenate([dpo[0], dpt[0]], axis=0)
    mixed_t = jnp.concatenate([mo[...], mt[...]], axis=0).T
    for i, (kc, ky) in enumerate(PAIRS):
        x_t = jnp.concatenate([lanes(xo, t[i]), lanes(xt, t[i])], axis=0).T
        grad = jnp.concatenate([lanes(go, t[i]), lanes(gt, t[i])], axis=0)
        out = (keep, send)[kc]
        proj = nn(mixed_t, grad).astype(bf16)
        side = jnp.concatenate([proj[:, :128], proj[:, 128:]], axis=0)
        out[ky, 0] = jnp.concatenate([nn(x_t, dpacked).astype(bf16), side], axis=1)


def dmid_kernel(t, part, got, middle, branch, first, second, mod, dmid, out, sums):
    rows_of = []
    for i, ref in enumerate((first, second)):
        rows = slice(i * 128, (i + 1) * 128)
        dn = part[rows] + got[rows].astype(f32)
        unit, scale = norm(middle[rows])
        grad = dn * (1.0 + mod[4:5])
        back = scale * (
            grad
            - jnp.mean(grad, axis=-1, keepdims=True)
            - unit * jnp.mean(grad * unit, axis=-1, keepdims=True)
        )
        dm = ref[...].astype(f32) + back
        dbranch = (mod[2:3] * dm).astype(bf16)
        dmid[rows] = dm
        out[rows] = dbranch
        rows_of.append(
            [dn, dn * unit, dm * branch[rows], dbranch.astype(f32)]
        )
    sums[...] = jnp.concatenate(
        [total_rows(a) + total_rows(b) for a, b in zip(*rows_of)] + [jnp.zeros((4, 1024), f32)], axis=0
    )


def out_kernel(t, middle, part, got, first, second, mod, out0, out1, sums):
    total = jnp.zeros((1, 1024), f32)
    for i, (ref, out) in enumerate(((first, out0), (second, out1))):
        rows = slice(i * 128, (i + 1) * 128)
        branch = part[rows] + got[rows].astype(f32) + mod[7:8]
        out[...] = (middle[rows] + mod[5:6] * branch).astype(bf16)
        total = total + total_rows(ref[...].astype(f32) * branch)
    sums[...] = total


def qkv_back_kernel(t, dqo, dqt, n0, n1, f0, f1, wo, wt, packo, packt, sums, outo, outt, acco, acct):
    j = pl.program_id(0)

    @pl.when(j == 0)
    def _():
        acco[...] = jnp.zeros_like(acco)
        acct[...] = jnp.zeros_like(acct)

    dkv = n0[...].astype(f32) + n1[...].astype(f32) + f0[...].astype(f32) + f1[...].astype(f32)
    dkv = dkv.astype(bf16)
    dqs = (dqo[...], dqt[...])
    packed = [
        jnp.concatenate([dqs[i], dkv[0, i * 256 : i * 256 + 256], dkv[1, i * 256 : i * 256 + 256]], axis=1)
        for i in range(2)
    ]
    packo[0] = packed[0]
    packt[0] = packed[1]
    sums[...] = jnp.concatenate(
        [
            total_rows(dqs[0].astype(f32)) + total_rows(dqs[1].astype(f32)),
            total_rows(dkv[1].astype(f32)),
            jnp.zeros((6, 128), f32),
        ],
        axis=0,
    )
    for i, (kc, ky) in enumerate(PAIRS):
        w = (wo, wt)[kc][ky, 0, :, :384]
        acco[i] += nt(packed[0], w)
        acct[i] += nt(packed[1], w)

    @pl.when(j == 3)
    def _():
        for i in range(4):
            where = pl.ds(pl.multiple_of(t[i] * 256, 256), 256)
            outo[:, where] = acco[i]
            outt[:, where] = acct[i].astype(bf16)


def din_kernel(t, part, got, dmid, first, second, mod, out0, out1, sums):
    rows_of = []
    for i, (ref, out) in enumerate(((first, out0), (second, out1))):
        rows = slice(i * 128, (i + 1) * 128)
        dn = part[rows] + got[rows].astype(f32)
        unit, scale = norm(ref[...].astype(f32))
        grad = dn * (1.0 + mod[1:2])
        back = scale * (
            grad
            - jnp.mean(grad, axis=-1, keepdims=True)
            - unit * jnp.mean(grad * unit, axis=-1, keepdims=True)
        )
        out[...] = (dmid[rows] + back).astype(bf16)
        rows_of.append([dn, dn * unit])
    sums[...] = jnp.concatenate([total_rows(a) + total_rows(b) for a, b in zip(*rows_of)], axis=0)


def small_kernel(t, din_sums, dgate_mlp, dmid_sums, bfc2, qkv_sums, fc1o, fc1t, out):
    out[...] = jnp.zeros_like(out)
    out[0:2] = din_sums[...]
    out[2:3] = dmid_sums[2:3]
    out[3:5] = dmid_sums[0:2]
    out[5:6] = dgate_mlp[...]
    out[6:7] = dmid_sums[3:4]
    out[7:8] = bfc2[...]
    for j in range(4):
        where = pl.ds(pl.multiple_of(t[4 + j] * 128, 128), 128)
        out[8:10, where] = qkv_sums[0:2, j * 128 : (j + 1) * 128]
        fc1 = fc1o[:, j * COLS : (j + 1) * COLS] + fc1t[:, j * COLS : (j + 1) * COLS]
        for zz in range(4):
            for xx in range(2):
                @pl.when((t[8 + j] == zz) & (t[12] == xx))
                def _(fc1=fc1, zz=zz, xx=xx):
                    out[10 + zz : 11 + zz, xx * COLS : (xx + 1) * COLS] = fc1


def fast_body(
    tokens, conditioning, cotangent, w_qkv, b_qkv, w_proj, b_proj, w_fc1, b_fc1, w_fc2, b_fc2, w_ada, b_ada
):
    y, c = lax.axis_index("y"), lax.axis_index("c")
    z, x = lax.axis_index("z"), lax.axis_index("x")
    z0, z1 = z % 2, z // 2
    D = 1024
    own = y * 2 + c
    blocks = [(y ^ ky) * 2 + (c ^ kc) for kc, ky in PAIRS]
    z_of = [z ^ (kz1 * 2 + kz0) for kz0 in range(2) for kz1 in range(2)]
    table = jnp.stack(blocks + [zz * 2 + x for zz in z_of] + z_of + [x, own]).astype(jnp.int32)
    call = functools.partial(kernel_call)

    def flip(v, axis, count, offset):
        return lax.ppermute(v, axis, [(i, i ^ offset) for i in range(count)])

    def route(k):
        return [
            (cc * 4 + zz, (zz // 2) * 4 + cc * 2 + ((zz % 2) ^ k)) for cc in range(2) for zz in range(4)
        ]

    def spread(array):
        flat = array.reshape(128, 2 * D)
        low, high = flat[:, :D], flat[:, D:]
        first = jnp.where(z0 == 0, low, high)
        second = jnp.where(z0 == 0, high, low)
        return [lax.ppermute(p, ("c", "z"), route(k)) for k, p in enumerate((first, second))]

    def collect(pieces, dtype):
        got = [
            lax.ppermute(p, ("c", "z"), [(b, a) for a, b in route(k)]) for k, p in enumerate(pieces)
        ]
        low = jnp.where(z0 == 0, got[0], got[1])
        high = jnp.where(z0 == 0, got[1], got[0])
        return jnp.concatenate([low, high], axis=1).astype(dtype).reshape(128, 2, D)

    def gather_w(block):
        v = jnp.stack([block, flip(block, "z", 4, 2)])
        v = jnp.concatenate([v, flip(v, "z", 4, 1)])
        v = jnp.stack([v, flip(v, "y", 2, 1)])
        return v, flip(v, "c", 2, 1)

    def reduce_w(keep, send):
        add = lambda a, b: (a.astype(f32) + b.astype(f32)).astype(bf16)
        got = flip(send, "c", 2, 1)
        mine, theirs = add(keep[0], got[0]), add(keep[1], got[1])
        got = flip(theirs, "y", 2, 1)
        mine, theirs = add(mine[:2], got[:2]), add(mine[2:], got[2:])
        got = flip(theirs, "z", 4, 1)
        mine, theirs = add(mine[0], got[0]), add(mine[1], got[1])
        return mine.astype(f32) + flip(theirs, "z", 4, 2).astype(f32)

    cond_c = jnp.stack([conditioning, flip(conditioning, "c", 2, 1)])
    cond_c = jnp.where(c == 0, cond_c, cond_c[::-1])
    cond_all = jnp.stack([cond_c, flip(cond_c, "y", 2, 1)]).reshape(2, 4, D)
    act_abs = jax.nn.silu(cond_all.astype(f32)).astype(bf16)
    act_abs = lax.dynamic_slice_in_dim(act_abs, own * 256, 256, 2)
    act_here = lax.dynamic_slice_in_dim(act_abs, z, 1, 1)[:, 0]
    packed_mod = call(
        mod_kernel,
        table,
        [
            jnp.pad(act_here, ((0, 6), (0, 0))),
            w_ada,
            b_ada.reshape(1, -1),
            b_qkv,
            b_proj.reshape(1, -1),
            b_fc1.reshape(1, -1),
            b_fc2.reshape(1, -1),
        ],
        [whole((8, 256)), whole((256, 6144)), whole((1, 1536)), whole((2, 256)), whole((1, 256)), whole((1, 1024)), whole((1, 256))],
        whole((2, 16, D)),
        shaped((2, 16, D), f32),
        flops=2 * 8 * 256 * 6144,
        name="modulate",
    )
    mod = packed_mod[0] + flip(packed_mod[1], "y", 2, 1)
    mod = mod + flip(mod, "c", 2, 1)
    mod_spec = whole((16, D))

    tok = spread(tokens)
    heads = w_qkv.reshape(256, 2, 3, HD).transpose(0, 2, 1, 3).reshape(256, 384)
    pack_a = jnp.concatenate(
        [heads, jnp.concatenate([w_proj[:, :128], w_proj[:, 128:]], axis=0)], axis=1
    )
    wa = gather_w(pack_a)
    w1 = gather_w(w_fc1)
    w2 = gather_w(jnp.concatenate([w_fc2[:256], w_fc2[256:]], axis=1))
    cot = spread(cotangent)

    half, full = whole((128, D)), whole((256, D))
    row_b, row_f = shaped((256, D), bf16), shaped((256, D), f32)
    normed = call(ln_kernel, table, [*tok, mod], [half, half, mod_spec], full, row_b, name="norm_in")
    normed_t = flip(normed, "x", 2, 1)

    bias_spec = pl.BlockSpec((16, 128), lambda j, t: (0, t[4 + j]))
    pair_spec = pl.BlockSpec((2, 256, 128), lambda j, t: (0, 0, j))

    def make_qkv(rows):
        return call(
            qkv_kernel,
            table,
            [rows, *wa, mod],
            [full, *weight_specs(), bias_spec],
            [column_spec(128), pair_spec],
            [shaped((256, 512), bf16), shaped((2, 256, 512), bf16)],
            steps=4,
            flops=2 * 256 * 1024 * 1536,
            name="qkv",
        )

    q_o, kv_o = make_qkv(normed)
    far_o = flip(kv_o, "c", 2, 1)
    q_t, kv_t = make_qkv(normed_t)
    far_t = flip(kv_t, "c", 2, 1)
    chunks = [kv_o, kv_t, far_o, far_t]
    lse_spec = pl.BlockSpec((1, 2, 256), lambda j, t: (j, 0, 0))

    def attend(queries):
        return call(
            attn_kernel,
            table,
            [queries, *chunks],
            [column_spec(128)] + [pair_spec] * 4,
            [column_spec(128), lse_spec],
            [shaped((256, 512), bf16), shaped((4, 2, 256), f32)],
            steps=4,
            flops=4 * 256 * 1024 * 64 * 8 * 4,
            name="attend",
        )

    acc_d = pltpu.VMEM((4, 256, 256), f32)

    def project(rows, kind):
        return call(
            proj_kernel,
            table,
            [rows, *wa],
            [column_spec(128), *weight_specs()],
            full,
            shaped((256, D), kind),
            steps=4,
            scratch=[acc_d],
            flops=2 * 256 * 512 * 1024,
            name="project",
        )

    mixed_t, lse_t = attend(q_t)
    got_branch = flip(project(mixed_t, bf16), "x", 2, 1)
    mixed_o, lse_o = attend(q_o)
    branch, middle, normed_mlp = call(
        mid_kernel,
        table,
        [*tok, project(mixed_o, f32), got_branch, mod],
        [half, half, full, full, mod_spec],
        [full] * 3,
        [row_f, row_f, row_b],
        name="norm_mid",
    )
    dmlp_o, bfc2_sum = call(
        dmlp_kernel, table, [*cot, mod], [half, half, mod_spec], [full, whole((1, D))], [row_b, shaped((1, D), f32)], name="dbranch_mlp"
    )
    dmlp_t = flip(dmlp_o, "x", 2, 1)
    mlp_t = flip(normed_mlp, "x", 2, 1)
    wide = shaped((256, 2048), bf16)
    fc1_bias = pl.BlockSpec((16, COLS), lambda j, t: (0, t[12]))

    def up(rows):
        return call(
            fc1_kernel,
            table,
            [rows, *w1, mod],
            [full, *weight_specs(), fc1_bias],
            [column_spec(COLS)] * 2,
            [wide, wide],
            steps=4,
            flops=2 * 256 * 1024 * 2048,
            name="up",
        )

    def down(act, kind):
        return call(
            fc2_kernel,
            table,
            [act, *w2],
            [column_spec(COLS), *weight_specs()],
            full,
            shaped((256, D), kind),
            steps=4,
            scratch=[acc_d],
            flops=2 * 256 * 1024 * 2048,
            name="down",
        )

    def mlp_back(grad, slope, kind):
        return call(
            mlp_back_kernel,
            table,
            [grad, slope, *w2, *w1],
            [full, column_spec(COLS), *weight_specs(), *weight_specs()],
            [column_spec(COLS), column_spec(COLS, 1), full],
            [wide, shaped((1, 2048), f32), shaped((256, D), kind)],
            steps=4,
            scratch=[acc_d],
            flops=4 * 256 * 1024 * 2048,
            name="mlp_back",
        )

    act_o, slope_o = up(normed_mlp)
    act_t, slope_t = up(mlp_t)
    dh_t, fc1_t, dn_t = mlp_back(dmlp_t, slope_t, bf16)
    got_dn = flip(dn_t, "x", 2, 1)
    dh_o, fc1_o, dn_o = mlp_back(dmlp_o, slope_o, f32)
    got_mlp = flip(down(act_t, bf16), "x", 2, 1)
    down_o = down(act_o, f32)
    grad_specs = lambda *tail: pl.BlockSpec((2, 1) + tail, lambda j, t: (0, j) + (0,) * len(tail))
    mlp_grad = shaped((2, 4, 2, 256, COLS), bf16)
    keep_m, send_m = call(
        mlp_grads_kernel,
        table,
        [normed_mlp, mlp_t, dh_o, dh_t, act_o, act_t, dmlp_o, dmlp_t],
        [full, full] + [column_spec(COLS)] * 4 + [full, full],
        [grad_specs(2, 256, COLS)] * 2,
        [mlp_grad, mlp_grad],
        steps=4,
        flops=8 * 256 * 1024 * 2048,
        name="mlp_grads",
    )
    g_mlp = reduce_w(keep_m, send_m)
    g_fc1 = g_mlp[0]
    g_fc2 = jnp.concatenate([g_mlp[1][:, :256], g_mlp[1][:, 256:]], axis=0)

    sums_spec = whole((8, D))
    dmid, dbr_o, dmid_sums = call(
        dmid_kernel,
        table,
        [dn_o, got_dn, middle, branch, *cot, mod],
        [full] * 4 + [half, half, mod_spec],
        [full, full, sums_spec],
        [row_f, row_b, shaped((8, D), f32)],
        name="norm_mid_back",
    )
    dbr_t = flip(dbr_o, "x", 2, 1)
    out0, out1, dgate_mlp = call(
        out_kernel,
        table,
        [middle, down_o, got_mlp, *cot, mod],
        [full] * 3 + [half, half, mod_spec],
        [half, half, whole((1, D))],
        [shaped((128, D), bf16)] * 2 + [shaped((1, D), f32)],
        name="finish",
    )
    out = collect([out0, out1], bf16)

    def attend_back(queries, grad, mixed, lse):
        dmixed = call(
            proj_back_kernel,
            table,
            [grad, *wa],
            [full, *weight_specs()],
            column_spec(128),
            shaped((256, 512), bf16),
            steps=4,
            flops=2 * 256 * 512 * 1024,
            name="project_back",
        )
        long_spec = pl.BlockSpec((2, 512, 128), lambda j, t: (0, 0, j))
        return call(
            attn_back_kernel,
            table,
            [queries, dmixed, mixed, lse, *chunks],
            [column_spec(128)] * 3 + [lse_spec] + [pair_spec] * 4,
            [column_spec(128), long_spec, long_spec],
            [shaped((256, 512), bf16), shaped((2, 512, 512), bf16), shaped((2, 512, 512), bf16)],
            steps=4,
            flops=10 * 256 * 1024 * 64 * 8 * 4,
            name="attend_back",
        )

    dq_o, near_o, away_o = attend_back(q_o, dbr_o, mixed_o, lse_o)
    back_o = flip(away_o, "c", 2, 1)
    dq_t, near_t, away_t = attend_back(q_t, dbr_t, mixed_t, lse_t)
    back_t = flip(away_t, "c", 2, 1)
    long_spec = pl.BlockSpec((2, 512, 128), lambda j, t: (0, 0, j))
    pack_spec = pl.BlockSpec((1, 256, 384), lambda j, t: (j, 0, 0))
    pack_o, pack_t, qkv_sums, din_o, din_t = call(
        qkv_back_kernel,
        table,
        [dq_o, dq_t, near_o, near_t, back_o, back_t, *wa],
        [column_spec(128)] * 2 + [long_spec] * 4 + weight_specs(),
        [pack_spec, pack_spec, pl.BlockSpec((8, 128), lambda j, t: (0, j)), full, full],
        [shaped((4, 256, 384), bf16)] * 2 + [shaped((8, 512), f32), row_f, row_b],
        steps=4,
        scratch=[acc_d, acc_d],
        flops=4 * 256 * 1024 * 1536,
        name="qkv_back",
    )
    got_din = flip(din_t, "x", 2, 1)
    attn_grad = shaped((2, 4, 256, COLS), bf16)
    keep_a, send_a = call(
        attn_grads_kernel,
        table,
        [normed, normed_t, pack_o, pack_t, mixed_o, mixed_t, dbr_o, dbr_t],
        [full, full, pack_spec, pack_spec, column_spec(128), column_spec(128), full, full],
        [grad_specs(256, COLS)] * 2,
        [attn_grad, attn_grad],
        steps=4,
        flops=4 * 256 * 1024 * 2048,
        name="attn_grads",
    )
    g_a = reduce_w(keep_a, send_a)
    g_qkv = g_a[:, :384].reshape(256, 3, 2, HD).transpose(0, 2, 1, 3).reshape(256, 2, 3 * HD)
    g_proj = jnp.concatenate([g_a[:128, 384:], g_a[128:, 384:]], axis=1)
    dt0, dt1, din_sums = call(
        din_kernel,
        table,
        [din_o, got_din, dmid, *tok, mod],
        [full] * 3 + [half, half, mod_spec],
        [half, half, whole((2, D))],
        [shaped((128, D), bf16)] * 2 + [shaped((2, D), f32)],
        name="norm_in_back",
    )
    d_tokens = collect([dt0, dt1], f32)

    small = call(
        small_kernel,
        table,
        [din_sums, dgate_mlp, dmid_sums, bfc2_sum, qkv_sums, fc1_o, fc1_t],
        [whole((2, D)), whole((1, D)), sums_spec, whole((1, D)), whole((8, 512)), whole((1, 2048)), whole((1, 2048))],
        whole((16, D)),
        shaped((16, D), f32),
        name="small",
    )
    small = small + flip(small, "x", 2, 1)
    small = small + flip(small, "c", 2, 1)
    for axis, count, offset in (("z", 4, 2), ("z", 4, 1), ("y", 2, 1)):
        got = flip(small, axis, count, offset)
        small = jnp.concatenate([small[:-10], got[:-10], small[-10:] + got[-10:]])
    bias_sum = small[-10:]
    dmod_all = small[:-10].reshape(8, 6 * D)
    take = lambda v, n: lax.dynamic_slice_in_dim(v.reshape(-1), own * n, n, 0)
    out_bproj, out_bfc2 = take(bias_sum[0], 256), take(bias_sum[1], 256)
    out_bqkv = lax.dynamic_slice_in_dim(bias_sum[2:4], own * 256, 256, 1)
    out_bfc1 = take(bias_sum[4:8], 1024)
    out_bada = take(jnp.sum(dmod_all, axis=0), 1536)
    act_rel = jnp.swapaxes(flip_bits(act_abs, 1, 4, z).reshape(2, 2, 2, 256), 1, 2).reshape(8, 256)
    dmod_cols = lax.dynamic_slice_in_dim(dmod_all, (z * 2 + x) * 768, 768, 1)
    out_ada = dot(
        jnp.concatenate([act_rel] * 3), jnp.concatenate(split_three(dmod_cols)), ((0,), (0,))
    )
    dact = dot(jnp.concatenate(split_three(dmod_all)), w_ada, ((1,), (1,)))
    dact = dact[:8] + dact[8:16] + dact[16:]
    dact = jnp.swapaxes(dact.reshape(2, 2, 2, 256), 1, 2).reshape(2, 4, 256)
    dact = flip_bits(dact, 1, 4, z)
    dact = jnp.stack([dact[0], flip(dact[1], "y", 2, 1)]).reshape(2, 2, 2, 256)
    dact = jnp.where(c == 0, dact, dact[:, ::-1])
    dact = jnp.stack([dact[:, 0], flip(dact[:, 1], "c", 2, 1)], axis=1)
    dact = flip_bits(flip_bits(dact, 0, 2, y), 1, 2, c).transpose(2, 0, 1, 3).reshape(2, D)
    d_cond = jax.vjp(jax.nn.silu, conditioning.astype(f32))[1](dact)[0]
    return (
        out,
        d_tokens,
        d_cond,
        g_qkv,
        out_bqkv,
        g_proj,
        out_bproj,
        g_fc1,
        out_bfc1,
        g_fc2,
        out_bfc2,
        out_ada,
        out_bada,
    )


def solution(mesh):
    dp, tensor = mesh.shape["dp"], mesh.shape["tensor"]
    ny, nx = dp // NC, tensor // NZ
    fine = Mesh(mesh.devices.reshape(ny, NC, NZ, nx), ("y", "c", "z", "x"))
    rows, cols = ("y", "c"), ("z", "x")
    placed = (
        P(cols, rows, None),
        P(rows, None),
        P(cols, rows, None),
        P(rows, cols, None),
        P(None, rows),
        P(cols, rows),
        P(rows),
        P(rows, cols),
        P(rows),
        P(cols, rows),
        P(rows),
        P(rows, None),
        P(rows),
    )
    out_placed = (
        P(cols, rows, None),
        P(cols, rows, None),
        P(rows, None),
        P(rows, cols, None),
        P(None, rows),
        P(cols, rows),
        P(rows),
        P(rows, cols),
        P(rows),
        P(cols, rows),
        P(rows),
        P(rows, cols),
        P(rows),
    )
    body = fast_body if (ny, nx) == (2, 2) else make_body(ny, nx)
    return jax.shard_map(
        body, mesh=fine, in_specs=placed, out_specs=out_placed, check_vma=False
    )
```

```python
import functools
import math

import jax
import jax.numpy as jnp
from jax import lax
from jax.experimental import pallas as pl
from jax.experimental.pallas import tpu as pltpu
from jax.sharding import Mesh, PartitionSpec as P

HD = 64
NZ = 4
NC = 2
norm_eps = 1e-06
f32 = jnp.float32
bf16 = jnp.bfloat16


def flip_bits(array, axis, count, index):
    bit = 1
    while bit < count:
        shape = array.shape
        view = array.reshape(
            shape[:axis] + (count // (2 * bit), 2, bit) + shape[axis + 1 :]
        )
        swapped = jnp.flip(view, axis=axis + 1)
        on = ((index // bit) % 2) == 1
        array = jnp.where(on, swapped, view).reshape(shape)
        bit *= 2
    return array


def swap_with(array, axis_name, count, offset):
    return lax.ppermute(array, axis_name, [(i, i ^ offset) for i in range(count)])


def layer_stats(rows):
    center = rows - jnp.mean(rows, axis=-1, keepdims=True)
    scale = lax.rsqrt(jnp.mean(center * center, axis=-1, keepdims=True) + norm_eps)
    return center * scale, scale


def layer_back(grad, unit, scale):
    return scale * (
        grad
        - jnp.mean(grad, axis=-1, keepdims=True)
        - unit * jnp.mean(grad * unit, axis=-1, keepdims=True)
    )


def split_three(values):
    high = lax.reduce_precision(values, 8, 7)
    rest = values - high
    middle = lax.reduce_precision(rest, 8, 7)
    return [part.astype(bf16) for part in (high, middle, rest - middle)]


def dot(a, b, dims):
    return lax.dot_general(a, b, (dims, ((), ())), preferred_element_type=f32)


def attn_forward(queries, keys, values, factor):
    samples, rows, width = queries.shape
    heads = width // HD
    qh = queries.reshape(samples, rows, heads, HD)
    kh = keys.reshape(samples, keys.shape[1], heads, HD)
    vh = values.reshape(samples, keys.shape[1], heads, HD)
    scores = jnp.einsum("sqhe,skhe->shqk", qh, kh, preferred_element_type=f32) * factor
    top = jnp.max(scores, axis=-1, keepdims=True)
    exps = jnp.exp(scores - top)
    total = jnp.sum(exps, axis=-1, keepdims=True)
    probs = (exps / total).astype(bf16)
    mixed = jnp.einsum("shqk,skhe->sqhe", probs, vh, preferred_element_type=f32)
    return mixed.reshape(queries.shape).astype(bf16), (top + jnp.log(total))


def attn_backward(queries, keys, values, grads, log_norm, factor):
    samples, rows, width = queries.shape
    heads = width // HD
    qh = queries.reshape(samples, rows, heads, HD)
    gh = grads.reshape(samples, rows, heads, HD)
    kh = keys.reshape(samples, keys.shape[1], heads, HD)
    vh = values.reshape(samples, keys.shape[1], heads, HD)
    scores = jnp.einsum("sqhe,skhe->shqk", qh, kh, preferred_element_type=f32) * factor
    probs = jnp.exp(scores - log_norm)
    dprobs = jnp.einsum("sqhe,skhe->shqk", gh, vh, preferred_element_type=f32)
    delta = jnp.sum(probs * dprobs, axis=-1, keepdims=True)
    dscores = (probs * (dprobs - delta)).astype(bf16)
    dq = jnp.einsum("shqk,skhe->sqhe", dscores, kh, preferred_element_type=f32) * factor
    dk = jnp.einsum("shqk,sqhe->skhe", dscores, qh, preferred_element_type=f32) * factor
    dv = jnp.einsum("shqk,sqhe->skhe", probs.astype(bf16), gh, preferred_element_type=f32)
    return dq.reshape(queries.shape), dk.reshape(keys.shape), dv.reshape(keys.shape)


def make_body(ny, nx):
    def to_cores(k):
        return [
            (c * NZ + z, (z // 2) * NZ + c * 2 + ((z % 2) ^ k))
            for c in range(NC)
            for z in range(NZ)
        ]

    def body(
        tokens,
        conditioning,
        cotangent,
        w_qkv,
        b_qkv,
        w_proj,
        b_proj,
        w_fc1,
        b_fc1,
        w_fc2,
        b_fc2,
        w_ada,
        b_ada,
    ):
        y, c = lax.axis_index("y"), lax.axis_index("c")
        z, x = lax.axis_index("z"), lax.axis_index("x")
        z0, z1 = z % 2, z // 2
        place, ns, D = tokens.shape
        q = ns // 2
        L = 2 * place
        dp = ny * NC
        B = D // dp
        own = y * NC + c
        hpt = w_qkv.shape[1]
        HW = hpt * HD
        F = w_fc1.shape[1]
        FF = F * NZ * nx
        factor = HD ** (-0.5)

        def rel(array):
            shape = array.shape
            view = array.reshape(shape[:-1] + (ny, NC, B))
            view = flip_bits(view, len(shape) - 1, ny, y)
            view = flip_bits(view, len(shape), NC, c)
            return view.reshape(shape)

        def spread(array):
            view = array.reshape(place, 2, q, D)
            first = jnp.where(z0 == 0, view[:, 0], view[:, 1])
            second = jnp.where(z0 == 0, view[:, 1], view[:, 0])
            got = [
                lax.ppermute(piece, ("c", "z"), to_cores(k))
                for k, piece in enumerate((first, second))
            ]
            return jnp.concatenate([g.transpose(1, 0, 2) for g in got], axis=1)

        def collect(array):
            pieces = [
                array[:, k * place : (k + 1) * place].transpose(1, 0, 2) for k in range(2)
            ]
            got = [
                lax.ppermute(piece, ("c", "z"), [(b, a) for a, b in to_cores(k)])
                for k, piece in enumerate(pieces)
            ]
            first = jnp.where(z0 == 0, got[0], got[1])
            second = jnp.where(z0 == 0, got[1], got[0])
            return jnp.stack([first, second], axis=1).reshape(place, ns, D)

        def gather_x(array):
            return jnp.stack(
                [array] + [swap_with(array, "x", nx, k) for k in range(1, nx)]
            )

        def reduce_x(parts):
            total = parts[0]
            for k in range(1, nx):
                total = total + swap_with(parts[k].astype(bf16), "x", nx, k).astype(f32)
            return total

        def gather_w(shard, by_rows):
            along = 1 if by_rows else 0
            over_z = jnp.concatenate(
                [shard] + [swap_with(shard, "z", NZ, k) for k in range(1, NZ)], axis=along
            )
            over_y = jnp.stack(
                [over_z] + [swap_with(over_z, "y", ny, k) for k in range(1, ny)]
            )
            other = swap_with(over_y, "c", NC, 1)
            if by_rows:
                return jnp.stack([over_y, other], axis=1).reshape(D, shard.shape[1] * NZ)
            pieces = [p for k in range(ny) for p in (over_y[k], other[k])]
            return jnp.concatenate(pieces, axis=1)

        def reduce_w(grad, by_rows):
            if by_rows:
                view = grad.reshape(ny, NC, B, NZ, grad.shape[1] // NZ)
                part = lambda ky, kc, kz: view[ky, kc, :, kz]
            else:
                view = grad.reshape(NZ, grad.shape[0] // NZ, ny, NC, B)
                part = lambda ky, kc, kz: view[kz, :, ky, kc]
            pick = lambda kc: jnp.stack(
                [jnp.stack([part(ky, kc, kz) for kz in range(NZ)]) for ky in range(ny)]
            )
            got = swap_with(pick(1).astype(bf16), "c", NC, 1)
            over_c = pick(0) + got.astype(f32)
            over_y = over_c[0]
            for k in range(1, ny):
                over_y = over_y + swap_with(over_c[k].astype(bf16), "y", ny, k).astype(f32)
            over_z = over_y[0]
            for k in range(1, NZ):
                over_z = over_z + swap_with(over_y[k].astype(bf16), "z", NZ, k).astype(f32)
            return over_z

        cond_c = jnp.stack([conditioning, swap_with(conditioning, "c", NC, 1)])
        cond_c = flip_bits(cond_c, 0, NC, c)
        cond_all = jnp.stack([cond_c] + [swap_with(cond_c, "y", ny, k) for k in range(1, ny)])
        cond_all = flip_bits(cond_all.reshape(ny, NZ, q, D), 1, NZ, z)
        act_all = jax.nn.silu(cond_all.astype(f32)).astype(bf16)
        act_rows = lax.dynamic_slice_in_dim(act_all, own * B, B, 3)

        partial_mod = dot(act_rows[:, 0].reshape(ny * q, B), w_ada, ((1,), (0,)))
        pad = lambda v, n: lax.dynamic_update_slice_in_dim(
            jnp.zeros((n,), f32), v.astype(f32), own * v.shape[0], 0
        )
        partial_mod = partial_mod + pad(b_ada, 6 * D)
        bias_vec = jnp.concatenate(
            [pad(b_qkv[0], D), pad(b_qkv[1], D), pad(b_proj, D), pad(b_fc1, FF), pad(b_fc2, D)]
        )
        partial_mod = partial_mod.reshape(ny, q * 6 * D)
        packed_mod = jnp.concatenate(
            [partial_mod, jnp.broadcast_to(bias_vec, (ny,) + bias_vec.shape)], axis=1
        )
        total_mod = packed_mod[0]
        for k in range(1, ny):
            total_mod = total_mod + swap_with(packed_mod[k], "y", ny, k)
        total_mod = total_mod + swap_with(total_mod, "c", NC, 1)
        modulation = rel(total_mod[: q * 6 * D].reshape(q, 6, 1, D))
        biases = total_mod[q * 6 * D :]
        bias_heads = biases[: 2 * D].reshape(2, NZ, nx, HW)
        bias_heads = lax.dynamic_index_in_dim(bias_heads, x, 2, keepdims=False)
        bias_heads = flip_bits(bias_heads, 1, NZ, z).reshape(2, NZ * HW)
        bias_proj = rel(biases[2 * D : 3 * D])
        bias_fc1 = biases[3 * D : 3 * D + FF].reshape(NZ, nx, F)
        bias_fc1 = lax.dynamic_index_in_dim(bias_fc1, x, 1, keepdims=False)
        bias_fc1 = flip_bits(bias_fc1, 0, NZ, z).reshape(NZ * F)
        bias_fc2 = rel(biases[3 * D + FF :])
        shift_attn, scale_attn, gate_attn, shift_mlp, scale_mlp, gate_mlp = (
            modulation[:, i] for i in range(6)
        )

        block_in = rel(spread(tokens)).astype(f32)
        w_heads = w_qkv.reshape(B, hpt, 3, HD).transpose(0, 2, 1, 3).reshape(B, 3 * HW)
        full_qkv = gather_w(w_heads, True)
        full_proj = gather_w(w_proj, False)
        full_fc1 = gather_w(w_fc1, True)
        full_fc2 = gather_w(w_fc2, False)
        grad_top = rel(spread(cotangent)).astype(f32)

        unit_in, rstd_in = layer_stats(block_in)
        normed = (unit_in * (1.0 + scale_attn) + shift_attn).astype(bf16)
        normed_all = gather_x(normed).reshape(nx * q * L, D)
        T = nx * q * L
        packed = dot(normed_all, full_qkv, ((1,), (0,))).reshape(T, NZ, 3, HW)
        queries = (packed[:, :, 0].reshape(T, NZ * HW) + bias_heads[0]).astype(bf16)
        keys = packed[:, :, 1].reshape(T, NZ * HW).astype(bf16)
        vals = (packed[:, :, 2].reshape(T, NZ * HW) + bias_heads[1]).astype(bf16)

        def by_sample(array):
            return array.reshape(nx, q, L, -1).transpose(1, 0, 2, 3).reshape(q, nx * L, -1)

        def by_rank(array):
            return array.reshape(q, nx, L, -1).transpose(1, 0, 2, 3).reshape(T, -1)

        queries, keys, vals = by_sample(queries), by_sample(keys), by_sample(vals)
        key_vals = jnp.stack([keys, vals])
        other_kv = swap_with(key_vals, "c", NC, 1)
        keys_all = jnp.concatenate([keys, other_kv[0]], axis=1)
        vals_all = jnp.concatenate([vals, other_kv[1]], axis=1)
        mixed, log_norm = attn_forward(queries, keys_all, vals_all, factor)
        mixed_rows = by_rank(mixed)
        branch_part = dot(mixed_rows, full_proj, ((1,), (0,))).reshape(nx, q, L, D)
        branch = reduce_x(branch_part) + bias_proj
        middle = block_in + gate_attn * branch
        unit_mid, rstd_mid = layer_stats(middle)
        normed_mlp = (unit_mid * (1.0 + scale_mlp) + shift_mlp).astype(bf16)
        mlp_all = gather_x(normed_mlp).reshape(T, D)
        hidden = dot(mlp_all, full_fc1, ((1,), (0,))) + bias_fc1
        activated, gelu_pull = jax.vjp(lambda h: jax.nn.gelu(h, approximate=True), hidden)
        act_low = activated.astype(bf16)
        mlp_part = dot(act_low, full_fc2, ((1,), (0,))).reshape(nx, q, L, D)
        branch_mlp = reduce_x(mlp_part) + bias_fc2
        block_out = (middle + gate_mlp * branch_mlp).astype(bf16)
        out = collect(rel(block_out))

        dgate_mlp = jnp.sum(grad_top * branch_mlp, axis=1)
        dbranch_mlp = (gate_mlp * grad_top).astype(bf16)
        g_bfc2 = jnp.sum(dbranch_mlp, axis=(0, 1), dtype=f32)
        dmlp_all = gather_x(dbranch_mlp).reshape(T, D)
        g_fc2 = reduce_w(dot(act_low, dmlp_all, ((0,), (0,))), False)
        dactiv = dot(dmlp_all, full_fc2, ((1,), (1,)))
        dhidden = gelu_pull(dactiv)[0].astype(bf16)
        g_bfc1 = jnp.sum(dhidden, axis=0, dtype=f32)
        g_fc1 = reduce_w(dot(mlp_all, dhidden, ((0,), (0,))), True)
        dnormed_mlp = reduce_x(dot(dhidden, full_fc1, ((1,), (1,))).reshape(nx, q, L, D))
        dshift_mlp = jnp.sum(dnormed_mlp, axis=1)
        dscale_mlp = jnp.sum(dnormed_mlp * unit_mid, axis=1)
        dmiddle = grad_top + layer_back(dnormed_mlp * (1.0 + scale_mlp), unit_mid, rstd_mid)
        dgate_attn = jnp.sum(dmiddle * branch, axis=1)
        dbranch = (gate_attn * dmiddle).astype(bf16)
        g_bproj = jnp.sum(dbranch, axis=(0, 1), dtype=f32)
        dattn_all = gather_x(dbranch).reshape(T, D)
        g_proj = reduce_w(dot(mixed_rows, dattn_all, ((0,), (0,))), False)
        dmixed = by_sample(dot(dattn_all, full_proj, ((1,), (1,))).astype(bf16))
        dq, dk, dv = attn_backward(queries, keys_all, vals_all, dmixed, log_norm, factor)
        half = nx * L
        dkv = jnp.stack([dk, dv])
        got_dkv = swap_with(dkv[:, :, half:].astype(bf16), "c", NC, 1)
        dkv = (dkv[:, :, :half] + got_dkv.astype(f32)).astype(bf16)
        dq = dq.astype(bf16)
        g_bq = jnp.sum(dq, axis=(0, 1), dtype=f32)
        g_bv = jnp.sum(dkv[1], axis=(0, 1), dtype=f32)
        dpacked = jnp.stack(
            [by_rank(v).reshape(T, NZ, HW) for v in (dq, dkv[0], dkv[1])], axis=2
        ).reshape(T, NZ * 3 * HW)
        g_qkv = reduce_w(dot(normed_all, dpacked, ((0,), (0,))), True)
        g_qkv = g_qkv.reshape(B, 3, hpt, HD).transpose(0, 2, 1, 3).reshape(B, hpt, 3 * HD)
        dnormed = reduce_x(dot(dpacked, full_qkv, ((1,), (1,))).reshape(nx, q, L, D))
        dshift_attn = jnp.sum(dnormed, axis=1)
        dscale_attn = jnp.sum(dnormed * unit_in, axis=1)
        dblock = dmiddle + layer_back(dnormed * (1.0 + scale_attn), unit_in, rstd_in)
        d_tokens = collect(rel(dblock.astype(bf16))).astype(f32)

        dmod = jnp.stack(
            [dshift_attn, dscale_attn, dgate_attn, dshift_mlp, dscale_mlp, dgate_mlp], axis=1
        )
        here = (jnp.arange(nx) == x).astype(f32)[:, None]

        def head_bias(vec, width):
            vec = flip_bits(vec.reshape(NZ, 1, width), 0, NZ, z)
            return (vec * here).reshape(NZ * nx * width)

        small = jnp.concatenate(
            [
                rel(dmod).reshape(q * 6 * D),
                head_bias(g_bq, HW),
                head_bias(g_bv, HW),
                rel(g_bproj),
                head_bias(g_bfc1, F),
                rel(g_bfc2),
            ]
        )
        for k in range(1, nx):
            small_k = swap_with(small, "x", nx, k)
            total = small_k if k == 1 else total + small_k
        small = small + total
        small = small + swap_with(small, "c", NC, 1)
        cut = q * 6 * D
        over_z = [small] + [swap_with(small, "z", NZ, k) for k in range(1, NZ)]
        bias_sum = sum(v[cut:] for v in over_z)
        flat = jnp.concatenate([v[:cut] for v in over_z] + [bias_sum])
        over_y = [flat] + [swap_with(flat, "y", ny, k) for k in range(1, ny)]
        bias_sum = sum(v[NZ * cut :] for v in over_y)
        dmod_all = jnp.stack([v[: NZ * cut] for v in over_y]).reshape(ny * NZ * q, 6 * D)

        take = lambda v, n: lax.dynamic_slice_in_dim(v, own * n, n, 0)
        out_bqkv = jnp.stack([take(bias_sum[:D], B), take(bias_sum[D : 2 * D], B)])
        out_bproj = take(bias_sum[2 * D : 3 * D], B)
        out_bfc1 = take(bias_sum[3 * D : 3 * D + FF], FF // dp)
        out_bfc2 = take(bias_sum[3 * D + FF :], B)
        out_bada = take(jnp.sum(dmod_all, axis=0), 6 * D // dp)
        cols = 6 * D // (NZ * nx)
        dmod_cols = lax.dynamic_slice_in_dim(dmod_all, (z * nx + x) * cols, cols, 1)
        act_mine = act_rows.reshape(ny * NZ * q, B)
        out_ada = dot(
            jnp.concatenate([act_mine] * 3),
            jnp.concatenate(split_three(dmod_cols)),
            ((0,), (0,)),
        )
        dact = sum(
            dot(part, w_ada, ((1,), (1,))) for part in split_three(dmod_all)
        ).reshape(ny, NZ, q, B)
        over_y = jnp.stack([dact[0]] + [swap_with(dact[k], "y", ny, k) for k in range(1, ny)])
        over_y = flip_bits(over_y, 1, NZ, z)
        over_y = flip_bits(over_y.reshape(ny, NC, 2 * q, B), 1, NC, c)
        other = swap_with(over_y[:, 1], "c", NC, 1)
        dact_rows = jnp.stack([over_y[:, 0], other], axis=1)
        dact_rows = rel(dact_rows.transpose(2, 0, 1, 3).reshape(ns, D))
        silu_pull = jax.vjp(jax.nn.silu, conditioning.astype(f32))[1]
        d_cond = silu_pull(dact_rows)[0]
        return (
            out,
            d_tokens,
            d_cond,
            g_qkv,
            out_bqkv,
            g_proj,
            out_bproj,
            g_fc1,
            out_bfc1,
            g_fc2,
            out_bfc2,
            out_ada,
            out_bada,
        )

    return body


LOG2E = 1.4426950408889634


def nn(a, b):
    return lax.dot_general(a, b, (((1,), (0,)), ((), ())), preferred_element_type=f32)


def nt(a, b):
    return lax.dot_general(a, b, (((1,), (1,)), ((), ())), preferred_element_type=f32)


def lanes(ref, block, width=256):
    return ref[:, pl.ds(pl.multiple_of(block * width, width), width)]


def total_rows(array):
    return jnp.sum(array, axis=0, keepdims=True)


def whole(shape):
    zeros = (0,) * len(shape)
    return pl.BlockSpec(shape, lambda *_: zeros)


def kernel_call(body, table, operands, in_specs, out_specs, outs, steps=1, scratch=(), flops=0, name=None):
    moved = sum(o.size * o.dtype.itemsize for o in operands)
    listed = outs if isinstance(outs, list) else [outs]
    moved += sum(math.prod(o.shape) * jnp.dtype(o.dtype).itemsize for o in listed)
    return pl.pallas_call(
        body,
        grid_spec=pltpu.PrefetchScalarGridSpec(
            num_scalar_prefetch=1,
            grid=(steps,),
            in_specs=in_specs,
            out_specs=out_specs,
            scratch_shapes=list(scratch),
        ),
        out_shape=outs,
        cost_estimate=pl.CostEstimate(flops=flops, bytes_accessed=moved, transcendentals=0),
        name=name,
    )(table, *operands)


def shaped(shape, dtype):
    return jax.ShapeDtypeStruct(shape, dtype)


COLS = 512


def block_spec(rows, cols):
    return pl.BlockSpec((2, 1, rows, cols), lambda j, t: (0, j, 0, 0))


def halves_specs():
    return [block_spec(128, COLS)] * 4


def halves(refs, kc, ky, cols):
    return jnp.concatenate([refs[kc][ky, 0, :, cols], refs[2 + kc][ky, 0, :, cols]], axis=0)


def column_spec(width, rows=256):
    return pl.BlockSpec((rows, width), lambda j, t: (0, j))


PAIRS = [(kc, ky) for kc in range(2) for ky in range(2)]


def mod_kernel(t, act, w_ada, b_ada, b_qkv, b_proj, b_fc1, b_fc2, out):
    own = t[13]

    def placed(vec, count):
        tiled = jnp.concatenate([vec.astype(f32)] * count, axis=1)
        width = vec.shape[1]
        lane = lax.broadcasted_iota(jnp.int32, tiled.shape, 1)
        here = (lane >= own * width) & (lane < own * width + width)
        return jnp.where(here, tiled, 0.0)

    bias_ada = placed(b_ada[...], 4)
    rows = []
    for i in range(6):
        part = slice(i * 1024, (i + 1) * 1024)
        rows.append(nn(act[...], w_ada[:, part]) + bias_ada[:, part])
    tail = [placed(b_proj[...], 4), placed(b_fc2[...], 4), placed(b_qkv[0:1], 4), placed(b_qkv[1:2], 4)]
    fc1 = b_fc1[...].astype(f32)
    tail += [jnp.where(own == r, fc1, 0.0) for r in range(4)]
    tail += [jnp.zeros((1, 1024), f32)] * 2
    for ky in range(2):
        out[ky] = jnp.concatenate([r[ky : ky + 1] for r in rows] + tail, axis=0)


def norm(rows):
    center = rows - jnp.mean(rows, axis=-1, keepdims=True)
    scale = lax.rsqrt(jnp.mean(center * center, axis=-1, keepdims=True) + norm_eps)
    return center * scale, scale


def ln_kernel(t, first, second, mod, out):
    for i, ref in enumerate((first, second)):
        unit, _ = norm(ref[...].astype(f32))
        out[i * 128 : (i + 1) * 128] = (unit * (1.0 + mod[1:2]) + mod[0:1]).astype(bf16)


def dmlp_kernel(t, first, second, mod, out, sums):
    total = jnp.zeros((1, 1024), f32)
    for i, ref in enumerate((first, second)):
        grad = (mod[5:6] * ref[...].astype(f32)).astype(bf16)
        out[i * 128 : (i + 1) * 128] = grad
        total = total + total_rows(grad.astype(f32))
    sums[...] = total


def qkv_kernel(t, x, *refs):
    ws, (bias, q, kv) = refs[:4], refs[4:]
    acc = jnp.zeros((256, 384), f32)
    for kc, ky in PAIRS:
        acc = acc + nn(lanes(x, t[kc * 2 + ky]), halves(ws, kc, ky, slice(0, 384)))
    q[...] = (acc[:, :128] + bias[8:9]).astype(bf16)
    kv[0] = acc[:, 128:256].astype(bf16)
    kv[1] = (acc[:, 256:] + bias[9:10]).astype(bf16)


def attn_kernel(t, q, a, b, c, d, mixed, lse):
    scale = HD**-0.5 * LOG2E
    chunks = (a, b, c, d)
    keys = jnp.concatenate([r[0] for r in chunks], axis=0)
    vals_t = jnp.concatenate([r[1] for r in chunks], axis=0).T
    lane = lax.broadcasted_iota(jnp.int32, (256, 128), 1)
    queries = q[...]
    parts = []
    for h in range(2):
        qm = jnp.where((lane // HD) == h, queries, jnp.zeros_like(queries))
        s = nt(keys, qm)
        top = jnp.max(s, axis=0, keepdims=True)
        p = jnp.exp2((s - top) * scale)
        total = jnp.sum(p, axis=0, keepdims=True)
        o = nn(vals_t, p.astype(bf16)) / total
        parts.append(o[h * HD : (h + 1) * HD])
        lse[0, h : h + 1] = top * scale + jnp.log2(total)
    mixed[...] = jnp.concatenate(parts, axis=0).T.astype(bf16)


def attn_back_kernel(t, q, do, mixed, lse, a, b, c, d, dq, near, far):
    factor = HD**-0.5
    scale = factor * LOG2E
    lane = lax.broadcasted_iota(jnp.int32, (256, 128), 1)
    queries, grads = q[...], do[...]
    product_t = (grads.astype(f32) * mixed[...].astype(f32)).T
    zero = jnp.zeros_like(queries)
    qms = [jnp.where((lane // HD) == h, queries, zero) for h in range(2)]
    gms = [jnp.where((lane // HD) == h, grads, zero) for h in range(2)]
    deltas = [total_rows(product_t[h * HD : (h + 1) * HD]) for h in range(2)]
    dq_t = [jnp.zeros((128, 256), f32) for _ in range(2)]
    for i, ref in enumerate((a, b, c, d)):
        key, val = ref[0], ref[1]
        key_t = key.T
        dk = jnp.zeros((256, 128), f32)
        dv = jnp.zeros((256, 128), f32)
        for h in range(2):
            p = jnp.exp2(nt(key, qms[h]) * scale - lse[0, h : h + 1])
            ds = (p * (nt(val, gms[h]) - deltas[h])).astype(bf16)
            dv = dv + nn(p.astype(bf16), gms[h])
            dk = dk + nn(ds, qms[h])
            dq_t[h] = dq_t[h] + nn(key_t, ds)
        out = (near, far)[i // 2]
        rows = slice((i % 2) * 256, (i % 2) * 256 + 256)
        out[0, rows] = (dk * factor).astype(bf16)
        out[1, rows] = dv.astype(bf16)
    both = jnp.concatenate([dq_t[h][h * HD : (h + 1) * HD] for h in range(2)], axis=0)
    dq[...] = (both * factor).T.astype(bf16)


def unpack_proj(refs, kc, ky):
    return jnp.concatenate([refs[kc][ky, 0, :, 384:], refs[2 + kc][ky, 0, :, 384:]], axis=1)


def proj_kernel(t, mixed, *refs):
    ws, (out, acc) = refs[:4], refs[4:]
    j = pl.program_id(0)

    @pl.when(j == 0)
    def _():
        acc[...] = jnp.zeros_like(acc)

    for i, (kc, ky) in enumerate(PAIRS):
        acc[i] += nn(mixed[...], unpack_proj(ws, kc, ky))

    @pl.when(j == 3)
    def _():
        for i in range(4):
            out[:, pl.ds(pl.multiple_of(t[i] * 256, 256), 256)] = acc[i].astype(out.dtype)


def proj_back_kernel(t, grad, *refs):
    ws, out = refs[:4], refs[4]
    acc = jnp.zeros((256, 128), f32)
    for kc, ky in PAIRS:
        acc = acc + nt(lanes(grad, t[kc * 2 + ky]), unpack_proj(ws, kc, ky))
    out[...] = acc.astype(bf16)


def mid_kernel(t, first, second, part, got, mod, branch, middle, out):
    for i, ref in enumerate((first, second)):
        rows = slice(i * 128, (i + 1) * 128)
        br = part[rows] + got[rows].astype(f32) + mod[6:7]
        mid = ref[...].astype(f32) + mod[2:3] * br
        unit, _ = norm(mid)
        branch[rows] = br
        middle[rows] = mid
        out[rows] = (unit * (1.0 + mod[4:5]) + mod[3:4]).astype(bf16)


def fc1_kernel(t, x, wo, wt, bias, act, slope):
    j = pl.program_id(0)
    h = jnp.zeros((256, COLS), f32)
    for kc, ky in PAIRS:
        h = h + nn(lanes(x, t[kc * 2 + ky]), (wo, wt)[kc][ky, 0])
    h = h + bias[pl.ds(10 + t[8 + j], 1), :]
    root = 0.7978845608028654
    inner = jnp.tanh(root * h * (1.0 + 0.044715 * h * h))
    half = 0.5 * (1.0 + inner)
    act[...] = (h * half).astype(bf16)
    slope[...] = (half + (0.5 * root) * h * (1.0 - inner * inner) * (1.0 + 3 * 0.044715 * h * h)).astype(bf16)


def fc2_kernel(t, act, wo, wt, out, acc):
    j = pl.program_id(0)

    @pl.when(j == 0)
    def _():
        acc[...] = jnp.zeros_like(acc)

    for i, (kc, ky) in enumerate(PAIRS):
        w = (wo, wt)[kc]
        acc[i] += nn(act[:, :256], w[ky, 0, :, :256]) + nn(act[:, 256:], w[ky, 0, :, 256:])

    @pl.when(j == 3)
    def _():
        for i in range(4):
            out[:, pl.ds(pl.multiple_of(t[i] * 256, 256), 256)] = acc[i].astype(out.dtype)


def mlp_back_kernel(t, grad, slope, w2o, w2t, w1o, w1t, dh, sums, out, acc):
    j = pl.program_id(0)

    @pl.when(j == 0)
    def _():
        acc[...] = jnp.zeros_like(acc)

    left = jnp.zeros((256, 256), f32)
    right = jnp.zeros((256, 256), f32)
    for kc, ky in PAIRS:
        w, g = (w2o, w2t)[kc], lanes(grad, t[kc * 2 + ky])
        left = left + nt(g, w[ky, 0, :, :256])
        right = right + nt(g, w[ky, 0, :, 256:])
    dhidden = (jnp.concatenate([left, right], axis=1) * slope[...].astype(f32)).astype(bf16)
    dh[...] = dhidden
    sums[...] = total_rows(dhidden.astype(f32))
    for i, (kc, ky) in enumerate(PAIRS):
        acc[i] += nt(dhidden, (w1o, w1t)[kc][ky, 0])

    @pl.when(j == 3)
    def _():
        for i in range(4):
            out[:, pl.ds(pl.multiple_of(t[i] * 256, 256), 256)] = acc[i].astype(out.dtype)


def keep_rows(own, other, turned):
    @pl.when(pl.program_id(0) == 0)
    def _():
        for i in range(4):
            part = slice(i * 256, (i + 1) * 256)
            turned[part] = jnp.concatenate([own[:, part], other[:, part]], axis=0).T


def feature_rows(turned, block):
    return turned[pl.ds(pl.multiple_of(block * 256, 256), 256)]


def fc1_grads_kernel(t, xo, xt, dho, dht, keep, send, turned):
    keep_rows(xo, xt, turned)
    dh = jnp.concatenate([dho[...], dht[...]], axis=0)
    for i, (kc, ky) in enumerate(PAIRS):
        (keep, send)[kc][ky, 0] = nn(feature_rows(turned, t[i]), dh).astype(bf16)


def fc2_grads_kernel(t, acto, actt, go, gt, keep, send):
    act_t = jnp.concatenate([acto[...], actt[...]], axis=0).T
    for i, (kc, ky) in enumerate(PAIRS):
        grad = jnp.concatenate([lanes(go, t[i]), lanes(gt, t[i])], axis=0)
        fc2 = nn(act_t, grad).astype(bf16)
        (keep, send)[kc][ky, 0] = jnp.concatenate([fc2[:256], fc2[256:]], axis=1)


def proj_grads_kernel(t, mo, mt, go, gt, keep, send):
    mixed_t = jnp.concatenate([mo[...], mt[...]], axis=0).T
    for i, (kc, ky) in enumerate(PAIRS):
        grad = jnp.concatenate([lanes(go, t[i]), lanes(gt, t[i])], axis=0)
        (keep, send)[kc][ky, 0] = nn(mixed_t, grad).astype(bf16)


def qkv_grads_kernel(t, xo, xt, dpo, dpt, keep0, send0, keep1, send1, turned):
    keep_rows(xo, xt, turned)
    dpacked = jnp.concatenate([dpo[0], dpt[0]], axis=0)
    for i, (kc, ky) in enumerate(PAIRS):
        grad = nn(feature_rows(turned, t[i]), dpacked).astype(bf16)
        (keep0, send0)[kc][ky, 0] = grad[:128]
        (keep1, send1)[kc][ky, 0] = grad[128:]


def dmid_kernel(t, part, got, middle, branch, first, second, mod, dmid, out, sums):
    rows_of = []
    for i, ref in enumerate((first, second)):
        rows = slice(i * 128, (i + 1) * 128)
        dn = part[rows] + got[rows].astype(f32)
        unit, scale = norm(middle[rows])
        grad = dn * (1.0 + mod[4:5])
        back = scale * (
            grad
            - jnp.mean(grad, axis=-1, keepdims=True)
            - unit * jnp.mean(grad * unit, axis=-1, keepdims=True)
        )
        dm = ref[...].astype(f32) + back
        dbranch = (mod[2:3] * dm).astype(bf16)
        dmid[rows] = dm
        out[rows] = dbranch
        rows_of.append(
            [dn, dn * unit, dm * branch[rows], dbranch.astype(f32)]
        )
    sums[...] = jnp.concatenate(
        [total_rows(a) + total_rows(b) for a, b in zip(*rows_of)] + [jnp.zeros((4, 1024), f32)], axis=0
    )


def out_kernel(t, middle, part, got, first, second, mod, out0, out1, sums):
    total = jnp.zeros((1, 1024), f32)
    for i, (ref, out) in enumerate(((first, out0), (second, out1))):
        rows = slice(i * 128, (i + 1) * 128)
        branch = part[rows] + got[rows].astype(f32) + mod[7:8]
        out[...] = (middle[rows] + mod[5:6] * branch).astype(bf16)
        total = total + total_rows(ref[...].astype(f32) * branch)
    sums[...] = total


def qkv_back_kernel(t, dqo, dqt, n0, n1, f0, f1, *refs):
    ws, (packo, packt, sums, outo, outt, acco, acct) = refs[:4], refs[4:]
    j = pl.program_id(0)

    @pl.when(j == 0)
    def _():
        acco[...] = jnp.zeros_like(acco)
        acct[...] = jnp.zeros_like(acct)

    dkv = n0[...].astype(f32) + n1[...].astype(f32) + f0[...].astype(f32) + f1[...].astype(f32)
    dkv = dkv.astype(bf16)
    dqs = (dqo[...], dqt[...])
    packed = [
        jnp.concatenate([dqs[i], dkv[0, i * 256 : i * 256 + 256], dkv[1, i * 256 : i * 256 + 256]], axis=1)
        for i in range(2)
    ]
    packo[0] = packed[0]
    packt[0] = packed[1]
    sums[...] = jnp.concatenate(
        [
            total_rows(dqs[0].astype(f32)) + total_rows(dqs[1].astype(f32)),
            total_rows(dkv[1].astype(f32)),
            jnp.zeros((6, 128), f32),
        ],
        axis=0,
    )
    for i, (kc, ky) in enumerate(PAIRS):
        w = halves(ws, kc, ky, slice(0, 384))
        acco[i] += nt(packed[0], w)
        acct[i] += nt(packed[1], w)

    @pl.when(j == 3)
    def _():
        for i in range(4):
            where = pl.ds(pl.multiple_of(t[i] * 256, 256), 256)
            outo[:, where] = acco[i]
            outt[:, where] = acct[i].astype(bf16)


def din_kernel(t, part, got, dmid, first, second, mod, out0, out1, sums):
    rows_of = []
    for i, (ref, out) in enumerate(((first, out0), (second, out1))):
        rows = slice(i * 128, (i + 1) * 128)
        dn = part[rows] + got[rows].astype(f32)
        unit, scale = norm(ref[...].astype(f32))
        grad = dn * (1.0 + mod[1:2])
        back = scale * (
            grad
            - jnp.mean(grad, axis=-1, keepdims=True)
            - unit * jnp.mean(grad * unit, axis=-1, keepdims=True)
        )
        out[...] = (dmid[rows] + back).astype(bf16)
        rows_of.append([dn, dn * unit])
    sums[...] = jnp.concatenate([total_rows(a) + total_rows(b) for a, b in zip(*rows_of)], axis=0)


def pack_kernel(t, qkv, proj, fc2, upper, lower, side):
    for i, out in enumerate((upper, lower)):
        rows = qkv[i * 128 : (i + 1) * 128]
        parts = [rows[:, 192 * g + HD * k : 192 * g + HD * k + HD] for k in range(3) for g in range(2)]
        out[0] = jnp.concatenate(parts + [proj[:, i * 128 : (i + 1) * 128]], axis=1)
    side[0] = jnp.concatenate([fc2[:256], fc2[256:]], axis=1)


def assemble_kernel(t, up, up_got, low, low_got, out):
    for i, (own, got) in enumerate(((up, up_got), (low, low_got))):
        rows = own[0].astype(f32) + got[0].astype(f32)
        parts = [rows[:, 128 * k + HD * g : 128 * k + HD * g + HD] for g in range(2) for k in range(3)]
        out[i * 128 : (i + 1) * 128] = jnp.concatenate(parts, axis=1)


def small_kernel(t, din_sums, dgate_mlp, dmid_sums, bfc2, qkv_sums, fc1o, fc1t, out):
    out[...] = jnp.zeros_like(out)
    out[0:2] = din_sums[...]
    out[2:3] = dmid_sums[2:3]
    out[3:5] = dmid_sums[0:2]
    out[5:6] = dgate_mlp[...]
    out[6:7] = dmid_sums[3:4]
    out[7:8] = bfc2[...]
    for j in range(4):
        where = pl.ds(pl.multiple_of(t[4 + j] * 128, 128), 128)
        out[8:10, where] = qkv_sums[0:2, j * 128 : (j + 1) * 128]
        fc1 = fc1o[:, j * COLS : (j + 1) * COLS] + fc1t[:, j * COLS : (j + 1) * COLS]
        for zz in range(4):
            for xx in range(2):
                @pl.when((t[8 + j] == zz) & (t[12] == xx))
                def _(fc1=fc1, zz=zz, xx=xx):
                    out[10 + zz : 11 + zz, xx * COLS : (xx + 1) * COLS] = fc1


def fast_body(
    tokens, conditioning, cotangent, w_qkv, b_qkv, w_proj, b_proj, w_fc1, b_fc1, w_fc2, b_fc2, w_ada, b_ada
):
    y, c = lax.axis_index("y"), lax.axis_index("c")
    z, x = lax.axis_index("z"), lax.axis_index("x")
    z0, z1 = z % 2, z // 2
    D = 1024
    own = y * 2 + c
    blocks = [(y ^ ky) * 2 + (c ^ kc) for kc, ky in PAIRS]
    z_of = [z ^ k1 ^ (2 * k2) for k1 in range(2) for k2 in range(2)]
    table = jnp.stack(blocks + [zz * 2 + x for zz in z_of] + z_of + [x, own]).astype(jnp.int32)
    call = functools.partial(kernel_call)

    def flip(v, axis, count, offset):
        return lax.ppermute(v, axis, [(i, i ^ offset) for i in range(count)])

    def route(k):
        return [
            (cc * 4 + zz, (zz // 2) * 4 + cc * 2 + ((zz % 2) ^ k)) for cc in range(2) for zz in range(4)
        ]

    def spread_parts(array):
        flat = array.reshape(128, 2 * D)
        low, high = flat[:, :D], flat[:, D:]
        return jnp.where(z0 == 0, low, high), jnp.where(z0 == 0, high, low)

    def spread(array):
        return [lax.ppermute(p, ("c", "z"), route(k)) for k, p in enumerate(spread_parts(array))]

    def send_back(pieces):
        return [lax.ppermute(p, ("c", "z"), [(b, a) for a, b in route(k)]) for k, p in enumerate(pieces)]

    def collect(got, dtype, *others):
        got = lax.optimization_barrier((*got, *others))[:2]
        low = jnp.where(z0 == 0, got[0], got[1])
        high = jnp.where(z0 == 0, got[1], got[0])
        return jnp.concatenate([low, high], axis=1).astype(dtype).reshape(128, 2, D)

    def after(value, *others):
        return lax.optimization_barrier((value, *others))[0]

    STEPS = {"near": ("z", 4, 1), "far": ("z", 4, 2), "y": ("y", 2, 1)}

    def widen(v, step, *others):
        v, got = lax.optimization_barrier((v, flip(v, *STEPS[step]), *others))[:2]
        return jnp.concatenate([v, got])

    def both_cores(v):
        v = v.reshape((2, 4) + v.shape[1:])
        return [v, flip(v, "c", 2, 1)]

    def cross(keep, send):
        flat = (8,) + keep.shape[2:]
        return keep.reshape(flat), flip(send.reshape(flat), "c", 2, 1)

    def fold(pair, *others):
        own, got = lax.optimization_barrier((*pair, *others))[:2]
        half = own.shape[0] // 2
        cut = lambda v, k: v[k * half : (k + 1) * half].astype(f32)
        return [(cut(own, k) + cut(got, k)).astype(bf16) for k in range(2)]

    def onward(parts, step):
        return parts[0], flip(parts[1], *STEPS[step])

    def total(pair, *others):
        own, got = lax.optimization_barrier((*pair, *others))[:2]
        v = own.astype(f32) + got.astype(f32)
        return v.reshape(v.shape[-2:])

    cond_c = jnp.stack([conditioning, flip(conditioning, "c", 2, 1)])
    cond_c = jnp.where(c == 0, cond_c, cond_c[::-1])
    cond_all = jnp.stack([cond_c, flip(cond_c, "y", 2, 1)]).reshape(2, 4, D)
    tok_parts = spread_parts(tokens)
    tok = [lax.ppermute(p, ("c", "z"), route(k)) for k, p in enumerate(tok_parts)]
    upper, lower, packed_fc2 = call(
        pack_kernel,
        table,
        [w_qkv.reshape(256, 384), w_proj, w_fc2],
        [whole((256, 384)), whole((128, 256)), whole((512, 256))],
        [whole((1, 128, COLS)), whole((1, 128, COLS)), whole((1, 256, COLS))],
        [shaped((1, 128, COLS), bf16), shaped((1, 128, COLS), bf16), shaped((1, 256, COLS), bf16)],
        name="pack",
    )
    upper = widen(upper, "far")
    upper, cond_all, *tok = lax.optimization_barrier((upper, cond_all, *tok))
    upper, lower = widen(upper, "near"), widen(after(lower, upper), "far")
    act_abs = jax.nn.silu(cond_all.astype(f32)).astype(bf16)
    act_abs = lax.dynamic_slice_in_dim(act_abs, own * 256, 256, 2)
    act_here = lax.dynamic_slice_in_dim(act_abs, z, 1, 1)[:, 0]
    packed_mod = call(
        mod_kernel,
        table,
        [
            jnp.pad(act_here, ((0, 6), (0, 0))),
            w_ada,
            b_ada.reshape(1, -1),
            b_qkv,
            b_proj.reshape(1, -1),
            b_fc1.reshape(1, -1),
            b_fc2.reshape(1, -1),
        ],
        [whole((8, 256)), whole((256, 6144)), whole((1, 1536)), whole((2, 256)), whole((1, 256)), whole((1, 1024)), whole((1, 256))],
        whole((2, 16, D)),
        shaped((2, 16, D), f32),
        flops=2 * 8 * 256 * 6144,
        name="modulate",
    )
    mod = packed_mod[0] + flip(packed_mod[1], "y", 2, 1)
    mod = mod + flip(mod, "c", 2, 1)
    mod_spec = whole((16, D))
    upper, lower, mod = lax.optimization_barrier((upper, lower, mod))

    half, full = whole((128, D)), whole((256, D))
    row_b, row_f = shaped((256, D), bf16), shaped((256, D), f32)
    normed = call(ln_kernel, table, [*tok, mod], [half, half, mod_spec], full, row_b, name="norm_in")
    normed_t = flip(normed, "x", 2, 1)
    upper = widen(upper, "y")
    lower = widen(lower, "near")
    w1 = after(w_fc1[None], lower)
    lower, got_low, w1, got_w1, normed_t = lax.optimization_barrier(
        (lower, flip(lower, *STEPS["y"]), w1, flip(w1, *STEPS["far"]), normed_t)
    )
    lower, w1 = jnp.concatenate([lower, got_low]), jnp.concatenate([w1, got_w1])
    wa = both_cores(upper) + both_cores(after(lower, w1))

    bias_spec = pl.BlockSpec((16, 128), lambda j, t: (0, t[4 + j]))
    pair_spec = pl.BlockSpec((2, 256, 128), lambda j, t: (0, 0, j))

    def make_qkv(rows):
        return call(
            qkv_kernel,
            table,
            [rows, *wa, mod],
            [full, *halves_specs(), bias_spec],
            [column_spec(128), pair_spec],
            [shaped((256, 512), bf16), shaped((2, 256, 512), bf16)],
            steps=4,
            flops=2 * 256 * 1024 * 1536,
            name="qkv",
        )

    q_o, kv_o = make_qkv(normed)
    far_o = flip(kv_o, "c", 2, 1)
    q_t, kv_t = make_qkv(normed_t)
    far_t = flip(kv_t, "c", 2, 1)
    chunks = [kv_o, kv_t, far_o, far_t]
    w1 = widen(w1, "near", kv_t)
    q_t, w1 = lax.optimization_barrier((q_t, w1))
    lse_spec = pl.BlockSpec((1, 2, 256), lambda j, t: (j, 0, 0))

    def attend(queries):
        return call(
            attn_kernel,
            table,
            [queries, *chunks],
            [column_spec(128)] + [pair_spec] * 4,
            [column_spec(128), lse_spec],
            [shaped((256, 512), bf16), shaped((4, 2, 256), f32)],
            steps=4,
            flops=4 * 256 * 1024 * 64 * 8 * 4,
            name="attend",
        )

    acc_d = pltpu.VMEM((4, 256, 256), f32)

    def project(rows, kind):
        return call(
            proj_kernel,
            table,
            [rows, *wa],
            [column_spec(128), *halves_specs()],
            full,
            shaped((256, D), kind),
            steps=4,
            scratch=[acc_d],
            flops=2 * 256 * 512 * 1024,
            name="project",
        )

    mixed_t, lse_t = attend(q_t)
    w2 = widen(after(packed_fc2, q_t), "far", mixed_t)
    part_t = project(after(mixed_t, w2), bf16)
    got_branch = flip(part_t, "x", 2, 1)
    q_o, part_t = lax.optimization_barrier((q_o, part_t))
    mixed_o, lse_o = attend(q_o)
    w1, w2 = widen(w1, "y", mixed_o), widen(w2, "near", mixed_o)
    mixed_o, w1, w2, got_branch = lax.optimization_barrier((mixed_o, w1, w2, got_branch))
    w1 = both_cores(w1)
    cot = [lax.ppermute(p, ("c", "z"), route(k)) for k, p in enumerate(spread_parts(after(cotangent, mixed_o)))]
    branch, middle, normed_mlp = call(
        mid_kernel,
        table,
        [*tok, project(mixed_o, f32), got_branch, mod],
        [half, half, full, full, mod_spec],
        [full] * 3,
        [row_f, row_f, row_b],
        name="norm_mid",
    )
    dmlp_o, bfc2_sum = call(
        dmlp_kernel,
        table,
        [*cot, after(mod, normed_mlp)],
        [half, half, mod_spec],
        [full, whole((1, D))],
        [row_b, shaped((1, D), f32)],
        name="dbranch_mlp",
    )
    dmlp_t = flip(dmlp_o, "x", 2, 1)
    mlp_t = flip(normed_mlp, "x", 2, 1)
    wide = shaped((256, 2048), bf16)
    wide_specs = [block_spec(256, COLS)] * 2
    fc1_bias = pl.BlockSpec((16, COLS), lambda j, t: (0, t[12]))

    def up(rows):
        return call(
            fc1_kernel,
            table,
            [rows, *w1, mod],
            [full, *wide_specs, fc1_bias],
            [column_spec(COLS)] * 2,
            [wide, wide],
            steps=4,
            flops=2 * 256 * 1024 * 2048,
            name="up",
        )

    def down(act, kind):
        return call(
            fc2_kernel,
            table,
            [act, *w2],
            [column_spec(COLS), *wide_specs],
            full,
            shaped((256, D), kind),
            steps=4,
            scratch=[acc_d],
            flops=2 * 256 * 1024 * 2048,
            name="down",
        )

    def mlp_back(grad, slope, kind):
        return call(
            mlp_back_kernel,
            table,
            [grad, slope, *w2, *w1],
            [full, column_spec(COLS), *wide_specs, *wide_specs],
            [column_spec(COLS), column_spec(COLS, 1), full],
            [wide, shaped((1, 2048), f32), shaped((256, D), kind)],
            steps=4,
            scratch=[acc_d],
            flops=4 * 256 * 1024 * 2048,
            name="mlp_back",
        )

    act_o, slope_o = up(after(normed_mlp, dmlp_o))
    w2 = both_cores(widen(w2, "y", act_o, mlp_t))
    act_t, slope_t = up(after(mlp_t, act_o))
    dh_t, fc1_t, dn_t = mlp_back(dmlp_t, slope_t, bf16)
    got_dn = flip(dn_t, "x", 2, 1)
    turned = pltpu.VMEM((D, 512), bf16)
    fc2_keep, fc2_send = call(
        fc2_grads_kernel,
        table,
        [act_o, act_t, after(dmlp_o, dn_t), dmlp_t],
        [column_spec(COLS)] * 2 + [full, full],
        [block_spec(256, COLS)] * 2,
        [shaped((2, 4, 256, COLS), bf16)] * 2,
        steps=4,
        flops=4 * 256 * 1024 * 2048,
        name="fc2_grads",
    )
    g_fc2 = cross(fc2_keep, fc2_send)
    dh_o, fc1_o, dn_o = mlp_back(dmlp_o, after(slope_o, fc2_send), f32)
    g_fc2 = fold(g_fc2, dn_o)
    fc1_keep, fc1_send = call(
        fc1_grads_kernel,
        table,
        [normed_mlp, mlp_t, after(dh_o, got_dn, *g_fc2), dh_t],
        [full, full] + [column_spec(COLS)] * 2,
        [block_spec(256, COLS)] * 2,
        [shaped((2, 4, 256, COLS), bf16)] * 2,
        steps=4,
        scratch=[turned],
        flops=4 * 256 * 1024 * 2048,
        name="fc1_grads",
    )
    g_fc1 = cross(fc1_keep, fc1_send)
    g_fc2 = onward(g_fc2, "y")
    dn_o = after(dn_o, fc1_send)

    sums_spec = whole((8, D))
    dmid, dbr_o, dmid_sums = call(
        dmid_kernel,
        table,
        [dn_o, got_dn, middle, branch, *cot, mod],
        [full] * 4 + [half, half, mod_spec],
        [full, full, sums_spec],
        [row_f, row_b, shaped((8, D), f32)],
        name="norm_mid_back",
    )
    dbr_t = flip(dbr_o, "x", 2, 1)
    finish = lambda down_o, got_mlp: call(
        out_kernel,
        table,
        [middle, down_o, got_mlp, *cot, mod],
        [full] * 3 + [half, half, mod_spec],
        [half, half, whole((1, D))],
        [shaped((128, D), bf16)] * 2 + [shaped((1, D), f32)],
        name="finish",
    )

    def project_back(grad):
        return call(
            proj_back_kernel,
            table,
            [grad, *wa],
            [full, *halves_specs()],
            column_spec(128),
            shaped((256, 512), bf16),
            steps=4,
            flops=2 * 256 * 512 * 1024,
            name="project_back",
        )

    def attend_back(queries, dmixed, mixed, lse):
        long_spec = pl.BlockSpec((2, 512, 128), lambda j, t: (0, 0, j))
        return call(
            attn_back_kernel,
            table,
            [queries, dmixed, mixed, lse, *chunks],
            [column_spec(128)] * 3 + [lse_spec] + [pair_spec] * 4,
            [column_spec(128), long_spec, long_spec],
            [shaped((256, 512), bf16), shaped((2, 512, 512), bf16), shaped((2, 512, 512), bf16)],
            steps=4,
            flops=10 * 256 * 1024 * 64 * 8 * 4,
            name="attend_back",
        )

    dmixed_o = project_back(dbr_o)
    g_fc1 = fold(g_fc1, dmixed_o)
    dmixed_o = after(dmixed_o, *g_fc1)
    g_fc1 = onward(g_fc1, "y")
    dq_o, near_o, away_o = attend_back(q_o, dmixed_o, mixed_o, lse_o)
    back_o = flip(away_o, "c", 2, 1)
    g_fc2 = fold(g_fc2, away_o)
    dmixed_t = project_back(after(dbr_t, *g_fc2))
    g_fc2 = onward(g_fc2, "near")
    p_keep, p_send = call(
        proj_grads_kernel,
        table,
        [mixed_o, mixed_t, after(dbr_o, dmixed_t), dbr_t],
        [column_spec(128)] * 2 + [full, full],
        [block_spec(128, 256)] * 2,
        [shaped((2, 4, 128, 256), bf16)] * 2,
        steps=4,
        flops=4 * 256 * 512 * 1024,
        name="proj_grads",
    )
    g_proj = cross(p_keep, p_send)
    dmixed_t = after(dmixed_t, p_send)
    dq_t, near_t, away_t = attend_back(q_t, dmixed_t, mixed_t, lse_t)
    back_t = flip(away_t, "c", 2, 1)
    g_fc1, g_fc2, g_proj = (fold(v, away_t) for v in (g_fc1, g_fc2, g_proj))
    dq_t = after(dq_t, *g_fc1, *g_fc2, *g_proj)
    g_fc2, g_fc1, g_proj = onward(g_fc2, "far"), onward(g_fc1, "near"), onward(g_proj, "y")
    long_spec = pl.BlockSpec((2, 512, 128), lambda j, t: (0, 0, j))
    pack_spec = pl.BlockSpec((1, 256, 384), lambda j, t: (j, 0, 0))
    pack_o, pack_t, qkv_sums, din_o, din_t = call(
        qkv_back_kernel,
        table,
        [dq_o, dq_t, near_o, near_t, back_o, back_t, *wa],
        [column_spec(128)] * 2 + [long_spec] * 4 + halves_specs(),
        [pack_spec, pack_spec, pl.BlockSpec((8, 128), lambda j, t: (0, j)), full, full],
        [shaped((4, 256, 384), bf16)] * 2 + [shaped((8, 512), f32), row_f, row_b],
        steps=4,
        scratch=[acc_d, acc_d],
        flops=4 * 256 * 1024 * 1536,
        name="qkv_back",
    )
    got_din = flip(din_t, "x", 2, 1)
    qkv_out = [shaped((2, 4, 128, 384), bf16)] * 4
    k0, s0, k1, s1 = call(
        qkv_grads_kernel,
        table,
        [normed, normed_t, after(pack_o, din_t), pack_t],
        [full, full, pack_spec, pack_spec],
        [block_spec(128, 384)] * 4,
        qkv_out,
        steps=4,
        scratch=[turned],
        flops=4 * 256 * 1024 * 1536,
        name="qkv_grads",
    )
    g_up, g_low = cross(k0, s0), cross(k1, s1)
    down_t = down(after(act_t, s0, s1), bf16)
    got_mlp = flip(down_t, "x", 2, 1)
    g_up, g_low = fold(g_up, down_t), fold(g_low, down_t)
    act_o, got_din, *_ = lax.optimization_barrier((act_o, got_din, *g_up, *g_low))
    g_up, g_low = onward(g_up, "y"), onward(g_low, "y")
    down_o = down(act_o, f32)
    g_proj, g_fc1 = fold(g_proj, down_o), fold(g_fc1, down_o)
    din_o = after(din_o, *g_proj, *g_fc1)
    g_proj, g_fc1 = onward(g_proj, "near"), onward(g_fc1, "far")
    dt0, dt1, din_sums = call(
        din_kernel,
        table,
        [din_o, got_din, dmid, *tok, mod],
        [full] * 3 + [half, half, mod_spec],
        [half, half, whole((2, D))],
        [shaped((128, D), bf16)] * 2 + [shaped((2, D), f32)],
        name="norm_in_back",
    )
    dt_got = send_back([dt0, dt1])
    g_up = fold(g_up, dt0)
    out0, out1, dgate_mlp = finish(after(down_o, din_sums, *g_up), got_mlp)
    g_up = onward(g_up, "near")
    out_got = send_back([out0, out1])

    small = call(
        small_kernel,
        table,
        [din_sums, dgate_mlp, dmid_sums, bfc2_sum, qkv_sums, fc1_o, fc1_t],
        [whole((2, D)), whole((1, D)), sums_spec, whole((1, D)), whole((8, 512)), whole((1, 2048)), whole((1, 2048))],
        whole((16, D)),
        shaped((16, D), f32),
        name="small",
    )
    g_proj = onward(fold(g_proj, small), "far")
    small = small + flip(small, "x", 2, 1)
    g_fc1, g_fc2 = total(g_fc1, small), total(g_fc2, small)
    g_fc2 = jnp.concatenate([g_fc2[:, :256], g_fc2[:, 256:]], axis=0)
    small = small + flip(small, "c", 2, 1)

    def spread_small(v, axis, count, offset):
        got = flip(v, axis, count, offset)
        return jnp.concatenate([v[:-10], got[:-10], v[-10:] + got[-10:]])

    g_up, g_low = onward(fold(g_up, small), "far"), onward(fold(g_low, small), "near")
    small = spread_small(small, "z", 4, 2)
    g_proj = total(g_proj, small)
    small = spread_small(small, "z", 4, 1)
    g_low = onward(fold(g_low, small), "far")
    d_tokens = collect(dt_got, f32, small)
    small = spread_small(small, "y", 2, 1)
    out = collect(out_got, bf16, small)
    g_qkv = call(
        assemble_kernel,
        table,
        [*g_up, *g_low],
        [whole((1, 128, 384))] * 4,
        whole((256, 384)),
        shaped((256, 384), f32),
        name="assemble",
    ).reshape(256, 2, 3 * HD)
    bias_sum = small[-10:]
    dmod_all = small[:-10].reshape(8, 6 * D)
    take = lambda v, n: lax.dynamic_slice_in_dim(v.reshape(-1), own * n, n, 0)
    out_bproj, out_bfc2 = take(bias_sum[0], 256), take(bias_sum[1], 256)
    out_bqkv = lax.dynamic_slice_in_dim(bias_sum[2:4], own * 256, 256, 1)
    out_bfc1 = take(bias_sum[4:8], 1024)
    out_bada = take(jnp.sum(dmod_all, axis=0), 1536)
    act_rel = jnp.swapaxes(flip_bits(act_abs, 1, 4, z).reshape(2, 2, 2, 256), 1, 2).reshape(8, 256)
    dmod_cols = lax.dynamic_slice_in_dim(dmod_all, (z * 2 + x) * 768, 768, 1)
    out_ada = dot(
        jnp.concatenate([act_rel] * 3), jnp.concatenate(split_three(dmod_cols)), ((0,), (0,))
    )
    dact = dot(jnp.concatenate(split_three(dmod_all)), w_ada, ((1,), (1,)))
    dact = dact[:8] + dact[8:16] + dact[16:]
    dact = jnp.swapaxes(dact.reshape(2, 2, 2, 256), 1, 2).reshape(2, 4, 256)
    dact = flip_bits(dact, 1, 4, z)
    dact = jnp.stack([dact[0], flip(dact[1], "y", 2, 1)]).reshape(2, 2, 2, 256)
    dact = jnp.where(c == 0, dact, dact[:, ::-1])
    dact = jnp.stack([dact[:, 0], flip(dact[:, 1], "c", 2, 1)], axis=1)
    dact = flip_bits(flip_bits(dact, 0, 2, y), 1, 2, c).transpose(2, 0, 1, 3).reshape(2, D)
    d_cond = jax.vjp(jax.nn.silu, conditioning.astype(f32))[1](dact)[0]
    return (
        out,
        d_tokens,
        d_cond,
        g_qkv,
        out_bqkv,
        g_proj,
        out_bproj,
        g_fc1,
        out_bfc1,
        g_fc2,
        out_bfc2,
        out_ada,
        out_bada,
    )


def solution(mesh):
    dp, tensor = mesh.shape["dp"], mesh.shape["tensor"]
    ny, nx = dp // NC, tensor // NZ
    fine = Mesh(mesh.devices.reshape(ny, NC, NZ, nx), ("y", "c", "z", "x"))
    rows, cols = ("y", "c"), ("z", "x")
    placed = (
        P(cols, rows, None),
        P(rows, None),
        P(cols, rows, None),
        P(rows, cols, None),
        P(None, rows),
        P(cols, rows),
        P(rows),
        P(rows, cols),
        P(rows),
        P(cols, rows),
        P(rows),
        P(rows, None),
        P(rows),
    )
    out_placed = (
        P(cols, rows, None),
        P(cols, rows, None),
        P(rows, None),
        P(rows, cols, None),
        P(None, rows),
        P(cols, rows),
        P(rows),
        P(rows, cols),
        P(rows),
        P(cols, rows),
        P(rows),
        P(rows, cols),
        P(rows),
    )
    body = fast_body if (ny, nx) == (2, 2) else make_body(ny, nx)
    return jax.shard_map(
        body, mesh=fine, in_specs=placed, out_specs=out_placed, check_vma=False
    )
```

```python
import functools
import math

import jax
import jax.numpy as jnp
from jax import lax
from jax.experimental import pallas as pl
from jax.experimental.pallas import tpu as pltpu
from jax.sharding import Mesh, PartitionSpec as P

HD = 64
NZ = 4
NC = 2
norm_eps = 1e-06
f32 = jnp.float32
bf16 = jnp.bfloat16


def flip_bits(array, axis, count, index):
    bit = 1
    while bit < count:
        shape = array.shape
        view = array.reshape(
            shape[:axis] + (count // (2 * bit), 2, bit) + shape[axis + 1 :]
        )
        swapped = jnp.flip(view, axis=axis + 1)
        on = ((index // bit) % 2) == 1
        array = jnp.where(on, swapped, view).reshape(shape)
        bit *= 2
    return array


def swap_with(array, axis_name, count, offset):
    return lax.ppermute(array, axis_name, [(i, i ^ offset) for i in range(count)])


def layer_stats(rows):
    center = rows - jnp.mean(rows, axis=-1, keepdims=True)
    scale = lax.rsqrt(jnp.mean(center * center, axis=-1, keepdims=True) + norm_eps)
    return center * scale, scale


def layer_back(grad, unit, scale):
    return scale * (
        grad
        - jnp.mean(grad, axis=-1, keepdims=True)
        - unit * jnp.mean(grad * unit, axis=-1, keepdims=True)
    )


def split_three(values):
    high = lax.reduce_precision(values, 8, 7)
    rest = values - high
    middle = lax.reduce_precision(rest, 8, 7)
    return [part.astype(bf16) for part in (high, middle, rest - middle)]


def dot(a, b, dims):
    return lax.dot_general(a, b, (dims, ((), ())), preferred_element_type=f32)


def attn_forward(queries, keys, values, factor):
    samples, rows, width = queries.shape
    heads = width // HD
    qh = queries.reshape(samples, rows, heads, HD)
    kh = keys.reshape(samples, keys.shape[1], heads, HD)
    vh = values.reshape(samples, keys.shape[1], heads, HD)
    scores = jnp.einsum("sqhe,skhe->shqk", qh, kh, preferred_element_type=f32) * factor
    top = jnp.max(scores, axis=-1, keepdims=True)
    exps = jnp.exp(scores - top)
    total = jnp.sum(exps, axis=-1, keepdims=True)
    probs = (exps / total).astype(bf16)
    mixed = jnp.einsum("shqk,skhe->sqhe", probs, vh, preferred_element_type=f32)
    return mixed.reshape(queries.shape).astype(bf16), (top + jnp.log(total))


def attn_backward(queries, keys, values, grads, log_norm, factor):
    samples, rows, width = queries.shape
    heads = width // HD
    qh = queries.reshape(samples, rows, heads, HD)
    gh = grads.reshape(samples, rows, heads, HD)
    kh = keys.reshape(samples, keys.shape[1], heads, HD)
    vh = values.reshape(samples, keys.shape[1], heads, HD)
    scores = jnp.einsum("sqhe,skhe->shqk", qh, kh, preferred_element_type=f32) * factor
    probs = jnp.exp(scores - log_norm)
    dprobs = jnp.einsum("sqhe,skhe->shqk", gh, vh, preferred_element_type=f32)
    delta = jnp.sum(probs * dprobs, axis=-1, keepdims=True)
    dscores = (probs * (dprobs - delta)).astype(bf16)
    dq = jnp.einsum("shqk,skhe->sqhe", dscores, kh, preferred_element_type=f32) * factor
    dk = jnp.einsum("shqk,sqhe->skhe", dscores, qh, preferred_element_type=f32) * factor
    dv = jnp.einsum("shqk,sqhe->skhe", probs.astype(bf16), gh, preferred_element_type=f32)
    return dq.reshape(queries.shape), dk.reshape(keys.shape), dv.reshape(keys.shape)


def make_body(ny, nx):
    def to_cores(k):
        return [
            (c * NZ + z, (z // 2) * NZ + c * 2 + ((z % 2) ^ k))
            for c in range(NC)
            for z in range(NZ)
        ]

    def body(
        tokens,
        conditioning,
        cotangent,
        w_qkv,
        b_qkv,
        w_proj,
        b_proj,
        w_fc1,
        b_fc1,
        w_fc2,
        b_fc2,
        w_ada,
        b_ada,
    ):
        y, c = lax.axis_index("y"), lax.axis_index("c")
        z, x = lax.axis_index("z"), lax.axis_index("x")
        z0, z1 = z % 2, z // 2
        place, ns, D = tokens.shape
        q = ns // 2
        L = 2 * place
        dp = ny * NC
        B = D // dp
        own = y * NC + c
        hpt = w_qkv.shape[1]
        HW = hpt * HD
        F = w_fc1.shape[1]
        FF = F * NZ * nx
        factor = HD ** (-0.5)

        def rel(array):
            shape = array.shape
            view = array.reshape(shape[:-1] + (ny, NC, B))
            view = flip_bits(view, len(shape) - 1, ny, y)
            view = flip_bits(view, len(shape), NC, c)
            return view.reshape(shape)

        def spread(array):
            view = array.reshape(place, 2, q, D)
            first = jnp.where(z0 == 0, view[:, 0], view[:, 1])
            second = jnp.where(z0 == 0, view[:, 1], view[:, 0])
            got = [
                lax.ppermute(piece, ("c", "z"), to_cores(k))
                for k, piece in enumerate((first, second))
            ]
            return jnp.concatenate([g.transpose(1, 0, 2) for g in got], axis=1)

        def collect(array):
            pieces = [
                array[:, k * place : (k + 1) * place].transpose(1, 0, 2) for k in range(2)
            ]
            got = [
                lax.ppermute(piece, ("c", "z"), [(b, a) for a, b in to_cores(k)])
                for k, piece in enumerate(pieces)
            ]
            first = jnp.where(z0 == 0, got[0], got[1])
            second = jnp.where(z0 == 0, got[1], got[0])
            return jnp.stack([first, second], axis=1).reshape(place, ns, D)

        def gather_x(array):
            return jnp.stack(
                [array] + [swap_with(array, "x", nx, k) for k in range(1, nx)]
            )

        def reduce_x(parts):
            total = parts[0]
            for k in range(1, nx):
                total = total + swap_with(parts[k].astype(bf16), "x", nx, k).astype(f32)
            return total

        def gather_w(shard, by_rows):
            along = 1 if by_rows else 0
            over_z = jnp.concatenate(
                [shard] + [swap_with(shard, "z", NZ, k) for k in range(1, NZ)], axis=along
            )
            over_y = jnp.stack(
                [over_z] + [swap_with(over_z, "y", ny, k) for k in range(1, ny)]
            )
            other = swap_with(over_y, "c", NC, 1)
            if by_rows:
                return jnp.stack([over_y, other], axis=1).reshape(D, shard.shape[1] * NZ)
            pieces = [p for k in range(ny) for p in (over_y[k], other[k])]
            return jnp.concatenate(pieces, axis=1)

        def reduce_w(grad, by_rows):
            if by_rows:
                view = grad.reshape(ny, NC, B, NZ, grad.shape[1] // NZ)
                part = lambda ky, kc, kz: view[ky, kc, :, kz]
            else:
                view = grad.reshape(NZ, grad.shape[0] // NZ, ny, NC, B)
                part = lambda ky, kc, kz: view[kz, :, ky, kc]
            pick = lambda kc: jnp.stack(
                [jnp.stack([part(ky, kc, kz) for kz in range(NZ)]) for ky in range(ny)]
            )
            got = swap_with(pick(1).astype(bf16), "c", NC, 1)
            over_c = pick(0) + got.astype(f32)
            over_y = over_c[0]
            for k in range(1, ny):
                over_y = over_y + swap_with(over_c[k].astype(bf16), "y", ny, k).astype(f32)
            over_z = over_y[0]
            for k in range(1, NZ):
                over_z = over_z + swap_with(over_y[k].astype(bf16), "z", NZ, k).astype(f32)
            return over_z

        cond_c = jnp.stack([conditioning, swap_with(conditioning, "c", NC, 1)])
        cond_c = flip_bits(cond_c, 0, NC, c)
        cond_all = jnp.stack([cond_c] + [swap_with(cond_c, "y", ny, k) for k in range(1, ny)])
        cond_all = flip_bits(cond_all.reshape(ny, NZ, q, D), 1, NZ, z)
        act_all = jax.nn.silu(cond_all.astype(f32)).astype(bf16)
        act_rows = lax.dynamic_slice_in_dim(act_all, own * B, B, 3)

        partial_mod = dot(act_rows[:, 0].reshape(ny * q, B), w_ada, ((1,), (0,)))
        pad = lambda v, n: lax.dynamic_update_slice_in_dim(
            jnp.zeros((n,), f32), v.astype(f32), own * v.shape[0], 0
        )
        partial_mod = partial_mod + pad(b_ada, 6 * D)
        bias_vec = jnp.concatenate(
            [pad(b_qkv[0], D), pad(b_qkv[1], D), pad(b_proj, D), pad(b_fc1, FF), pad(b_fc2, D)]
        )
        partial_mod = partial_mod.reshape(ny, q * 6 * D)
        packed_mod = jnp.concatenate(
            [partial_mod, jnp.broadcast_to(bias_vec, (ny,) + bias_vec.shape)], axis=1
        )
        total_mod = packed_mod[0]
        for k in range(1, ny):
            total_mod = total_mod + swap_with(packed_mod[k], "y", ny, k)
        total_mod = total_mod + swap_with(total_mod, "c", NC, 1)
        modulation = rel(total_mod[: q * 6 * D].reshape(q, 6, 1, D))
        biases = total_mod[q * 6 * D :]
        bias_heads = biases[: 2 * D].reshape(2, NZ, nx, HW)
        bias_heads = lax.dynamic_index_in_dim(bias_heads, x, 2, keepdims=False)
        bias_heads = flip_bits(bias_heads, 1, NZ, z).reshape(2, NZ * HW)
        bias_proj = rel(biases[2 * D : 3 * D])
        bias_fc1 = biases[3 * D : 3 * D + FF].reshape(NZ, nx, F)
        bias_fc1 = lax.dynamic_index_in_dim(bias_fc1, x, 1, keepdims=False)
        bias_fc1 = flip_bits(bias_fc1, 0, NZ, z).reshape(NZ * F)
        bias_fc2 = rel(biases[3 * D + FF :])
        shift_attn, scale_attn, gate_attn, shift_mlp, scale_mlp, gate_mlp = (
            modulation[:, i] for i in range(6)
        )

        block_in = rel(spread(tokens)).astype(f32)
        w_heads = w_qkv.reshape(B, hpt, 3, HD).transpose(0, 2, 1, 3).reshape(B, 3 * HW)
        full_qkv = gather_w(w_heads, True)
        full_proj = gather_w(w_proj, False)
        full_fc1 = gather_w(w_fc1, True)
        full_fc2 = gather_w(w_fc2, False)
        grad_top = rel(spread(cotangent)).astype(f32)

        unit_in, rstd_in = layer_stats(block_in)
        normed = (unit_in * (1.0 + scale_attn) + shift_attn).astype(bf16)
        normed_all = gather_x(normed).reshape(nx * q * L, D)
        T = nx * q * L
        packed = dot(normed_all, full_qkv, ((1,), (0,))).reshape(T, NZ, 3, HW)
        queries = (packed[:, :, 0].reshape(T, NZ * HW) + bias_heads[0]).astype(bf16)
        keys = packed[:, :, 1].reshape(T, NZ * HW).astype(bf16)
        vals = (packed[:, :, 2].reshape(T, NZ * HW) + bias_heads[1]).astype(bf16)

        def by_sample(array):
            return array.reshape(nx, q, L, -1).transpose(1, 0, 2, 3).reshape(q, nx * L, -1)

        def by_rank(array):
            return array.reshape(q, nx, L, -1).transpose(1, 0, 2, 3).reshape(T, -1)

        queries, keys, vals = by_sample(queries), by_sample(keys), by_sample(vals)
        key_vals = jnp.stack([keys, vals])
        other_kv = swap_with(key_vals, "c", NC, 1)
        keys_all = jnp.concatenate([keys, other_kv[0]], axis=1)
        vals_all = jnp.concatenate([vals, other_kv[1]], axis=1)
        mixed, log_norm = attn_forward(queries, keys_all, vals_all, factor)
        mixed_rows = by_rank(mixed)
        branch_part = dot(mixed_rows, full_proj, ((1,), (0,))).reshape(nx, q, L, D)
        branch = reduce_x(branch_part) + bias_proj
        middle = block_in + gate_attn * branch
        unit_mid, rstd_mid = layer_stats(middle)
        normed_mlp = (unit_mid * (1.0 + scale_mlp) + shift_mlp).astype(bf16)
        mlp_all = gather_x(normed_mlp).reshape(T, D)
        hidden = dot(mlp_all, full_fc1, ((1,), (0,))) + bias_fc1
        activated, gelu_pull = jax.vjp(lambda h: jax.nn.gelu(h, approximate=True), hidden)
        act_low = activated.astype(bf16)
        mlp_part = dot(act_low, full_fc2, ((1,), (0,))).reshape(nx, q, L, D)
        branch_mlp = reduce_x(mlp_part) + bias_fc2
        block_out = (middle + gate_mlp * branch_mlp).astype(bf16)
        out = collect(rel(block_out))

        dgate_mlp = jnp.sum(grad_top * branch_mlp, axis=1)
        dbranch_mlp = (gate_mlp * grad_top).astype(bf16)
        g_bfc2 = jnp.sum(dbranch_mlp, axis=(0, 1), dtype=f32)
        dmlp_all = gather_x(dbranch_mlp).reshape(T, D)
        g_fc2 = reduce_w(dot(act_low, dmlp_all, ((0,), (0,))), False)
        dactiv = dot(dmlp_all, full_fc2, ((1,), (1,)))
        dhidden = gelu_pull(dactiv)[0].astype(bf16)
        g_bfc1 = jnp.sum(dhidden, axis=0, dtype=f32)
        g_fc1 = reduce_w(dot(mlp_all, dhidden, ((0,), (0,))), True)
        dnormed_mlp = reduce_x(dot(dhidden, full_fc1, ((1,), (1,))).reshape(nx, q, L, D))
        dshift_mlp = jnp.sum(dnormed_mlp, axis=1)
        dscale_mlp = jnp.sum(dnormed_mlp * unit_mid, axis=1)
        dmiddle = grad_top + layer_back(dnormed_mlp * (1.0 + scale_mlp), unit_mid, rstd_mid)
        dgate_attn = jnp.sum(dmiddle * branch, axis=1)
        dbranch = (gate_attn * dmiddle).astype(bf16)
        g_bproj = jnp.sum(dbranch, axis=(0, 1), dtype=f32)
        dattn_all = gather_x(dbranch).reshape(T, D)
        g_proj = reduce_w(dot(mixed_rows, dattn_all, ((0,), (0,))), False)
        dmixed = by_sample(dot(dattn_all, full_proj, ((1,), (1,))).astype(bf16))
        dq, dk, dv = attn_backward(queries, keys_all, vals_all, dmixed, log_norm, factor)
        half = nx * L
        dkv = jnp.stack([dk, dv])
        got_dkv = swap_with(dkv[:, :, half:].astype(bf16), "c", NC, 1)
        dkv = (dkv[:, :, :half] + got_dkv.astype(f32)).astype(bf16)
        dq = dq.astype(bf16)
        g_bq = jnp.sum(dq, axis=(0, 1), dtype=f32)
        g_bv = jnp.sum(dkv[1], axis=(0, 1), dtype=f32)
        dpacked = jnp.stack(
            [by_rank(v).reshape(T, NZ, HW) for v in (dq, dkv[0], dkv[1])], axis=2
        ).reshape(T, NZ * 3 * HW)
        g_qkv = reduce_w(dot(normed_all, dpacked, ((0,), (0,))), True)
        g_qkv = g_qkv.reshape(B, 3, hpt, HD).transpose(0, 2, 1, 3).reshape(B, hpt, 3 * HD)
        dnormed = reduce_x(dot(dpacked, full_qkv, ((1,), (1,))).reshape(nx, q, L, D))
        dshift_attn = jnp.sum(dnormed, axis=1)
        dscale_attn = jnp.sum(dnormed * unit_in, axis=1)
        dblock = dmiddle + layer_back(dnormed * (1.0 + scale_attn), unit_in, rstd_in)
        d_tokens = collect(rel(dblock.astype(bf16))).astype(f32)

        dmod = jnp.stack(
            [dshift_attn, dscale_attn, dgate_attn, dshift_mlp, dscale_mlp, dgate_mlp], axis=1
        )
        here = (jnp.arange(nx) == x).astype(f32)[:, None]

        def head_bias(vec, width):
            vec = flip_bits(vec.reshape(NZ, 1, width), 0, NZ, z)
            return (vec * here).reshape(NZ * nx * width)

        small = jnp.concatenate(
            [
                rel(dmod).reshape(q * 6 * D),
                head_bias(g_bq, HW),
                head_bias(g_bv, HW),
                rel(g_bproj),
                head_bias(g_bfc1, F),
                rel(g_bfc2),
            ]
        )
        for k in range(1, nx):
            small_k = swap_with(small, "x", nx, k)
            total = small_k if k == 1 else total + small_k
        small = small + total
        small = small + swap_with(small, "c", NC, 1)
        cut = q * 6 * D
        over_z = [small] + [swap_with(small, "z", NZ, k) for k in range(1, NZ)]
        bias_sum = sum(v[cut:] for v in over_z)
        flat = jnp.concatenate([v[:cut] for v in over_z] + [bias_sum])
        over_y = [flat] + [swap_with(flat, "y", ny, k) for k in range(1, ny)]
        bias_sum = sum(v[NZ * cut :] for v in over_y)
        dmod_all = jnp.stack([v[: NZ * cut] for v in over_y]).reshape(ny * NZ * q, 6 * D)

        take = lambda v, n: lax.dynamic_slice_in_dim(v, own * n, n, 0)
        out_bqkv = jnp.stack([take(bias_sum[:D], B), take(bias_sum[D : 2 * D], B)])
        out_bproj = take(bias_sum[2 * D : 3 * D], B)
        out_bfc1 = take(bias_sum[3 * D : 3 * D + FF], FF // dp)
        out_bfc2 = take(bias_sum[3 * D + FF :], B)
        out_bada = take(jnp.sum(dmod_all, axis=0), 6 * D // dp)
        cols = 6 * D // (NZ * nx)
        dmod_cols = lax.dynamic_slice_in_dim(dmod_all, (z * nx + x) * cols, cols, 1)
        act_mine = act_rows.reshape(ny * NZ * q, B)
        out_ada = dot(
            jnp.concatenate([act_mine] * 3),
            jnp.concatenate(split_three(dmod_cols)),
            ((0,), (0,)),
        )
        dact = sum(
            dot(part, w_ada, ((1,), (1,))) for part in split_three(dmod_all)
        ).reshape(ny, NZ, q, B)
        over_y = jnp.stack([dact[0]] + [swap_with(dact[k], "y", ny, k) for k in range(1, ny)])
        over_y = flip_bits(over_y, 1, NZ, z)
        over_y = flip_bits(over_y.reshape(ny, NC, 2 * q, B), 1, NC, c)
        other = swap_with(over_y[:, 1], "c", NC, 1)
        dact_rows = jnp.stack([over_y[:, 0], other], axis=1)
        dact_rows = rel(dact_rows.transpose(2, 0, 1, 3).reshape(ns, D))
        silu_pull = jax.vjp(jax.nn.silu, conditioning.astype(f32))[1]
        d_cond = silu_pull(dact_rows)[0]
        return (
            out,
            d_tokens,
            d_cond,
            g_qkv,
            out_bqkv,
            g_proj,
            out_bproj,
            g_fc1,
            out_bfc1,
            g_fc2,
            out_bfc2,
            out_ada,
            out_bada,
        )

    return body


LOG2E = 1.4426950408889634


def nn(a, b):
    return lax.dot_general(a, b, (((1,), (0,)), ((), ())), preferred_element_type=f32)


def nt(a, b):
    return lax.dot_general(a, b, (((1,), (1,)), ((), ())), preferred_element_type=f32)


def lanes(ref, block, width=256):
    return ref[:, pl.ds(pl.multiple_of(block * width, width), width)]


def total_rows(array):
    return jnp.sum(array, axis=0, keepdims=True)


def whole(shape):
    zeros = (0,) * len(shape)
    return pl.BlockSpec(shape, lambda *_: zeros)


def kernel_call(body, table, operands, in_specs, out_specs, outs, steps=1, scratch=(), flops=0, name=None):
    moved = sum(o.size * o.dtype.itemsize for o in operands)
    listed = outs if isinstance(outs, list) else [outs]
    moved += sum(math.prod(o.shape) * jnp.dtype(o.dtype).itemsize for o in listed)
    return pl.pallas_call(
        body,
        grid_spec=pltpu.PrefetchScalarGridSpec(
            num_scalar_prefetch=1,
            grid=(steps,),
            in_specs=in_specs,
            out_specs=out_specs,
            scratch_shapes=list(scratch),
        ),
        out_shape=outs,
        cost_estimate=pl.CostEstimate(flops=flops // 1000, bytes_accessed=moved // 1000, transcendentals=0),
        name=name,
    )(table, *operands)


def shaped(shape, dtype):
    return jax.ShapeDtypeStruct(shape, dtype)


COLS = 512


def block_spec(rows, cols):
    return pl.BlockSpec((2, 1, rows, cols), lambda j, t: (0, j, 0, 0))


def halves_specs():
    return [block_spec(128, COLS)] * 4


def halves(refs, kc, ky, cols):
    return jnp.concatenate([refs[kc][ky, 0, :, cols], refs[2 + kc][ky, 0, :, cols]], axis=0)


def column_spec(width, rows=256):
    return pl.BlockSpec((rows, width), lambda j, t: (0, j))


PAIRS = [(kc, ky) for kc in range(2) for ky in range(2)]


def mod_kernel(t, act, w_ada, b_ada, b_qkv, b_proj, b_fc1, b_fc2, out):
    own = t[13]

    def placed(vec, count):
        tiled = jnp.concatenate([vec.astype(f32)] * count, axis=1)
        width = vec.shape[1]
        lane = lax.broadcasted_iota(jnp.int32, tiled.shape, 1)
        here = (lane >= own * width) & (lane < own * width + width)
        return jnp.where(here, tiled, 0.0)

    bias_ada = placed(b_ada[...], 4)
    rows = []
    for i in range(6):
        part = slice(i * 1024, (i + 1) * 1024)
        rows.append(nn(act[...], w_ada[:, part]) + bias_ada[:, part])
    tail = [placed(b_proj[...], 4), placed(b_fc2[...], 4), placed(b_qkv[0:1], 4), placed(b_qkv[1:2], 4)]
    fc1 = b_fc1[...].astype(f32)
    tail += [jnp.where(own == r, fc1, 0.0) for r in range(4)]
    tail += [jnp.zeros((1, 1024), f32)] * 2
    for ky in range(2):
        out[ky] = jnp.concatenate([r[ky : ky + 1] for r in rows] + tail, axis=0)


def norm(rows):
    center = rows - jnp.mean(rows, axis=-1, keepdims=True)
    scale = lax.rsqrt(jnp.mean(center * center, axis=-1, keepdims=True) + norm_eps)
    return center * scale, scale


def ln_kernel(t, first, second, mod, out):
    for i, ref in enumerate((first, second)):
        unit, _ = norm(ref[...].astype(f32))
        out[i * 128 : (i + 1) * 128] = (unit * (1.0 + mod[1:2]) + mod[0:1]).astype(bf16)


def dmlp_kernel(t, first, second, mod, out, sums):
    total = jnp.zeros((1, 1024), f32)
    for i, ref in enumerate((first, second)):
        grad = (mod[5:6] * ref[...].astype(f32)).astype(bf16)
        out[i * 128 : (i + 1) * 128] = grad
        total = total + total_rows(grad.astype(f32))
    sums[...] = total


def qkv_kernel(t, x, *refs):
    ws, (bias, q, kv) = refs[:4], refs[4:]
    acc = jnp.zeros((256, 384), f32)
    for kc, ky in PAIRS:
        acc = acc + nn(lanes(x, t[kc * 2 + ky]), halves(ws, kc, ky, slice(0, 384)))
    q[...] = (acc[:, :128] + bias[8:9]).astype(bf16)
    kv[0] = acc[:, 128:256].astype(bf16)
    kv[1] = (acc[:, 256:] + bias[9:10]).astype(bf16)


def attn_kernel(t, q, a, b, c, d, mixed, lse):
    scale = HD**-0.5 * LOG2E
    chunks = (a, b, c, d)
    keys = jnp.concatenate([r[0] for r in chunks], axis=0)
    vals_t = jnp.concatenate([r[1] for r in chunks], axis=0).T
    lane = lax.broadcasted_iota(jnp.int32, (256, 128), 1)
    queries = q[...]
    parts = []
    for h in range(2):
        qm = jnp.where((lane // HD) == h, queries, jnp.zeros_like(queries))
        s = nt(keys, qm)
        top = jnp.max(s, axis=0, keepdims=True)
        p = jnp.exp2((s - top) * scale)
        total = jnp.sum(p, axis=0, keepdims=True)
        o = nn(vals_t, p.astype(bf16)) / total
        parts.append(o[h * HD : (h + 1) * HD])
        lse[0, h : h + 1] = top * scale + jnp.log2(total)
    mixed[...] = jnp.concatenate(parts, axis=0).T.astype(bf16)


def attn_back_kernel(t, q, do, mixed, lse, a, b, c, d, dq, near, far):
    factor = HD**-0.5
    scale = factor * LOG2E
    lane = lax.broadcasted_iota(jnp.int32, (256, 128), 1)
    queries, grads = q[...], do[...]
    product_t = (grads.astype(f32) * mixed[...].astype(f32)).T
    zero = jnp.zeros_like(queries)
    qms = [jnp.where((lane // HD) == h, queries, zero) for h in range(2)]
    gms = [jnp.where((lane // HD) == h, grads, zero) for h in range(2)]
    deltas = [total_rows(product_t[h * HD : (h + 1) * HD]) for h in range(2)]
    dq_t = [jnp.zeros((128, 256), f32) for _ in range(2)]
    for i, ref in enumerate((a, b, c, d)):
        key, val = ref[0], ref[1]
        key_t = key.T
        dk = jnp.zeros((256, 128), f32)
        dv = jnp.zeros((256, 128), f32)
        for h in range(2):
            p = jnp.exp2(nt(key, qms[h]) * scale - lse[0, h : h + 1])
            ds = (p * (nt(val, gms[h]) - deltas[h])).astype(bf16)
            dv = dv + nn(p.astype(bf16), gms[h])
            dk = dk + nn(ds, qms[h])
            dq_t[h] = dq_t[h] + nn(key_t, ds)
        out = (near, far)[i // 2]
        rows = slice((i % 2) * 256, (i % 2) * 256 + 256)
        out[0, rows] = (dk * factor).astype(bf16)
        out[1, rows] = dv.astype(bf16)
    both = jnp.concatenate([dq_t[h][h * HD : (h + 1) * HD] for h in range(2)], axis=0)
    dq[...] = (both * factor).T.astype(bf16)


def unpack_proj(refs, kc, ky):
    return jnp.concatenate([refs[kc][ky, 0, :, 384:], refs[2 + kc][ky, 0, :, 384:]], axis=1)


def proj_kernel(t, mixed, *refs):
    ws, (out, acc) = refs[:4], refs[4:]
    j = pl.program_id(0)

    @pl.when(j == 0)
    def _():
        acc[...] = jnp.zeros_like(acc)

    for i, (kc, ky) in enumerate(PAIRS):
        acc[i] += nn(mixed[...], unpack_proj(ws, kc, ky))

    @pl.when(j == 3)
    def _():
        for i in range(4):
            out[:, pl.ds(pl.multiple_of(t[i] * 256, 256), 256)] = acc[i].astype(out.dtype)


def proj_back_kernel(t, grad, *refs):
    ws, out = refs[:4], refs[4]
    acc = jnp.zeros((256, 128), f32)
    for kc, ky in PAIRS:
        acc = acc + nt(lanes(grad, t[kc * 2 + ky]), unpack_proj(ws, kc, ky))
    out[...] = acc.astype(bf16)


def mid_kernel(t, first, second, part, got, mod, branch, middle, out):
    for i, ref in enumerate((first, second)):
        rows = slice(i * 128, (i + 1) * 128)
        br = part[rows] + got[rows].astype(f32) + mod[6:7]
        mid = ref[...].astype(f32) + mod[2:3] * br
        unit, _ = norm(mid)
        branch[rows] = br
        middle[rows] = mid
        out[rows] = (unit * (1.0 + mod[4:5]) + mod[3:4]).astype(bf16)


def fc1_kernel(t, x, wo, wt, bias, act, slope):
    j = pl.program_id(0)
    h = jnp.zeros((256, COLS), f32)
    for kc, ky in PAIRS:
        h = h + nn(lanes(x, t[kc * 2 + ky]), (wo, wt)[kc][ky, 0])
    h = h + bias[pl.ds(10 + t[8 + j], 1), :]
    root = 0.7978845608028654
    inner = jnp.tanh(root * h * (1.0 + 0.044715 * h * h))
    half = 0.5 * (1.0 + inner)
    act[...] = (h * half).astype(bf16)
    slope[...] = (half + (0.5 * root) * h * (1.0 - inner * inner) * (1.0 + 3 * 0.044715 * h * h)).astype(bf16)


def fc2_kernel(t, act, wo, wt, out, acc):
    j = pl.program_id(0)

    @pl.when(j == 0)
    def _():
        acc[...] = jnp.zeros_like(acc)

    for i, (kc, ky) in enumerate(PAIRS):
        w = (wo, wt)[kc]
        acc[i] += nn(act[:, :256], w[ky, 0, :, :256]) + nn(act[:, 256:], w[ky, 0, :, 256:])

    @pl.when(j == 3)
    def _():
        for i in range(4):
            out[:, pl.ds(pl.multiple_of(t[i] * 256, 256), 256)] = acc[i].astype(out.dtype)


def mlp_back_kernel(t, grad, slope, w2o, w2t, w1o, w1t, dh, sums, out, acc):
    j = pl.program_id(0)

    @pl.when(j == 0)
    def _():
        acc[...] = jnp.zeros_like(acc)

    left = jnp.zeros((256, 256), f32)
    right = jnp.zeros((256, 256), f32)
    for kc, ky in PAIRS:
        w, g = (w2o, w2t)[kc], lanes(grad, t[kc * 2 + ky])
        left = left + nt(g, w[ky, 0, :, :256])
        right = right + nt(g, w[ky, 0, :, 256:])
    dhidden = (jnp.concatenate([left, right], axis=1) * slope[...].astype(f32)).astype(bf16)
    dh[...] = dhidden
    sums[...] = total_rows(dhidden.astype(f32))
    for i, (kc, ky) in enumerate(PAIRS):
        acc[i] += nt(dhidden, (w1o, w1t)[kc][ky, 0])

    @pl.when(j == 3)
    def _():
        for i in range(4):
            out[:, pl.ds(pl.multiple_of(t[i] * 256, 256), 256)] = acc[i].astype(out.dtype)


def keep_rows(own, other, turned):
    @pl.when(pl.program_id(0) == 0)
    def _():
        for i in range(4):
            part = slice(i * 256, (i + 1) * 256)
            turned[part] = jnp.concatenate([own[:, part], other[:, part]], axis=0).T


def feature_rows(turned, block):
    return turned[pl.ds(pl.multiple_of(block * 256, 256), 256)]


def fc1_grads_kernel(t, xo, xt, dho, dht, keep, send, turned):
    keep_rows(xo, xt, turned)
    dh = jnp.concatenate([dho[...], dht[...]], axis=0)
    for i, (kc, ky) in enumerate(PAIRS):
        (keep, send)[kc][ky, 0] = nn(feature_rows(turned, t[i]), dh).astype(bf16)


def fc2_grads_kernel(t, acto, actt, go, gt, keep, send):
    act_t = jnp.concatenate([acto[...], actt[...]], axis=0).T
    for i, (kc, ky) in enumerate(PAIRS):
        grad = jnp.concatenate([lanes(go, t[i]), lanes(gt, t[i])], axis=0)
        fc2 = nn(act_t, grad).astype(bf16)
        (keep, send)[kc][ky, 0] = jnp.concatenate([fc2[:256], fc2[256:]], axis=1)


def proj_grads_kernel(t, mo, mt, go, gt, keep, send):
    mixed_t = jnp.concatenate([mo[...], mt[...]], axis=0).T
    for i, (kc, ky) in enumerate(PAIRS):
        grad = jnp.concatenate([lanes(go, t[i]), lanes(gt, t[i])], axis=0)
        (keep, send)[kc][ky, 0] = nn(mixed_t, grad).astype(bf16)


def qkv_grads_kernel(t, xo, xt, dpo, dpt, keep0, send0, keep1, send1, turned):
    keep_rows(xo, xt, turned)
    dpacked = jnp.concatenate([dpo[0], dpt[0]], axis=0)
    for i, (kc, ky) in enumerate(PAIRS):
        grad = nn(feature_rows(turned, t[i]), dpacked).astype(bf16)
        (keep0, send0)[kc][ky, 0] = grad[:128]
        (keep1, send1)[kc][ky, 0] = grad[128:]


def dmid_kernel(t, part, got, middle, branch, first, second, mod, dmid, out, sums):
    rows_of = []
    for i, ref in enumerate((first, second)):
        rows = slice(i * 128, (i + 1) * 128)
        dn = part[rows] + got[rows].astype(f32)
        unit, scale = norm(middle[rows])
        grad = dn * (1.0 + mod[4:5])
        back = scale * (
            grad
            - jnp.mean(grad, axis=-1, keepdims=True)
            - unit * jnp.mean(grad * unit, axis=-1, keepdims=True)
        )
        dm = ref[...].astype(f32) + back
        dbranch = (mod[2:3] * dm).astype(bf16)
        dmid[rows] = dm
        out[rows] = dbranch
        rows_of.append(
            [dn, dn * unit, dm * branch[rows], dbranch.astype(f32)]
        )
    sums[...] = jnp.concatenate(
        [total_rows(a) + total_rows(b) for a, b in zip(*rows_of)] + [jnp.zeros((4, 1024), f32)], axis=0
    )


def out_kernel(t, middle, part, got, first, second, mod, out0, out1, sums):
    total = jnp.zeros((1, 1024), f32)
    for i, (ref, out) in enumerate(((first, out0), (second, out1))):
        rows = slice(i * 128, (i + 1) * 128)
        branch = part[rows] + got[rows].astype(f32) + mod[7:8]
        out[...] = (middle[rows] + mod[5:6] * branch).astype(bf16)
        total = total + total_rows(ref[...].astype(f32) * branch)
    sums[...] = total


def qkv_back_kernel(t, dqo, dqt, n0, n1, f0, f1, *refs):
    ws, (packo, packt, sums, outo, outt, acco, acct) = refs[:4], refs[4:]
    j = pl.program_id(0)

    @pl.when(j == 0)
    def _():
        acco[...] = jnp.zeros_like(acco)
        acct[...] = jnp.zeros_like(acct)

    dkv = n0[...].astype(f32) + n1[...].astype(f32) + f0[...].astype(f32) + f1[...].astype(f32)
    dkv = dkv.astype(bf16)
    dqs = (dqo[...], dqt[...])
    packed = [
        jnp.concatenate([dqs[i], dkv[0, i * 256 : i * 256 + 256], dkv[1, i * 256 : i * 256 + 256]], axis=1)
        for i in range(2)
    ]
    packo[0] = packed[0]
    packt[0] = packed[1]
    sums[...] = jnp.concatenate(
        [
            total_rows(dqs[0].astype(f32)) + total_rows(dqs[1].astype(f32)),
            total_rows(dkv[1].astype(f32)),
            jnp.zeros((6, 128), f32),
        ],
        axis=0,
    )
    for i, (kc, ky) in enumerate(PAIRS):
        w = halves(ws, kc, ky, slice(0, 384))
        acco[i] += nt(packed[0], w)
        acct[i] += nt(packed[1], w)

    @pl.when(j == 3)
    def _():
        for i in range(4):
            where = pl.ds(pl.multiple_of(t[i] * 256, 256), 256)
            outo[:, where] = acco[i]
            outt[:, where] = acct[i].astype(bf16)


def din_kernel(t, part, got, dmid, first, second, mod, out0, out1, sums):
    rows_of = []
    for i, (ref, out) in enumerate(((first, out0), (second, out1))):
        rows = slice(i * 128, (i + 1) * 128)
        dn = part[rows] + got[rows].astype(f32)
        unit, scale = norm(ref[...].astype(f32))
        grad = dn * (1.0 + mod[1:2])
        back = scale * (
            grad
            - jnp.mean(grad, axis=-1, keepdims=True)
            - unit * jnp.mean(grad * unit, axis=-1, keepdims=True)
        )
        out[...] = (dmid[rows] + back).astype(bf16)
        rows_of.append([dn, dn * unit])
    sums[...] = jnp.concatenate([total_rows(a) + total_rows(b) for a, b in zip(*rows_of)], axis=0)


def pack_kernel(t, qkv, proj, fc2, upper, lower, side):
    for i, out in enumerate((upper, lower)):
        rows = qkv[i * 128 : (i + 1) * 128]
        parts = [rows[:, 192 * g + HD * k : 192 * g + HD * k + HD] for k in range(3) for g in range(2)]
        out[0] = jnp.concatenate(parts + [proj[:, i * 128 : (i + 1) * 128]], axis=1)
    side[0] = jnp.concatenate([fc2[:256], fc2[256:]], axis=1)


def assemble_kernel(t, up, up_got, low, low_got, out):
    for i, (own, got) in enumerate(((up, up_got), (low, low_got))):
        rows = own[0].astype(f32) + got[0].astype(f32)
        parts = [rows[:, 128 * k + HD * g : 128 * k + HD * g + HD] for g in range(2) for k in range(3)]
        out[i * 128 : (i + 1) * 128] = jnp.concatenate(parts, axis=1)


def small_kernel(t, din_sums, dgate_mlp, dmid_sums, bfc2, qkv_sums, fc1o, fc1t, out):
    out[...] = jnp.zeros_like(out)
    out[0:2] = din_sums[...]
    out[2:3] = dmid_sums[2:3]
    out[3:5] = dmid_sums[0:2]
    out[5:6] = dgate_mlp[...]
    out[6:7] = dmid_sums[3:4]
    out[7:8] = bfc2[...]
    for j in range(4):
        where = pl.ds(pl.multiple_of(t[4 + j] * 128, 128), 128)
        out[8:10, where] = qkv_sums[0:2, j * 128 : (j + 1) * 128]
        fc1 = fc1o[:, j * COLS : (j + 1) * COLS] + fc1t[:, j * COLS : (j + 1) * COLS]
        for zz in range(4):
            for xx in range(2):
                @pl.when((t[8 + j] == zz) & (t[12] == xx))
                def _(fc1=fc1, zz=zz, xx=xx):
                    out[10 + zz : 11 + zz, xx * COLS : (xx + 1) * COLS] = fc1


def fast_body(
    tokens, conditioning, cotangent, w_qkv, b_qkv, w_proj, b_proj, w_fc1, b_fc1, w_fc2, b_fc2, w_ada, b_ada
):
    y, c = lax.axis_index("y"), lax.axis_index("c")
    z, x = lax.axis_index("z"), lax.axis_index("x")
    z0, z1 = z % 2, z // 2
    D = 1024
    own = y * 2 + c
    blocks = [(y ^ ky) * 2 + (c ^ kc) for kc, ky in PAIRS]
    z_of = [z ^ k1 ^ (2 * k2) for k1 in range(2) for k2 in range(2)]
    table = jnp.stack(blocks + [zz * 2 + x for zz in z_of] + z_of + [x, own]).astype(jnp.int32)
    call = functools.partial(kernel_call)

    def flip(v, axis, count, offset):
        return lax.ppermute(v, axis, [(i, i ^ offset) for i in range(count)])

    def route(k):
        return [
            (cc * 4 + zz, (zz // 2) * 4 + cc * 2 + ((zz % 2) ^ k)) for cc in range(2) for zz in range(4)
        ]

    def spread_parts(array):
        flat = array.reshape(128, 2 * D)
        low, high = flat[:, :D], flat[:, D:]
        return jnp.where(z0 == 0, low, high), jnp.where(z0 == 0, high, low)

    def spread(array):
        return [lax.ppermute(p, ("c", "z"), route(k)) for k, p in enumerate(spread_parts(array))]

    def send_back(pieces):
        return [lax.ppermute(p, ("c", "z"), [(b, a) for a, b in route(k)]) for k, p in enumerate(pieces)]

    def collect(got, dtype, *others):
        got = lax.optimization_barrier((*got, *others))[:2]
        low = jnp.where(z0 == 0, got[0], got[1])
        high = jnp.where(z0 == 0, got[1], got[0])
        return jnp.concatenate([low, high], axis=1).astype(dtype).reshape(128, 2, D)

    def after(value, *others):
        return lax.optimization_barrier((value, *others))[0]

    STEPS = {"near": ("z", 4, 1), "far": ("z", 4, 2), "y": ("y", 2, 1)}

    cut = lax.optimization_barrier

    def widen(v, step, *others):
        v, got = lax.optimization_barrier((v, flip(v, *STEPS[step]), *others))[:2]
        return jnp.concatenate([v, got])

    def both_cores(v):
        v = v.reshape((2, 4) + v.shape[1:])
        return [v, flip(v, "c", 2, 1)]

    def cross(keep, send):
        flat = (8,) + keep.shape[2:]
        return keep.reshape(flat), flip(send.reshape(flat), "c", 2, 1)

    def fold(pair, *others):
        own, got = lax.optimization_barrier((*pair, *others))[:2]
        half = own.shape[0] // 2
        cut = lambda v, k: v[k * half : (k + 1) * half].astype(f32)
        return [(cut(own, k) + cut(got, k)).astype(bf16) for k in range(2)]

    def onward(parts, step):
        return parts[0], flip(parts[1], *STEPS[step])

    def total(pair, *others):
        own, got = lax.optimization_barrier((*pair, *others))[:2]
        v = own.astype(f32) + got.astype(f32)
        return v.reshape(v.shape[-2:])

    cond_c = jnp.stack([conditioning, flip(conditioning, "c", 2, 1)])
    cond_c = jnp.where(c == 0, cond_c, cond_c[::-1])
    cond_all = jnp.stack([cond_c, flip(cond_c, "y", 2, 1)]).reshape(2, 4, D)
    tok_parts = spread_parts(tokens)
    tok = [lax.ppermute(p, ("c", "z"), route(k)) for k, p in enumerate(tok_parts)]
    upper, lower, packed_fc2 = call(
        pack_kernel,
        table,
        [w_qkv.reshape(256, 384), w_proj, w_fc2],
        [whole((256, 384)), whole((128, 256)), whole((512, 256))],
        [whole((1, 128, COLS)), whole((1, 128, COLS)), whole((1, 256, COLS))],
        [shaped((1, 128, COLS), bf16), shaped((1, 128, COLS), bf16), shaped((1, 256, COLS), bf16)],
        name="pack",
    )
    upper = widen(upper, "far")
    upper, lower, cond_all = cut((upper, lower, cond_all))
    got_up, got_low = flip(upper, *STEPS["near"]), flip(lower, *STEPS["far"])
    act_abs = jax.nn.silu(cond_all.astype(f32)).astype(bf16)
    act_abs = lax.dynamic_slice_in_dim(act_abs, own * 256, 256, 2)
    act_here = lax.dynamic_slice_in_dim(act_abs, z, 1, 1)[:, 0]
    packed_mod = call(
        mod_kernel,
        table,
        [
            jnp.pad(act_here, ((0, 6), (0, 0))),
            w_ada,
            b_ada.reshape(1, -1),
            b_qkv,
            b_proj.reshape(1, -1),
            b_fc1.reshape(1, -1),
            b_fc2.reshape(1, -1),
        ],
        [whole((8, 256)), whole((256, 6144)), whole((1, 1536)), whole((2, 256)), whole((1, 256)), whole((1, 1024)), whole((1, 256))],
        whole((2, 16, D)),
        shaped((2, 16, D), f32),
        flops=2 * 8 * 256 * 6144,
        name="modulate",
    )
    upper, got_up, lower, got_low, tok, packed_mod, got_mod = cut(
        (upper, got_up, lower, got_low, tok, packed_mod, flip(packed_mod[1], "y", 2, 1))
    )
    upper, lower = jnp.concatenate([upper, got_up]), jnp.concatenate([lower, got_low])
    mod = packed_mod[0] + got_mod
    mod = mod + flip(mod, "c", 2, 1)
    mod_spec = whole((16, D))

    half, full = whole((128, D)), whole((256, D))
    row_b, row_f = shaped((256, D), bf16), shaped((256, D), f32)
    lower = widen(lower, "near")
    normed = call(ln_kernel, table, [*tok, after(mod, lower)], [half, half, mod_spec], full, row_b, name="norm_in")
    normed_t = flip(normed, "x", 2, 1)
    upper = widen(upper, "y")
    w1 = after(w_fc1[None], lower)
    lower, got_low, w1, got_w1, normed_t = lax.optimization_barrier(
        (lower, flip(lower, *STEPS["y"]), w1, flip(w1, *STEPS["far"]), normed_t)
    )
    lower, w1 = jnp.concatenate([lower, got_low]), jnp.concatenate([w1, got_w1])
    wa = both_cores(upper) + both_cores(after(lower, w1))

    bias_spec = pl.BlockSpec((16, 128), lambda j, t: (0, t[4 + j]))
    pair_spec = pl.BlockSpec((2, 256, 128), lambda j, t: (0, 0, j))

    def make_qkv(rows):
        return call(
            qkv_kernel,
            table,
            [rows, *wa, mod],
            [full, *halves_specs(), bias_spec],
            [column_spec(128), pair_spec],
            [shaped((256, 512), bf16), shaped((2, 256, 512), bf16)],
            steps=4,
            flops=2 * 256 * 1024 * 1536,
            name="qkv",
        )

    q_o, kv_o = make_qkv(normed)
    far_o = flip(kv_o, "c", 2, 1)
    q_t, kv_t = make_qkv(normed_t)
    far_t = flip(kv_t, "c", 2, 1)
    chunks = [kv_o, kv_t, far_o, far_t]
    w1 = widen(w1, "near", kv_t)
    q_t, w1 = lax.optimization_barrier((q_t, w1))
    lse_spec = pl.BlockSpec((1, 2, 256), lambda j, t: (j, 0, 0))

    def attend(queries):
        return call(
            attn_kernel,
            table,
            [queries, *chunks],
            [column_spec(128)] + [pair_spec] * 4,
            [column_spec(128), lse_spec],
            [shaped((256, 512), bf16), shaped((4, 2, 256), f32)],
            steps=4,
            flops=4 * 256 * 1024 * 64 * 8 * 4,
            name="attend",
        )

    acc_d = pltpu.VMEM((4, 256, 256), f32)

    def project(rows, kind):
        return call(
            proj_kernel,
            table,
            [rows, *wa],
            [column_spec(128), *halves_specs()],
            full,
            shaped((256, D), kind),
            steps=4,
            scratch=[acc_d],
            flops=2 * 256 * 512 * 1024,
            name="project",
        )

    mixed_t, lse_t = attend(q_t)
    cot_parts = spread_parts(after(cotangent, normed))
    cot = [lax.ppermute(after(p, mixed_t), ("c", "z"), route(k)) for k, p in enumerate(cot_parts)]
    w2 = widen(after(packed_fc2, q_t), "far", mixed_t)
    part_t = project(after(mixed_t, w2), bf16)
    got_branch = flip(part_t, "x", 2, 1)
    q_o, part_t = lax.optimization_barrier((q_o, part_t))
    mixed_o, lse_o = attend(q_o)
    w1, w2 = widen(w1, "y", mixed_o), widen(w2, "near", mixed_o)
    dmlp_o, bfc2_sum = call(
        dmlp_kernel,
        table,
        [*cot, after(mod, mixed_o)],
        [half, half, mod_spec],
        [full, whole((1, D))],
        [row_b, shaped((1, D), f32)],
        name="dbranch_mlp",
    )
    dmlp_t = flip(dmlp_o, "x", 2, 1)
    mixed_o, w1, w2, got_branch, dmlp_o = lax.optimization_barrier((mixed_o, w1, w2, got_branch, dmlp_o))
    w1 = both_cores(w1)
    branch, middle, normed_mlp = call(
        mid_kernel,
        table,
        [*tok, project(mixed_o, f32), got_branch, mod],
        [half, half, full, full, mod_spec],
        [full] * 3,
        [row_f, row_f, row_b],
        name="norm_mid",
    )
    mlp_t = flip(normed_mlp, "x", 2, 1)
    wide = shaped((256, 2048), bf16)
    wide_specs = [block_spec(256, COLS)] * 2
    fc1_bias = pl.BlockSpec((16, COLS), lambda j, t: (0, t[12]))

    def up(rows):
        return call(
            fc1_kernel,
            table,
            [rows, *w1, mod],
            [full, *wide_specs, fc1_bias],
            [column_spec(COLS)] * 2,
            [wide, wide],
            steps=4,
            flops=2 * 256 * 1024 * 2048,
            name="up",
        )

    def down(act, kind):
        return call(
            fc2_kernel,
            table,
            [act, *w2],
            [column_spec(COLS), *wide_specs],
            full,
            shaped((256, D), kind),
            steps=4,
            scratch=[acc_d],
            flops=2 * 256 * 1024 * 2048,
            name="down",
        )

    def mlp_back(grad, slope, kind):
        return call(
            mlp_back_kernel,
            table,
            [grad, slope, *w2, *w1],
            [full, column_spec(COLS), *wide_specs, *wide_specs],
            [column_spec(COLS), column_spec(COLS, 1), full],
            [wide, shaped((1, 2048), f32), shaped((256, D), kind)],
            steps=4,
            scratch=[acc_d],
            flops=4 * 256 * 1024 * 2048,
            name="mlp_back",
        )

    act_o, slope_o = up(after(normed_mlp, dmlp_t))
    w2 = both_cores(widen(w2, "y", act_o, mlp_t))
    act_t, slope_t = up(after(mlp_t, act_o))
    dh_t, fc1_t, dn_t = mlp_back(dmlp_t, slope_t, bf16)
    got_dn = flip(dn_t, "x", 2, 1)
    turned = pltpu.VMEM((D, 512), bf16)
    fc2_keep, fc2_send = call(
        fc2_grads_kernel,
        table,
        [act_o, act_t, after(dmlp_o, dn_t), dmlp_t],
        [column_spec(COLS)] * 2 + [full, full],
        [block_spec(256, COLS)] * 2,
        [shaped((2, 4, 256, COLS), bf16)] * 2,
        steps=4,
        flops=4 * 256 * 1024 * 2048,
        name="fc2_grads",
    )
    g_fc2 = cross(fc2_keep, fc2_send)
    dh_o, fc1_o, dn_o = mlp_back(dmlp_o, after(slope_o, fc2_send), f32)
    g_fc2 = fold(g_fc2, dn_o)
    fc1_keep, fc1_send = call(
        fc1_grads_kernel,
        table,
        [normed_mlp, mlp_t, after(dh_o, got_dn, *g_fc2), dh_t],
        [full, full] + [column_spec(COLS)] * 2,
        [block_spec(256, COLS)] * 2,
        [shaped((2, 4, 256, COLS), bf16)] * 2,
        steps=4,
        scratch=[turned],
        flops=4 * 256 * 1024 * 2048,
        name="fc1_grads",
    )
    g_fc1 = cross(fc1_keep, fc1_send)
    g_fc2 = onward(g_fc2, "y")
    dn_o = after(dn_o, fc1_send)

    sums_spec = whole((8, D))
    dmid, dbr_o, dmid_sums = call(
        dmid_kernel,
        table,
        [dn_o, got_dn, middle, branch, *cot, mod],
        [full] * 4 + [half, half, mod_spec],
        [full, full, sums_spec],
        [row_f, row_b, shaped((8, D), f32)],
        name="norm_mid_back",
    )
    dbr_t = flip(dbr_o, "x", 2, 1)
    finish = lambda down_o, got_mlp: call(
        out_kernel,
        table,
        [middle, down_o, got_mlp, *cot, mod],
        [full] * 3 + [half, half, mod_spec],
        [half, half, whole((1, D))],
        [shaped((128, D), bf16)] * 2 + [shaped((1, D), f32)],
        name="finish",
    )

    def project_back(grad):
        return call(
            proj_back_kernel,
            table,
            [grad, *wa],
            [full, *halves_specs()],
            column_spec(128),
            shaped((256, 512), bf16),
            steps=4,
            flops=2 * 256 * 512 * 1024,
            name="project_back",
        )

    def attend_back(queries, dmixed, mixed, lse):
        long_spec = pl.BlockSpec((2, 512, 128), lambda j, t: (0, 0, j))
        return call(
            attn_back_kernel,
            table,
            [queries, dmixed, mixed, lse, *chunks],
            [column_spec(128)] * 3 + [lse_spec] + [pair_spec] * 4,
            [column_spec(128), long_spec, long_spec],
            [shaped((256, 512), bf16), shaped((2, 512, 512), bf16), shaped((2, 512, 512), bf16)],
            steps=4,
            flops=10 * 256 * 1024 * 64 * 8 * 4,
            name="attend_back",
        )

    dmixed_o = project_back(dbr_o)
    g_fc1 = fold(g_fc1, dmixed_o)
    dmixed_o = after(dmixed_o, *g_fc1)
    g_fc1 = onward(g_fc1, "y")
    dq_o, near_o, away_o = attend_back(q_o, dmixed_o, mixed_o, lse_o)
    back_o = flip(away_o, "c", 2, 1)
    g_fc2 = fold(g_fc2, away_o)
    dmixed_t = project_back(after(dbr_t, *g_fc2))
    g_fc2 = onward(g_fc2, "near")
    p_keep, p_send = call(
        proj_grads_kernel,
        table,
        [mixed_o, mixed_t, after(dbr_o, dmixed_t), dbr_t],
        [column_spec(128)] * 2 + [full, full],
        [block_spec(128, 256)] * 2,
        [shaped((2, 4, 128, 256), bf16)] * 2,
        steps=4,
        flops=4 * 256 * 512 * 1024,
        name="proj_grads",
    )
    g_proj = cross(p_keep, p_send)
    down_t = down(after(act_t, p_send), bf16)
    got_mlp = flip(down_t, "x", 2, 1)
    dmixed_t = after(dmixed_t, p_send, down_t)
    dq_t, near_t, away_t = attend_back(q_t, dmixed_t, mixed_t, lse_t)
    back_t = flip(away_t, "c", 2, 1)
    away_t, got_mlp, g_fc1, g_fc2, g_proj = cut((away_t, got_mlp, g_fc1, g_fc2, g_proj))
    g_fc1, g_fc2, g_proj = (fold(v) for v in (g_fc1, g_fc2, g_proj))
    dq_t = after(dq_t, *g_fc1, *g_fc2, *g_proj)
    g_fc2, g_fc1, g_proj = onward(g_fc2, "far"), onward(g_fc1, "near"), onward(g_proj, "y")
    long_spec = pl.BlockSpec((2, 512, 128), lambda j, t: (0, 0, j))
    pack_spec = pl.BlockSpec((1, 256, 384), lambda j, t: (j, 0, 0))
    pack_o, pack_t, qkv_sums, din_o, din_t = call(
        qkv_back_kernel,
        table,
        [dq_o, dq_t, near_o, near_t, back_o, back_t, *wa],
        [column_spec(128)] * 2 + [long_spec] * 4 + halves_specs(),
        [pack_spec, pack_spec, pl.BlockSpec((8, 128), lambda j, t: (0, j)), full, full],
        [shaped((4, 256, 384), bf16)] * 2 + [shaped((8, 512), f32), row_f, row_b],
        steps=4,
        scratch=[acc_d, acc_d],
        flops=4 * 256 * 1024 * 1536,
        name="qkv_back",
    )
    got_din = flip(din_t, "x", 2, 1)
    qkv_out = [shaped((2, 4, 128, 384), bf16)] * 4
    k0, s0, k1, s1 = call(
        qkv_grads_kernel,
        table,
        [normed, normed_t, after(pack_o, din_t), pack_t],
        [full, full, pack_spec, pack_spec],
        [block_spec(128, 384)] * 4,
        qkv_out,
        steps=4,
        scratch=[turned],
        flops=4 * 256 * 1024 * 1536,
        name="qkv_grads",
    )
    g_fc1 = fold(g_fc1, s0)
    k0, s0, k1, s1, got_din, g_fc1, g_fc2, g_proj = cut((k0, s0, k1, s1, got_din, g_fc1, g_fc2, g_proj))
    g_up, g_low = cross(k0, s0), cross(k1, s1)
    g_fc1, g_proj = onward(g_fc1, "far"), onward(fold(g_proj), "near")
    act_o = after(act_o, s0, s1)
    down_o, g_up, g_low, got_mlp = cut((down(act_o, f32), g_up, g_low, got_mlp))
    down_o, g_up, g_low = cut((down_o, fold(g_up), fold(g_low)))
    g_up, g_low = onward(g_up, "y"), onward(g_low, "y")
    out0, out1, dgate_mlp = finish(down_o, got_mlp)
    out_got = send_back([out0, out1])
    din_o = after(din_o, dgate_mlp)
    dt0, dt1, din_sums = call(
        din_kernel,
        table,
        [din_o, got_din, dmid, *tok, mod],
        [full] * 3 + [half, half, mod_spec],
        [half, half, whole((2, D))],
        [shaped((128, D), bf16)] * 2 + [shaped((2, D), f32)],
        name="norm_in_back",
    )
    din_sums, g_up, g_fc1, g_proj = cut((din_sums, g_up, g_fc1, g_proj))
    g_up, g_proj = onward(fold(g_up), "near"), onward(fold(g_proj), "far")
    g_fc1, g_fc2 = total(g_fc1), total(g_fc2, din_sums)
    g_fc2 = jnp.concatenate([g_fc2[:, :256], g_fc2[:, 256:]], axis=0)

    small = call(
        small_kernel,
        table,
        [din_sums, dgate_mlp, dmid_sums, bfc2_sum, qkv_sums, fc1_o, fc1_t],
        [whole((2, D)), whole((1, D)), sums_spec, whole((1, D)), whole((8, 512)), whole((1, 2048)), whole((1, 2048))],
        whole((16, D)),
        shaped((16, D), f32),
        name="small",
    )
    def joined(v, got):
        return jnp.concatenate([v[:-10], got[:-10], v[-10:] + got[-10:]])

    small, got, g_up, g_low, g_fc1, g_fc2 = cut((small, flip(small, "x", 2, 1), g_up, g_low, g_fc1, g_fc2))
    small = small + got
    g_up, g_low = onward(fold(g_up), "far"), onward(fold(g_low), "near")
    small, got, out_got = cut((small, flip(small, "c", 2, 1), out_got))
    small = small + got
    small, got, g_up, g_low, g_proj = cut((small, flip(small, "z", 4, 2), g_up, g_low, g_proj))
    small, dt0, dt1 = cut((joined(small, got), dt0, dt1))
    dt_got = send_back([dt0, dt1])
    g_low, g_proj = onward(fold(g_low), "far"), total(g_proj)
    out = collect(out_got, bf16)
    small, got, g_low, out, g_proj = cut((small, flip(small, "z", 4, 1), g_low, out, g_proj))
    small = joined(small, got)
    small, got, dt_got = cut((small, flip(small, "y", 2, 1), dt_got))
    small = joined(small, got)
    d_tokens = collect(dt_got, f32)
    g_qkv = call(
        assemble_kernel,
        table,
        [*g_up, *g_low],
        [whole((1, 128, 384))] * 4,
        whole((256, 384)),
        shaped((256, 384), f32),
        name="assemble",
    ).reshape(256, 2, 3 * HD)
    bias_sum = small[-10:]
    dmod_all = small[:-10].reshape(8, 6 * D)
    take = lambda v, n: lax.dynamic_slice_in_dim(v.reshape(-1), own * n, n, 0)
    out_bproj, out_bfc2 = take(bias_sum[0], 256), take(bias_sum[1], 256)
    out_bqkv = lax.dynamic_slice_in_dim(bias_sum[2:4], own * 256, 256, 1)
    out_bfc1 = take(bias_sum[4:8], 1024)
    out_bada = take(jnp.sum(dmod_all, axis=0), 1536)
    act_rel = jnp.swapaxes(flip_bits(act_abs, 1, 4, z).reshape(2, 2, 2, 256), 1, 2).reshape(8, 256)
    dmod_cols = lax.dynamic_slice_in_dim(dmod_all, (z * 2 + x) * 768, 768, 1)
    out_ada = dot(
        jnp.concatenate([act_rel] * 3), jnp.concatenate(split_three(dmod_cols)), ((0,), (0,))
    )
    dact = dot(jnp.concatenate(split_three(dmod_all)), w_ada, ((1,), (1,)))
    dact = dact[:8] + dact[8:16] + dact[16:]
    dact = jnp.swapaxes(dact.reshape(2, 2, 2, 256), 1, 2).reshape(2, 4, 256)
    dact = flip_bits(dact, 1, 4, z)
    dact = jnp.stack([dact[0], flip(dact[1], "y", 2, 1)]).reshape(2, 2, 2, 256)
    dact = jnp.where(c == 0, dact, dact[:, ::-1])
    dact = jnp.stack([dact[:, 0], flip(dact[:, 1], "c", 2, 1)], axis=1)
    dact = flip_bits(flip_bits(dact, 0, 2, y), 1, 2, c).transpose(2, 0, 1, 3).reshape(2, D)
    d_cond = jax.vjp(jax.nn.silu, conditioning.astype(f32))[1](dact)[0]
    return (
        out,
        d_tokens,
        d_cond,
        g_qkv,
        out_bqkv,
        g_proj,
        out_bproj,
        g_fc1,
        out_bfc1,
        g_fc2,
        out_bfc2,
        out_ada,
        out_bada,
    )


def solution(mesh):
    dp, tensor = mesh.shape["dp"], mesh.shape["tensor"]
    ny, nx = dp // NC, tensor // NZ
    fine = Mesh(mesh.devices.reshape(ny, NC, NZ, nx), ("y", "c", "z", "x"))
    rows, cols = ("y", "c"), ("z", "x")
    placed = (
        P(cols, rows, None),
        P(rows, None),
        P(cols, rows, None),
        P(rows, cols, None),
        P(None, rows),
        P(cols, rows),
        P(rows),
        P(rows, cols),
        P(rows),
        P(cols, rows),
        P(rows),
        P(rows, None),
        P(rows),
    )
    out_placed = (
        P(cols, rows, None),
        P(cols, rows, None),
        P(rows, None),
        P(rows, cols, None),
        P(None, rows),
        P(cols, rows),
        P(rows),
        P(rows, cols),
        P(rows),
        P(cols, rows),
        P(rows),
        P(rows, cols),
        P(rows),
    )
    body = fast_body if (ny, nx) == (2, 2) else make_body(ny, nx)
    return jax.shard_map(
        body, mesh=fine, in_specs=placed, out_specs=out_placed, check_vma=False
    )
```

```python
import functools
import math

import jax
import jax.numpy as jnp
from jax import lax
from jax.experimental import pallas as pl
from jax.experimental.pallas import tpu as pltpu
from jax.sharding import Mesh, PartitionSpec as P

HD = 64
NZ = 4
NC = 2
norm_eps = 1e-06
f32 = jnp.float32
bf16 = jnp.bfloat16


def flip_bits(array, axis, count, index):
    bit = 1
    while bit < count:
        shape = array.shape
        view = array.reshape(
            shape[:axis] + (count // (2 * bit), 2, bit) + shape[axis + 1 :]
        )
        swapped = jnp.flip(view, axis=axis + 1)
        on = ((index // bit) % 2) == 1
        array = jnp.where(on, swapped, view).reshape(shape)
        bit *= 2
    return array


def swap_with(array, axis_name, count, offset):
    return lax.ppermute(array, axis_name, [(i, i ^ offset) for i in range(count)])


def layer_stats(rows):
    center = rows - jnp.mean(rows, axis=-1, keepdims=True)
    scale = lax.rsqrt(jnp.mean(center * center, axis=-1, keepdims=True) + norm_eps)
    return center * scale, scale


def layer_back(grad, unit, scale):
    return scale * (
        grad
        - jnp.mean(grad, axis=-1, keepdims=True)
        - unit * jnp.mean(grad * unit, axis=-1, keepdims=True)
    )


def split_three(values):
    high = lax.reduce_precision(values, 8, 7)
    rest = values - high
    middle = lax.reduce_precision(rest, 8, 7)
    return [part.astype(bf16) for part in (high, middle, rest - middle)]


def dot(a, b, dims):
    return lax.dot_general(a, b, (dims, ((), ())), preferred_element_type=f32)


def attn_forward(queries, keys, values, factor):
    samples, rows, width = queries.shape
    heads = width // HD
    qh = queries.reshape(samples, rows, heads, HD)
    kh = keys.reshape(samples, keys.shape[1], heads, HD)
    vh = values.reshape(samples, keys.shape[1], heads, HD)
    scores = jnp.einsum("sqhe,skhe->shqk", qh, kh, preferred_element_type=f32) * factor
    top = jnp.max(scores, axis=-1, keepdims=True)
    exps = jnp.exp(scores - top)
    total = jnp.sum(exps, axis=-1, keepdims=True)
    probs = (exps / total).astype(bf16)
    mixed = jnp.einsum("shqk,skhe->sqhe", probs, vh, preferred_element_type=f32)
    return mixed.reshape(queries.shape).astype(bf16), (top + jnp.log(total))


def attn_backward(queries, keys, values, grads, log_norm, factor):
    samples, rows, width = queries.shape
    heads = width // HD
    qh = queries.reshape(samples, rows, heads, HD)
    gh = grads.reshape(samples, rows, heads, HD)
    kh = keys.reshape(samples, keys.shape[1], heads, HD)
    vh = values.reshape(samples, keys.shape[1], heads, HD)
    scores = jnp.einsum("sqhe,skhe->shqk", qh, kh, preferred_element_type=f32) * factor
    probs = jnp.exp(scores - log_norm)
    dprobs = jnp.einsum("sqhe,skhe->shqk", gh, vh, preferred_element_type=f32)
    delta = jnp.sum(probs * dprobs, axis=-1, keepdims=True)
    dscores = (probs * (dprobs - delta)).astype(bf16)
    dq = jnp.einsum("shqk,skhe->sqhe", dscores, kh, preferred_element_type=f32) * factor
    dk = jnp.einsum("shqk,sqhe->skhe", dscores, qh, preferred_element_type=f32) * factor
    dv = jnp.einsum("shqk,sqhe->skhe", probs.astype(bf16), gh, preferred_element_type=f32)
    return dq.reshape(queries.shape), dk.reshape(keys.shape), dv.reshape(keys.shape)


def make_body(ny, nx):
    def to_cores(k):
        return [
            (c * NZ + z, (z // 2) * NZ + c * 2 + ((z % 2) ^ k))
            for c in range(NC)
            for z in range(NZ)
        ]

    def body(
        tokens,
        conditioning,
        cotangent,
        w_qkv,
        b_qkv,
        w_proj,
        b_proj,
        w_fc1,
        b_fc1,
        w_fc2,
        b_fc2,
        w_ada,
        b_ada,
    ):
        y, c = lax.axis_index("y"), lax.axis_index("c")
        z, x = lax.axis_index("z"), lax.axis_index("x")
        z0, z1 = z % 2, z // 2
        place, ns, D = tokens.shape
        q = ns // 2
        L = 2 * place
        dp = ny * NC
        B = D // dp
        own = y * NC + c
        hpt = w_qkv.shape[1]
        HW = hpt * HD
        F = w_fc1.shape[1]
        FF = F * NZ * nx
        factor = HD ** (-0.5)

        def rel(array):
            shape = array.shape
            view = array.reshape(shape[:-1] + (ny, NC, B))
            view = flip_bits(view, len(shape) - 1, ny, y)
            view = flip_bits(view, len(shape), NC, c)
            return view.reshape(shape)

        def spread(array):
            view = array.reshape(place, 2, q, D)
            first = jnp.where(z0 == 0, view[:, 0], view[:, 1])
            second = jnp.where(z0 == 0, view[:, 1], view[:, 0])
            got = [
                lax.ppermute(piece, ("c", "z"), to_cores(k))
                for k, piece in enumerate((first, second))
            ]
            return jnp.concatenate([g.transpose(1, 0, 2) for g in got], axis=1)

        def collect(array):
            pieces = [
                array[:, k * place : (k + 1) * place].transpose(1, 0, 2) for k in range(2)
            ]
            got = [
                lax.ppermute(piece, ("c", "z"), [(b, a) for a, b in to_cores(k)])
                for k, piece in enumerate(pieces)
            ]
            first = jnp.where(z0 == 0, got[0], got[1])
            second = jnp.where(z0 == 0, got[1], got[0])
            return jnp.stack([first, second], axis=1).reshape(place, ns, D)

        def gather_x(array):
            return jnp.stack(
                [array] + [swap_with(array, "x", nx, k) for k in range(1, nx)]
            )

        def reduce_x(parts):
            total = parts[0]
            for k in range(1, nx):
                total = total + swap_with(parts[k].astype(bf16), "x", nx, k).astype(f32)
            return total

        def gather_w(shard, by_rows):
            along = 1 if by_rows else 0
            over_z = jnp.concatenate(
                [shard] + [swap_with(shard, "z", NZ, k) for k in range(1, NZ)], axis=along
            )
            over_y = jnp.stack(
                [over_z] + [swap_with(over_z, "y", ny, k) for k in range(1, ny)]
            )
            other = swap_with(over_y, "c", NC, 1)
            if by_rows:
                return jnp.stack([over_y, other], axis=1).reshape(D, shard.shape[1] * NZ)
            pieces = [p for k in range(ny) for p in (over_y[k], other[k])]
            return jnp.concatenate(pieces, axis=1)

        def reduce_w(grad, by_rows):
            if by_rows:
                view = grad.reshape(ny, NC, B, NZ, grad.shape[1] // NZ)
                part = lambda ky, kc, kz: view[ky, kc, :, kz]
            else:
                view = grad.reshape(NZ, grad.shape[0] // NZ, ny, NC, B)
                part = lambda ky, kc, kz: view[kz, :, ky, kc]
            pick = lambda kc: jnp.stack(
                [jnp.stack([part(ky, kc, kz) for kz in range(NZ)]) for ky in range(ny)]
            )
            got = swap_with(pick(1).astype(bf16), "c", NC, 1)
            over_c = pick(0) + got.astype(f32)
            over_y = over_c[0]
            for k in range(1, ny):
                over_y = over_y + swap_with(over_c[k].astype(bf16), "y", ny, k).astype(f32)
            over_z = over_y[0]
            for k in range(1, NZ):
                over_z = over_z + swap_with(over_y[k].astype(bf16), "z", NZ, k).astype(f32)
            return over_z

        cond_c = jnp.stack([conditioning, swap_with(conditioning, "c", NC, 1)])
        cond_c = flip_bits(cond_c, 0, NC, c)
        cond_all = jnp.stack([cond_c] + [swap_with(cond_c, "y", ny, k) for k in range(1, ny)])
        cond_all = flip_bits(cond_all.reshape(ny, NZ, q, D), 1, NZ, z)
        act_all = jax.nn.silu(cond_all.astype(f32)).astype(bf16)
        act_rows = lax.dynamic_slice_in_dim(act_all, own * B, B, 3)

        partial_mod = dot(act_rows[:, 0].reshape(ny * q, B), w_ada, ((1,), (0,)))
        pad = lambda v, n: lax.dynamic_update_slice_in_dim(
            jnp.zeros((n,), f32), v.astype(f32), own * v.shape[0], 0
        )
        partial_mod = partial_mod + pad(b_ada, 6 * D)
        bias_vec = jnp.concatenate(
            [pad(b_qkv[0], D), pad(b_qkv[1], D), pad(b_proj, D), pad(b_fc1, FF), pad(b_fc2, D)]
        )
        partial_mod = partial_mod.reshape(ny, q * 6 * D)
        packed_mod = jnp.concatenate(
            [partial_mod, jnp.broadcast_to(bias_vec, (ny,) + bias_vec.shape)], axis=1
        )
        total_mod = packed_mod[0]
        for k in range(1, ny):
            total_mod = total_mod + swap_with(packed_mod[k], "y", ny, k)
        total_mod = total_mod + swap_with(total_mod, "c", NC, 1)
        modulation = rel(total_mod[: q * 6 * D].reshape(q, 6, 1, D))
        biases = total_mod[q * 6 * D :]
        bias_heads = biases[: 2 * D].reshape(2, NZ, nx, HW)
        bias_heads = lax.dynamic_index_in_dim(bias_heads, x, 2, keepdims=False)
        bias_heads = flip_bits(bias_heads, 1, NZ, z).reshape(2, NZ * HW)
        bias_proj = rel(biases[2 * D : 3 * D])
        bias_fc1 = biases[3 * D : 3 * D + FF].reshape(NZ, nx, F)
        bias_fc1 = lax.dynamic_index_in_dim(bias_fc1, x, 1, keepdims=False)
        bias_fc1 = flip_bits(bias_fc1, 0, NZ, z).reshape(NZ * F)
        bias_fc2 = rel(biases[3 * D + FF :])
        shift_attn, scale_attn, gate_attn, shift_mlp, scale_mlp, gate_mlp = (
            modulation[:, i] for i in range(6)
        )

        block_in = rel(spread(tokens)).astype(f32)
        w_heads = w_qkv.reshape(B, hpt, 3, HD).transpose(0, 2, 1, 3).reshape(B, 3 * HW)
        full_qkv = gather_w(w_heads, True)
        full_proj = gather_w(w_proj, False)
        full_fc1 = gather_w(w_fc1, True)
        full_fc2 = gather_w(w_fc2, False)
        grad_top = rel(spread(cotangent)).astype(f32)

        unit_in, rstd_in = layer_stats(block_in)
        normed = (unit_in * (1.0 + scale_attn) + shift_attn).astype(bf16)
        normed_all = gather_x(normed).reshape(nx * q * L, D)
        T = nx * q * L
        packed = dot(normed_all, full_qkv, ((1,), (0,))).reshape(T, NZ, 3, HW)
        queries = (packed[:, :, 0].reshape(T, NZ * HW) + bias_heads[0]).astype(bf16)
        keys = packed[:, :, 1].reshape(T, NZ * HW).astype(bf16)
        vals = (packed[:, :, 2].reshape(T, NZ * HW) + bias_heads[1]).astype(bf16)

        def by_sample(array):
            return array.reshape(nx, q, L, -1).transpose(1, 0, 2, 3).reshape(q, nx * L, -1)

        def by_rank(array):
            return array.reshape(q, nx, L, -1).transpose(1, 0, 2, 3).reshape(T, -1)

        queries, keys, vals = by_sample(queries), by_sample(keys), by_sample(vals)
        key_vals = jnp.stack([keys, vals])
        other_kv = swap_with(key_vals, "c", NC, 1)
        keys_all = jnp.concatenate([keys, other_kv[0]], axis=1)
        vals_all = jnp.concatenate([vals, other_kv[1]], axis=1)
        mixed, log_norm = attn_forward(queries, keys_all, vals_all, factor)
        mixed_rows = by_rank(mixed)
        branch_part = dot(mixed_rows, full_proj, ((1,), (0,))).reshape(nx, q, L, D)
        branch = reduce_x(branch_part) + bias_proj
        middle = block_in + gate_attn * branch
        unit_mid, rstd_mid = layer_stats(middle)
        normed_mlp = (unit_mid * (1.0 + scale_mlp) + shift_mlp).astype(bf16)
        mlp_all = gather_x(normed_mlp).reshape(T, D)
        hidden = dot(mlp_all, full_fc1, ((1,), (0,))) + bias_fc1
        activated, gelu_pull = jax.vjp(lambda h: jax.nn.gelu(h, approximate=True), hidden)
        act_low = activated.astype(bf16)
        mlp_part = dot(act_low, full_fc2, ((1,), (0,))).reshape(nx, q, L, D)
        branch_mlp = reduce_x(mlp_part) + bias_fc2
        block_out = (middle + gate_mlp * branch_mlp).astype(bf16)
        out = collect(rel(block_out))

        dgate_mlp = jnp.sum(grad_top * branch_mlp, axis=1)
        dbranch_mlp = (gate_mlp * grad_top).astype(bf16)
        g_bfc2 = jnp.sum(dbranch_mlp, axis=(0, 1), dtype=f32)
        dmlp_all = gather_x(dbranch_mlp).reshape(T, D)
        g_fc2 = reduce_w(dot(act_low, dmlp_all, ((0,), (0,))), False)
        dactiv = dot(dmlp_all, full_fc2, ((1,), (1,)))
        dhidden = gelu_pull(dactiv)[0].astype(bf16)
        g_bfc1 = jnp.sum(dhidden, axis=0, dtype=f32)
        g_fc1 = reduce_w(dot(mlp_all, dhidden, ((0,), (0,))), True)
        dnormed_mlp = reduce_x(dot(dhidden, full_fc1, ((1,), (1,))).reshape(nx, q, L, D))
        dshift_mlp = jnp.sum(dnormed_mlp, axis=1)
        dscale_mlp = jnp.sum(dnormed_mlp * unit_mid, axis=1)
        dmiddle = grad_top + layer_back(dnormed_mlp * (1.0 + scale_mlp), unit_mid, rstd_mid)
        dgate_attn = jnp.sum(dmiddle * branch, axis=1)
        dbranch = (gate_attn * dmiddle).astype(bf16)
        g_bproj = jnp.sum(dbranch, axis=(0, 1), dtype=f32)
        dattn_all = gather_x(dbranch).reshape(T, D)
        g_proj = reduce_w(dot(mixed_rows, dattn_all, ((0,), (0,))), False)
        dmixed = by_sample(dot(dattn_all, full_proj, ((1,), (1,))).astype(bf16))
        dq, dk, dv = attn_backward(queries, keys_all, vals_all, dmixed, log_norm, factor)
        half = nx * L
        dkv = jnp.stack([dk, dv])
        got_dkv = swap_with(dkv[:, :, half:].astype(bf16), "c", NC, 1)
        dkv = (dkv[:, :, :half] + got_dkv.astype(f32)).astype(bf16)
        dq = dq.astype(bf16)
        g_bq = jnp.sum(dq, axis=(0, 1), dtype=f32)
        g_bv = jnp.sum(dkv[1], axis=(0, 1), dtype=f32)
        dpacked = jnp.stack(
            [by_rank(v).reshape(T, NZ, HW) for v in (dq, dkv[0], dkv[1])], axis=2
        ).reshape(T, NZ * 3 * HW)
        g_qkv = reduce_w(dot(normed_all, dpacked, ((0,), (0,))), True)
        g_qkv = g_qkv.reshape(B, 3, hpt, HD).transpose(0, 2, 1, 3).reshape(B, hpt, 3 * HD)
        dnormed = reduce_x(dot(dpacked, full_qkv, ((1,), (1,))).reshape(nx, q, L, D))
        dshift_attn = jnp.sum(dnormed, axis=1)
        dscale_attn = jnp.sum(dnormed * unit_in, axis=1)
        dblock = dmiddle + layer_back(dnormed * (1.0 + scale_attn), unit_in, rstd_in)
        d_tokens = collect(rel(dblock.astype(bf16))).astype(f32)

        dmod = jnp.stack(
            [dshift_attn, dscale_attn, dgate_attn, dshift_mlp, dscale_mlp, dgate_mlp], axis=1
        )
        here = (jnp.arange(nx) == x).astype(f32)[:, None]

        def head_bias(vec, width):
            vec = flip_bits(vec.reshape(NZ, 1, width), 0, NZ, z)
            return (vec * here).reshape(NZ * nx * width)

        small = jnp.concatenate(
            [
                rel(dmod).reshape(q * 6 * D),
                head_bias(g_bq, HW),
                head_bias(g_bv, HW),
                rel(g_bproj),
                head_bias(g_bfc1, F),
                rel(g_bfc2),
            ]
        )
        for k in range(1, nx):
            small_k = swap_with(small, "x", nx, k)
            total = small_k if k == 1 else total + small_k
        small = small + total
        small = small + swap_with(small, "c", NC, 1)
        cut = q * 6 * D
        over_z = [small] + [swap_with(small, "z", NZ, k) for k in range(1, NZ)]
        bias_sum = sum(v[cut:] for v in over_z)
        flat = jnp.concatenate([v[:cut] for v in over_z] + [bias_sum])
        over_y = [flat] + [swap_with(flat, "y", ny, k) for k in range(1, ny)]
        bias_sum = sum(v[NZ * cut :] for v in over_y)
        dmod_all = jnp.stack([v[: NZ * cut] for v in over_y]).reshape(ny * NZ * q, 6 * D)

        take = lambda v, n: lax.dynamic_slice_in_dim(v, own * n, n, 0)
        out_bqkv = jnp.stack([take(bias_sum[:D], B), take(bias_sum[D : 2 * D], B)])
        out_bproj = take(bias_sum[2 * D : 3 * D], B)
        out_bfc1 = take(bias_sum[3 * D : 3 * D + FF], FF // dp)
        out_bfc2 = take(bias_sum[3 * D + FF :], B)
        out_bada = take(jnp.sum(dmod_all, axis=0), 6 * D // dp)
        cols = 6 * D // (NZ * nx)
        dmod_cols = lax.dynamic_slice_in_dim(dmod_all, (z * nx + x) * cols, cols, 1)
        act_mine = act_rows.reshape(ny * NZ * q, B)
        out_ada = dot(
            jnp.concatenate([act_mine] * 3),
            jnp.concatenate(split_three(dmod_cols)),
            ((0,), (0,)),
        )
        dact = sum(
            dot(part, w_ada, ((1,), (1,))) for part in split_three(dmod_all)
        ).reshape(ny, NZ, q, B)
        over_y = jnp.stack([dact[0]] + [swap_with(dact[k], "y", ny, k) for k in range(1, ny)])
        over_y = flip_bits(over_y, 1, NZ, z)
        over_y = flip_bits(over_y.reshape(ny, NC, 2 * q, B), 1, NC, c)
        other = swap_with(over_y[:, 1], "c", NC, 1)
        dact_rows = jnp.stack([over_y[:, 0], other], axis=1)
        dact_rows = rel(dact_rows.transpose(2, 0, 1, 3).reshape(ns, D))
        silu_pull = jax.vjp(jax.nn.silu, conditioning.astype(f32))[1]
        d_cond = silu_pull(dact_rows)[0]
        return (
            out,
            d_tokens,
            d_cond,
            g_qkv,
            out_bqkv,
            g_proj,
            out_bproj,
            g_fc1,
            out_bfc1,
            g_fc2,
            out_bfc2,
            out_ada,
            out_bada,
        )

    return body


LOG2E = 1.4426950408889634


def nn(a, b):
    return lax.dot_general(a, b, (((1,), (0,)), ((), ())), preferred_element_type=f32)


def nt(a, b):
    return lax.dot_general(a, b, (((1,), (1,)), ((), ())), preferred_element_type=f32)


def lanes(ref, block, width=256):
    return ref[:, pl.ds(pl.multiple_of(block * width, width), width)]


def total_rows(array):
    return jnp.sum(array, axis=0, keepdims=True)


def whole(shape):
    zeros = (0,) * len(shape)
    return pl.BlockSpec(shape, lambda *_: zeros)


def kernel_call(body, table, operands, in_specs, out_specs, outs, steps=1, scratch=(), flops=0, name=None):
    moved = sum(o.size * o.dtype.itemsize for o in operands)
    listed = outs if isinstance(outs, list) else [outs]
    moved += sum(math.prod(o.shape) * jnp.dtype(o.dtype).itemsize for o in listed)
    return pl.pallas_call(
        body,
        grid_spec=pltpu.PrefetchScalarGridSpec(
            num_scalar_prefetch=1,
            grid=(steps,),
            in_specs=in_specs,
            out_specs=out_specs,
            scratch_shapes=list(scratch),
        ),
        out_shape=outs,
        cost_estimate=pl.CostEstimate(flops=flops // 1000, bytes_accessed=moved // 1000, transcendentals=0),
        name=name,
    )(table, *operands)


def shaped(shape, dtype):
    return jax.ShapeDtypeStruct(shape, dtype)


COLS = 512


def block_spec(rows, cols):
    return pl.BlockSpec((2, 1, rows, cols), lambda j, t: (0, j, 0, 0))


def qkv_specs():
    return [block_spec(128, 384)] * 4


def proj_specs():
    return [pl.BlockSpec((2, 1, 128, 128), lambda j, t: (0, j, 0, 3))] * 4


def halves(refs, kc, ky):
    return jnp.concatenate([refs[kc][ky, 0], refs[2 + kc][ky, 0]], axis=0)


def column_spec(width, rows=256):
    return pl.BlockSpec((rows, width), lambda j, t: (0, j))


PAIRS = [(kc, ky) for kc in range(2) for ky in range(2)]


def mod_kernel(t, act, w_ada, b_ada, b_qkv, b_proj, b_fc1, b_fc2, out):
    own = t[13]

    def placed(vec, count):
        tiled = jnp.concatenate([vec.astype(f32)] * count, axis=1)
        width = vec.shape[1]
        lane = lax.broadcasted_iota(jnp.int32, tiled.shape, 1)
        here = (lane >= own * width) & (lane < own * width + width)
        return jnp.where(here, tiled, 0.0)

    bias_ada = placed(b_ada[...], 4)
    rows = []
    for i in range(6):
        part = slice(i * 1024, (i + 1) * 1024)
        rows.append(nn(act[...], w_ada[:, part]) + bias_ada[:, part])
    tail = [placed(b_proj[...], 4), placed(b_fc2[...], 4), placed(b_qkv[0:1], 4), placed(b_qkv[1:2], 4)]
    fc1 = b_fc1[...].astype(f32)
    tail += [jnp.where(own == r, fc1, 0.0) for r in range(4)]
    tail += [jnp.zeros((1, 1024), f32)] * 2
    for ky in range(2):
        out[ky] = jnp.concatenate([r[ky : ky + 1] for r in rows] + tail, axis=0)


def norm(rows):
    center = rows - jnp.mean(rows, axis=-1, keepdims=True)
    scale = lax.rsqrt(jnp.mean(center * center, axis=-1, keepdims=True) + norm_eps)
    return center * scale, scale


def ln_kernel(t, first, second, mod, out):
    for i, ref in enumerate((first, second)):
        unit, _ = norm(ref[...].astype(f32))
        out[i * 128 : (i + 1) * 128] = (unit * (1.0 + mod[1:2]) + mod[0:1]).astype(bf16)


def dmlp_kernel(t, first, second, mod, out, sums):
    total = jnp.zeros((1, 1024), f32)
    for i, ref in enumerate((first, second)):
        grad = (mod[5:6] * ref[...].astype(f32)).astype(bf16)
        out[i * 128 : (i + 1) * 128] = grad
        total = total + total_rows(grad.astype(f32))
    sums[...] = total


def qkv_kernel(t, x, *refs):
    ws, (bias, q, kv) = refs[:4], refs[4:]
    acc = jnp.zeros((256, 384), f32)
    for kc, ky in PAIRS:
        acc = acc + nn(lanes(x, t[kc * 2 + ky]), halves(ws, kc, ky))
    q[...] = (acc[:, :128] + bias[8:9]).astype(bf16)
    kv[0] = acc[:, 128:256].astype(bf16)
    kv[1] = (acc[:, 256:] + bias[9:10]).astype(bf16)


def attn_kernel(t, q, a, b, c, d, mixed, lse):
    scale = HD**-0.5 * LOG2E
    chunks = (a, b, c, d)
    keys = jnp.concatenate([r[0] for r in chunks], axis=0)
    vals_t = jnp.concatenate([r[1] for r in chunks], axis=0).T
    lane = lax.broadcasted_iota(jnp.int32, (256, 128), 1)
    queries = q[...]
    parts = []
    for h in range(2):
        qm = jnp.where((lane // HD) == h, queries, jnp.zeros_like(queries))
        s = nt(keys, qm)
        top = jnp.max(s, axis=0, keepdims=True)
        p = jnp.exp2((s - top) * scale)
        total = jnp.sum(p, axis=0, keepdims=True)
        o = nn(vals_t, p.astype(bf16)) / total
        parts.append(o[h * HD : (h + 1) * HD])
        lse[0, h : h + 1] = top * scale + jnp.log2(total)
    mixed[...] = jnp.concatenate(parts, axis=0).T.astype(bf16)


def attn_back_kernel(t, q, grad, mixed, lse, a, b, c, d, *refs):
    ws, (dq, near, far) = refs[:4], refs[4:]
    dmixed = jnp.zeros((256, 128), f32)
    for kc, ky in PAIRS:
        dmixed = dmixed + nt(lanes(grad, t[kc * 2 + ky]), unpack_proj(ws, kc, ky))
    factor = HD**-0.5
    scale = factor * LOG2E
    lane = lax.broadcasted_iota(jnp.int32, (256, 128), 1)
    queries, grads = q[...], dmixed.astype(bf16)
    product_t = (grads.astype(f32) * mixed[...].astype(f32)).T
    zero = jnp.zeros_like(queries)
    qms = [jnp.where((lane // HD) == h, queries, zero) for h in range(2)]
    gms = [jnp.where((lane // HD) == h, grads, zero) for h in range(2)]
    deltas = [total_rows(product_t[h * HD : (h + 1) * HD]) for h in range(2)]
    dq_t = [jnp.zeros((128, 256), f32) for _ in range(2)]
    for i, ref in enumerate((a, b, c, d)):
        key, val = ref[0], ref[1]
        key_t = key.T
        dk = jnp.zeros((256, 128), f32)
        dv = jnp.zeros((256, 128), f32)
        for h in range(2):
            p = jnp.exp2(nt(key, qms[h]) * scale - lse[0, h : h + 1])
            ds = (p * (nt(val, gms[h]) - deltas[h])).astype(bf16)
            dv = dv + nn(p.astype(bf16), gms[h])
            dk = dk + nn(ds, qms[h])
            dq_t[h] = dq_t[h] + nn(key_t, ds)
        out = (near, far)[i // 2]
        rows = slice((i % 2) * 256, (i % 2) * 256 + 256)
        out[0, rows] = (dk * factor).astype(bf16)
        out[1, rows] = dv.astype(bf16)
    both = jnp.concatenate([dq_t[h][h * HD : (h + 1) * HD] for h in range(2)], axis=0)
    dq[...] = (both * factor).T.astype(bf16)


def unpack_proj(refs, kc, ky):
    return jnp.concatenate([refs[kc][ky, 0], refs[2 + kc][ky, 0]], axis=1)


def proj_kernel(t, mixed, *refs):
    ws, (out, acc) = refs[:4], refs[4:]
    j = pl.program_id(0)

    @pl.when(j == 0)
    def _():
        acc[...] = jnp.zeros_like(acc)

    for i, (kc, ky) in enumerate(PAIRS):
        acc[i] += nn(mixed[...], unpack_proj(ws, kc, ky))

    @pl.when(j == 3)
    def _():
        for i in range(4):
            out[:, pl.ds(pl.multiple_of(t[i] * 256, 256), 256)] = acc[i].astype(out.dtype)


def mid_kernel(t, first, second, part, got, mod, branch, middle, out):
    for i, ref in enumerate((first, second)):
        rows = slice(i * 128, (i + 1) * 128)
        br = part[rows] + got[rows].astype(f32) + mod[6:7]
        mid = ref[...].astype(f32) + mod[2:3] * br
        unit, _ = norm(mid)
        branch[rows] = br
        middle[rows] = mid
        out[rows] = (unit * (1.0 + mod[4:5]) + mod[3:4]).astype(bf16)


def fc1_kernel(t, x, wo, wt, bias, act, slope):
    j = pl.program_id(0)
    h = jnp.zeros((256, COLS), f32)
    for kc, ky in PAIRS:
        h = h + nn(lanes(x, t[kc * 2 + ky]), (wo, wt)[kc][ky, 0])
    h = h + bias[pl.ds(10 + t[8 + j], 1), :]
    root = 0.7978845608028654
    inner = jnp.tanh(root * h * (1.0 + 0.044715 * h * h))
    half = 0.5 * (1.0 + inner)
    act[...] = (h * half).astype(bf16)
    slope[...] = (half + (0.5 * root) * h * (1.0 - inner * inner) * (1.0 + 3 * 0.044715 * h * h)).astype(bf16)


def fc2_kernel(t, act, wo, wt, out, acc):
    j = pl.program_id(0)

    @pl.when(j == 0)
    def _():
        acc[...] = jnp.zeros_like(acc)

    for i, (kc, ky) in enumerate(PAIRS):
        w = (wo, wt)[kc]
        acc[i] += nn(act[:, :256], w[ky, 0, :, :256]) + nn(act[:, 256:], w[ky, 0, :, 256:])

    @pl.when(j == 3)
    def _():
        for i in range(4):
            out[:, pl.ds(pl.multiple_of(t[i] * 256, 256), 256)] = acc[i].astype(out.dtype)


def mlp_back_kernel(t, grad, slope, w2o, w2t, w1o, w1t, dh, sums, out, acc):
    j = pl.program_id(0)

    @pl.when(j == 0)
    def _():
        acc[...] = jnp.zeros_like(acc)

    left = jnp.zeros((256, 256), f32)
    right = jnp.zeros((256, 256), f32)
    for kc, ky in PAIRS:
        w, g = (w2o, w2t)[kc], lanes(grad, t[kc * 2 + ky])
        left = left + nt(g, w[ky, 0, :, :256])
        right = right + nt(g, w[ky, 0, :, 256:])
    dhidden = (jnp.concatenate([left, right], axis=1) * slope[...].astype(f32)).astype(bf16)
    dh[...] = dhidden
    sums[...] = total_rows(dhidden.astype(f32))
    for i, (kc, ky) in enumerate(PAIRS):
        acc[i] += nt(dhidden, (w1o, w1t)[kc][ky, 0])

    @pl.when(j == 3)
    def _():
        for i in range(4):
            out[:, pl.ds(pl.multiple_of(t[i] * 256, 256), 256)] = acc[i].astype(out.dtype)


def keep_rows(own, other, turned):
    @pl.when(pl.program_id(0) == 0)
    def _():
        for i in range(4):
            part = slice(i * 256, (i + 1) * 256)
            turned[part] = jnp.concatenate([own[:, part], other[:, part]], axis=0).T


def feature_rows(turned, block):
    return turned[pl.ds(pl.multiple_of(block * 256, 256), 256)]


def fc1_grads_kernel(t, xo, xt, dho, dht, keep, send, turned):
    keep_rows(xo, xt, turned)
    dh = jnp.concatenate([dho[...], dht[...]], axis=0)
    for i, (kc, ky) in enumerate(PAIRS):
        (keep, send)[kc][ky, 0] = nn(feature_rows(turned, t[i]), dh).astype(bf16)


def fc2_grads_kernel(t, acto, actt, go, gt, keep, send):
    act_t = jnp.concatenate([acto[...], actt[...]], axis=0).T
    for i, (kc, ky) in enumerate(PAIRS):
        grad = jnp.concatenate([lanes(go, t[i]), lanes(gt, t[i])], axis=0)
        fc2 = nn(act_t, grad).astype(bf16)
        (keep, send)[kc][ky, 0] = jnp.concatenate([fc2[:256], fc2[256:]], axis=1)


def proj_grads_kernel(t, mo, mt, go, gt, keep, send):
    mixed_t = jnp.concatenate([mo[...], mt[...]], axis=0).T
    for i, (kc, ky) in enumerate(PAIRS):
        grad = jnp.concatenate([lanes(go, t[i]), lanes(gt, t[i])], axis=0)
        (keep, send)[kc][ky, 0] = nn(mixed_t, grad).astype(bf16)


def qkv_grads_kernel(t, xo, xt, dpo, dpt, keep0, send0, keep1, send1, turned):
    keep_rows(xo, xt, turned)
    dpacked = jnp.concatenate([dpo[0], dpt[0]], axis=0)
    for i, (kc, ky) in enumerate(PAIRS):
        grad = nn(feature_rows(turned, t[i]), dpacked).astype(bf16)
        (keep0, send0)[kc][ky, 0] = grad[:128]
        (keep1, send1)[kc][ky, 0] = grad[128:]


def dmid_kernel(t, part, got, middle, branch, first, second, mod, dmid, out, sums):
    rows_of = []
    for i, ref in enumerate((first, second)):
        rows = slice(i * 128, (i + 1) * 128)
        dn = part[rows] + got[rows].astype(f32)
        unit, scale = norm(middle[rows])
        grad = dn * (1.0 + mod[4:5])
        back = scale * (
            grad
            - jnp.mean(grad, axis=-1, keepdims=True)
            - unit * jnp.mean(grad * unit, axis=-1, keepdims=True)
        )
        dm = ref[...].astype(f32) + back
        dbranch = (mod[2:3] * dm).astype(bf16)
        dmid[rows] = dm
        out[rows] = dbranch
        rows_of.append(
            [dn, dn * unit, dm * branch[rows], dbranch.astype(f32)]
        )
    sums[...] = jnp.concatenate(
        [total_rows(a) + total_rows(b) for a, b in zip(*rows_of)] + [jnp.zeros((4, 1024), f32)], axis=0
    )


def out_kernel(t, middle, part, got, first, second, mod, out0, out1, sums):
    total = jnp.zeros((1, 1024), f32)
    for i, (ref, out) in enumerate(((first, out0), (second, out1))):
        rows = slice(i * 128, (i + 1) * 128)
        branch = part[rows] + got[rows].astype(f32) + mod[7:8]
        out[...] = (middle[rows] + mod[5:6] * branch).astype(bf16)
        total = total + total_rows(ref[...].astype(f32) * branch)
    sums[...] = total


def qkv_back_kernel(t, dqo, dqt, n0, n1, f0, f1, *refs):
    ws, (packo, packt, sums, outo, outt, acco, acct) = refs[:4], refs[4:]
    j = pl.program_id(0)

    @pl.when(j == 0)
    def _():
        acco[...] = jnp.zeros_like(acco)
        acct[...] = jnp.zeros_like(acct)

    dkv = n0[...].astype(f32) + n1[...].astype(f32) + f0[...].astype(f32) + f1[...].astype(f32)
    dkv = dkv.astype(bf16)
    dqs = (dqo[...], dqt[...])
    packed = [
        jnp.concatenate([dqs[i], dkv[0, i * 256 : i * 256 + 256], dkv[1, i * 256 : i * 256 + 256]], axis=1)
        for i in range(2)
    ]
    packo[0] = packed[0]
    packt[0] = packed[1]
    sums[...] = jnp.concatenate(
        [
            total_rows(dqs[0].astype(f32)) + total_rows(dqs[1].astype(f32)),
            total_rows(dkv[1].astype(f32)),
            jnp.zeros((6, 128), f32),
        ],
        axis=0,
    )
    for i, (kc, ky) in enumerate(PAIRS):
        w = halves(ws, kc, ky)
        acco[i] += nt(packed[0], w)
        acct[i] += nt(packed[1], w)

    @pl.when(j == 3)
    def _():
        for i in range(4):
            where = pl.ds(pl.multiple_of(t[i] * 256, 256), 256)
            outo[:, where] = acco[i]
            outt[:, where] = acct[i].astype(bf16)


def din_kernel(t, part, got, dmid, first, second, mod, out0, out1, sums):
    rows_of = []
    for i, (ref, out) in enumerate(((first, out0), (second, out1))):
        rows = slice(i * 128, (i + 1) * 128)
        dn = part[rows] + got[rows].astype(f32)
        unit, scale = norm(ref[...].astype(f32))
        grad = dn * (1.0 + mod[1:2])
        back = scale * (
            grad
            - jnp.mean(grad, axis=-1, keepdims=True)
            - unit * jnp.mean(grad * unit, axis=-1, keepdims=True)
        )
        out[...] = (dmid[rows] + back).astype(bf16)
        rows_of.append([dn, dn * unit])
    sums[...] = jnp.concatenate([total_rows(a) + total_rows(b) for a, b in zip(*rows_of)], axis=0)


def pack_kernel(t, qkv, proj, fc2, upper, lower, side):
    for i, out in enumerate((upper, lower)):
        rows = qkv[i * 128 : (i + 1) * 128]
        parts = [rows[:, 192 * g + HD * k : 192 * g + HD * k + HD] for k in range(3) for g in range(2)]
        out[0] = jnp.concatenate(parts + [proj[:, i * 128 : (i + 1) * 128]], axis=1)
    side[0] = jnp.concatenate([fc2[:256], fc2[256:]], axis=1)


def assemble_kernel(t, up, up_got, low, low_got, out):
    for i, (own, got) in enumerate(((up, up_got), (low, low_got))):
        rows = own[0].astype(f32) + got[0].astype(f32)
        parts = [rows[:, 128 * k + HD * g : 128 * k + HD * g + HD] for g in range(2) for k in range(3)]
        out[i * 128 : (i + 1) * 128] = jnp.concatenate(parts, axis=1)


def small_kernel(t, din_sums, dgate_mlp, dmid_sums, bfc2, qkv_sums, fc1o, fc1t, out):
    out[...] = jnp.zeros_like(out)
    out[0:2] = din_sums[...]
    out[2:3] = dmid_sums[2:3]
    out[3:5] = dmid_sums[0:2]
    out[5:6] = dgate_mlp[...]
    out[6:7] = dmid_sums[3:4]
    out[7:8] = bfc2[...]
    for j in range(4):
        where = pl.ds(pl.multiple_of(t[4 + j] * 128, 128), 128)
        out[8:10, where] = qkv_sums[0:2, j * 128 : (j + 1) * 128]
        fc1 = fc1o[:, j * COLS : (j + 1) * COLS] + fc1t[:, j * COLS : (j + 1) * COLS]
        for zz in range(4):
            for xx in range(2):
                @pl.when((t[8 + j] == zz) & (t[12] == xx))
                def _(fc1=fc1, zz=zz, xx=xx):
                    out[10 + zz : 11 + zz, xx * COLS : (xx + 1) * COLS] = fc1


def fast_body(
    tokens, conditioning, cotangent, w_qkv, b_qkv, w_proj, b_proj, w_fc1, b_fc1, w_fc2, b_fc2, w_ada, b_ada
):
    y, c = lax.axis_index("y"), lax.axis_index("c")
    z, x = lax.axis_index("z"), lax.axis_index("x")
    z0, z1 = z % 2, z // 2
    D = 1024
    own = y * 2 + c
    blocks = [(y ^ ky) * 2 + (c ^ kc) for kc, ky in PAIRS]
    z_of = [z ^ k1 ^ (2 * k2) for k1 in range(2) for k2 in range(2)]
    table = jnp.stack(blocks + [zz * 2 + x for zz in z_of] + z_of + [x, own]).astype(jnp.int32)
    call = functools.partial(kernel_call)

    def flip(v, axis, count, offset):
        return lax.ppermute(v, axis, [(i, i ^ offset) for i in range(count)])

    def route(k):
        return [
            (cc * 4 + zz, (zz // 2) * 4 + cc * 2 + ((zz % 2) ^ k)) for cc in range(2) for zz in range(4)
        ]

    def spread_parts(array):
        flat = array.reshape(128, 2 * D)
        low, high = flat[:, :D], flat[:, D:]
        return jnp.where(z0 == 0, low, high), jnp.where(z0 == 0, high, low)

    def spread(array):
        return [lax.ppermute(p, ("c", "z"), route(k)) for k, p in enumerate(spread_parts(array))]

    def send_back(pieces):
        return [lax.ppermute(p, ("c", "z"), [(b, a) for a, b in route(k)]) for k, p in enumerate(pieces)]

    def collect(got, dtype, *others):
        got = lax.optimization_barrier((*got, *others))[:2]
        low = jnp.where(z0 == 0, got[0], got[1])
        high = jnp.where(z0 == 0, got[1], got[0])
        return jnp.concatenate([low, high], axis=1).astype(dtype).reshape(128, 2, D)

    def after(value, *others):
        return lax.optimization_barrier((value, *others))[0]

    STEPS = {"near": ("z", 4, 1), "far": ("z", 4, 2), "y": ("y", 2, 1)}

    cut = lax.optimization_barrier

    def widen(v, step, *others):
        v, got = lax.optimization_barrier((v, flip(v, *STEPS[step]), *others))[:2]
        return jnp.concatenate([v, got])

    def both_cores(v):
        v = v.reshape((2, 4) + v.shape[1:])
        return [v, flip(v, "c", 2, 1)]

    def cross(keep, send):
        flat = (8,) + keep.shape[2:]
        return keep.reshape(flat), flip(send.reshape(flat), "c", 2, 1)

    def fold(pair, *others):
        own, got = lax.optimization_barrier((*pair, *others))[:2]
        half = own.shape[0] // 2
        cut = lambda v, k: v[k * half : (k + 1) * half].astype(f32)
        return [(cut(own, k) + cut(got, k)).astype(bf16) for k in range(2)]

    def onward(parts, step):
        return parts[0], flip(parts[1], *STEPS[step])

    def total(pair, *others):
        own, got = lax.optimization_barrier((*pair, *others))[:2]
        v = own.astype(f32) + got.astype(f32)
        return v.reshape(v.shape[-2:])

    cond_c = jnp.stack([conditioning, flip(conditioning, "c", 2, 1)])
    cond_c = jnp.where(c == 0, cond_c, cond_c[::-1])
    cond_all = jnp.stack([cond_c, flip(cond_c, "y", 2, 1)]).reshape(2, 4, D)
    tok_parts = spread_parts(tokens)
    tok = [lax.ppermute(p, ("c", "z"), route(k)) for k, p in enumerate(tok_parts)]
    upper, lower, packed_fc2 = call(
        pack_kernel,
        table,
        [w_qkv.reshape(256, 384), w_proj, w_fc2],
        [whole((256, 384)), whole((128, 256)), whole((512, 256))],
        [whole((1, 128, COLS)), whole((1, 128, COLS)), whole((1, 256, COLS))],
        [shaped((1, 128, COLS), bf16), shaped((1, 128, COLS), bf16), shaped((1, 256, COLS), bf16)],
        name="pack",
    )
    upper = widen(upper, "far")
    upper, lower, cond_all = cut((upper, lower, cond_all))
    got_up, got_low = flip(upper, *STEPS["near"]), flip(lower, *STEPS["far"])
    act_abs = jax.nn.silu(cond_all.astype(f32)).astype(bf16)
    act_abs = lax.dynamic_slice_in_dim(act_abs, own * 256, 256, 2)
    act_here = lax.dynamic_slice_in_dim(act_abs, z, 1, 1)[:, 0]
    packed_mod = call(
        mod_kernel,
        table,
        [
            jnp.pad(act_here, ((0, 6), (0, 0))),
            w_ada,
            b_ada.reshape(1, -1),
            b_qkv,
            b_proj.reshape(1, -1),
            b_fc1.reshape(1, -1),
            b_fc2.reshape(1, -1),
        ],
        [whole((8, 256)), whole((256, 6144)), whole((1, 1536)), whole((2, 256)), whole((1, 256)), whole((1, 1024)), whole((1, 256))],
        whole((2, 16, D)),
        shaped((2, 16, D), f32),
        flops=2 * 8 * 256 * 6144,
        name="modulate",
    )
    upper, got_up, lower, got_low, tok, packed_mod, got_mod = cut(
        (upper, got_up, lower, got_low, tok, packed_mod, flip(packed_mod[1], "y", 2, 1))
    )
    upper, lower = jnp.concatenate([upper, got_up]), jnp.concatenate([lower, got_low])
    mod = packed_mod[0] + got_mod
    mod = mod + flip(mod, "c", 2, 1)
    mod_spec = whole((16, D))

    half, full = whole((128, D)), whole((256, D))
    row_b, row_f = shaped((256, D), bf16), shaped((256, D), f32)
    lower = widen(lower, "near")
    normed = call(ln_kernel, table, [*tok, after(mod, lower)], [half, half, mod_spec], full, row_b, name="norm_in")
    normed_t = flip(normed, "x", 2, 1)
    upper = widen(upper, "y")
    w1 = after(w_fc1[None], lower)
    lower, got_low, w1, got_w1, normed_t = lax.optimization_barrier(
        (lower, flip(lower, *STEPS["y"]), w1, flip(w1, *STEPS["far"]), normed_t)
    )
    lower, w1 = jnp.concatenate([lower, got_low]), jnp.concatenate([w1, got_w1])
    wa = both_cores(upper) + both_cores(after(lower, w1))

    bias_spec = pl.BlockSpec((16, 128), lambda j, t: (0, t[4 + j]))
    pair_spec = pl.BlockSpec((2, 256, 128), lambda j, t: (0, 0, j))

    def make_qkv(rows):
        return call(
            qkv_kernel,
            table,
            [rows, *wa, mod],
            [full, *qkv_specs(), bias_spec],
            [column_spec(128), pair_spec],
            [shaped((256, 512), bf16), shaped((2, 256, 512), bf16)],
            steps=4,
            flops=2 * 256 * 1024 * 1536,
            name="qkv",
        )

    q_o, kv_o = make_qkv(normed)
    far_o = flip(kv_o, "c", 2, 1)
    q_t, kv_t = make_qkv(normed_t)
    far_t = flip(kv_t, "c", 2, 1)
    chunks = [kv_o, kv_t, far_o, far_t]
    w1 = widen(w1, "near", kv_t)
    q_t, w1 = lax.optimization_barrier((q_t, w1))
    lse_spec = pl.BlockSpec((1, 2, 256), lambda j, t: (j, 0, 0))

    def attend(queries):
        return call(
            attn_kernel,
            table,
            [queries, *chunks],
            [column_spec(128)] + [pair_spec] * 4,
            [column_spec(128), lse_spec],
            [shaped((256, 512), bf16), shaped((4, 2, 256), f32)],
            steps=4,
            flops=4 * 256 * 1024 * 64 * 8 * 4,
            name="attend",
        )

    acc_d = pltpu.VMEM((4, 256, 256), f32)

    def project(rows, kind):
        return call(
            proj_kernel,
            table,
            [rows, *wa],
            [column_spec(128), *proj_specs()],
            full,
            shaped((256, D), kind),
            steps=4,
            scratch=[acc_d],
            flops=2 * 256 * 512 * 1024,
            name="project",
        )

    mixed_t, lse_t = attend(q_t)
    cot_parts = spread_parts(after(cotangent, normed))
    cot = [lax.ppermute(after(p, mixed_t), ("c", "z"), route(k)) for k, p in enumerate(cot_parts)]
    w2 = widen(after(packed_fc2, q_t), "far", mixed_t)
    part_t = project(after(mixed_t, w2), bf16)
    got_branch = flip(part_t, "x", 2, 1)
    q_o, part_t = lax.optimization_barrier((q_o, part_t))
    mixed_o, lse_o = attend(q_o)
    w1, w2 = widen(w1, "y", mixed_o), widen(w2, "near", mixed_o)
    dmlp_o, bfc2_sum = call(
        dmlp_kernel,
        table,
        [*cot, after(mod, mixed_o)],
        [half, half, mod_spec],
        [full, whole((1, D))],
        [row_b, shaped((1, D), f32)],
        name="dbranch_mlp",
    )
    dmlp_t = flip(dmlp_o, "x", 2, 1)
    mixed_o, w1, w2, got_branch, dmlp_o = lax.optimization_barrier((mixed_o, w1, w2, got_branch, dmlp_o))
    w1 = both_cores(w1)
    branch, middle, normed_mlp = call(
        mid_kernel,
        table,
        [*tok, project(mixed_o, f32), got_branch, mod],
        [half, half, full, full, mod_spec],
        [full] * 3,
        [row_f, row_f, row_b],
        name="norm_mid",
    )
    mlp_t = flip(normed_mlp, "x", 2, 1)
    wide = shaped((256, 2048), bf16)
    wide_specs = [block_spec(256, COLS)] * 2
    fc1_bias = pl.BlockSpec((16, COLS), lambda j, t: (0, t[12]))

    def up(rows):
        return call(
            fc1_kernel,
            table,
            [rows, *w1, mod],
            [full, *wide_specs, fc1_bias],
            [column_spec(COLS)] * 2,
            [wide, wide],
            steps=4,
            flops=2 * 256 * 1024 * 2048,
            name="up",
        )

    def down(act, kind):
        return call(
            fc2_kernel,
            table,
            [act, *w2],
            [column_spec(COLS), *wide_specs],
            full,
            shaped((256, D), kind),
            steps=4,
            scratch=[acc_d],
            flops=2 * 256 * 1024 * 2048,
            name="down",
        )

    def mlp_back(grad, slope, kind):
        return call(
            mlp_back_kernel,
            table,
            [grad, slope, *w2, *w1],
            [full, column_spec(COLS), *wide_specs, *wide_specs],
            [column_spec(COLS), column_spec(COLS, 1), full],
            [wide, shaped((1, 2048), f32), shaped((256, D), kind)],
            steps=4,
            scratch=[acc_d],
            flops=4 * 256 * 1024 * 2048,
            name="mlp_back",
        )

    act_o, slope_o = up(after(normed_mlp, dmlp_t))
    w2 = both_cores(widen(w2, "y", act_o, mlp_t))
    act_t, slope_t = up(after(mlp_t, act_o))
    dh_t, fc1_t, dn_t = mlp_back(dmlp_t, slope_t, bf16)
    got_dn = flip(dn_t, "x", 2, 1)
    turned = pltpu.VMEM((D, 512), bf16)
    fc2_keep, fc2_send = call(
        fc2_grads_kernel,
        table,
        [act_o, act_t, after(dmlp_o, dn_t), dmlp_t],
        [column_spec(COLS)] * 2 + [full, full],
        [block_spec(256, COLS)] * 2,
        [shaped((2, 4, 256, COLS), bf16)] * 2,
        steps=4,
        flops=4 * 256 * 1024 * 2048,
        name="fc2_grads",
    )
    g_fc2 = cross(fc2_keep, fc2_send)
    dh_o, fc1_o, dn_o = mlp_back(dmlp_o, after(slope_o, fc2_send), f32)
    g_fc2 = fold(g_fc2, dn_o)
    fc1_keep, fc1_send = call(
        fc1_grads_kernel,
        table,
        [normed_mlp, mlp_t, after(dh_o, got_dn, *g_fc2), dh_t],
        [full, full] + [column_spec(COLS)] * 2,
        [block_spec(256, COLS)] * 2,
        [shaped((2, 4, 256, COLS), bf16)] * 2,
        steps=4,
        scratch=[turned],
        flops=4 * 256 * 1024 * 2048,
        name="fc1_grads",
    )
    g_fc1 = cross(fc1_keep, fc1_send)
    g_fc2 = onward(g_fc2, "y")
    dn_o = after(dn_o, fc1_send)

    sums_spec = whole((8, D))
    dmid, dbr_o, dmid_sums = call(
        dmid_kernel,
        table,
        [dn_o, got_dn, middle, branch, *cot, mod],
        [full] * 4 + [half, half, mod_spec],
        [full, full, sums_spec],
        [row_f, row_b, shaped((8, D), f32)],
        name="norm_mid_back",
    )
    dbr_t = flip(dbr_o, "x", 2, 1)
    finish = lambda down_o, got_mlp: call(
        out_kernel,
        table,
        [middle, down_o, got_mlp, *cot, mod],
        [full] * 3 + [half, half, mod_spec],
        [half, half, whole((1, D))],
        [shaped((128, D), bf16)] * 2 + [shaped((1, D), f32)],
        name="finish",
    )

    def attend_back(queries, grad, mixed, lse):
        long_spec = pl.BlockSpec((2, 512, 128), lambda j, t: (0, 0, j))
        return call(
            attn_back_kernel,
            table,
            [queries, grad, mixed, lse, *chunks, *wa],
            [column_spec(128), full, column_spec(128), lse_spec] + [pair_spec] * 4 + proj_specs(),
            [column_spec(128), long_spec, long_spec],
            [shaped((256, 512), bf16), shaped((2, 512, 512), bf16), shaped((2, 512, 512), bf16)],
            steps=4,
            flops=10 * 256 * 1024 * 64 * 8 * 4,
            name="attend_back",
        )

    g_fc1 = fold(g_fc1, dbr_o)
    dq_o, near_o, away_o = attend_back(q_o, after(dbr_o, *g_fc1), mixed_o, lse_o)
    g_fc1 = onward(g_fc1, "y")
    back_o = flip(away_o, "c", 2, 1)
    g_fc2 = fold(g_fc2, away_o)
    dbr_t = after(dbr_t, away_o, *g_fc2)
    g_fc2 = onward(g_fc2, "near")
    p_keep, p_send = call(
        proj_grads_kernel,
        table,
        [mixed_o, mixed_t, dbr_o, dbr_t],
        [column_spec(128)] * 2 + [full, full],
        [block_spec(128, 256)] * 2,
        [shaped((2, 4, 128, 256), bf16)] * 2,
        steps=4,
        flops=4 * 256 * 512 * 1024,
        name="proj_grads",
    )
    g_proj = cross(p_keep, p_send)
    down_t = down(after(act_t, p_send), bf16)
    got_mlp = flip(down_t, "x", 2, 1)
    dbr_t = after(dbr_t, p_send, down_t)
    dq_t, near_t, away_t = attend_back(q_t, dbr_t, mixed_t, lse_t)
    back_t = flip(away_t, "c", 2, 1)
    away_t, got_mlp, g_fc1, g_fc2, g_proj = cut((away_t, got_mlp, g_fc1, g_fc2, g_proj))
    g_fc1, g_fc2, g_proj = (fold(v) for v in (g_fc1, g_fc2, g_proj))
    dq_t = after(dq_t, *g_fc1, *g_fc2, *g_proj)
    g_fc2, g_fc1, g_proj = onward(g_fc2, "far"), onward(g_fc1, "near"), onward(g_proj, "y")
    long_spec = pl.BlockSpec((2, 512, 128), lambda j, t: (0, 0, j))
    pack_spec = pl.BlockSpec((1, 256, 384), lambda j, t: (j, 0, 0))
    pack_o, pack_t, qkv_sums, din_o, din_t = call(
        qkv_back_kernel,
        table,
        [dq_o, dq_t, near_o, near_t, back_o, back_t, *wa],
        [column_spec(128)] * 2 + [long_spec] * 4 + qkv_specs(),
        [pack_spec, pack_spec, pl.BlockSpec((8, 128), lambda j, t: (0, j)), full, full],
        [shaped((4, 256, 384), bf16)] * 2 + [shaped((8, 512), f32), row_f, row_b],
        steps=4,
        scratch=[acc_d, acc_d],
        flops=4 * 256 * 1024 * 1536,
        name="qkv_back",
    )
    got_din = flip(din_t, "x", 2, 1)
    qkv_out = [shaped((2, 4, 128, 384), bf16)] * 4
    k0, s0, k1, s1 = call(
        qkv_grads_kernel,
        table,
        [normed, normed_t, after(pack_o, din_t), pack_t],
        [full, full, pack_spec, pack_spec],
        [block_spec(128, 384)] * 4,
        qkv_out,
        steps=4,
        scratch=[turned],
        flops=4 * 256 * 1024 * 1536,
        name="qkv_grads",
    )
    g_fc1 = fold(g_fc1, s0)
    k0, s0, k1, s1, got_din, g_fc1, g_fc2, g_proj = cut((k0, s0, k1, s1, got_din, g_fc1, g_fc2, g_proj))
    g_up, g_low = cross(k0, s0), cross(k1, s1)
    g_fc1, g_proj = onward(g_fc1, "far"), onward(fold(g_proj), "near")
    act_o = after(act_o, s0, s1)
    down_o, g_up, g_low, got_mlp = cut((down(act_o, f32), g_up, g_low, got_mlp))
    down_o, g_up, g_low = cut((down_o, fold(g_up), fold(g_low)))
    g_up, g_low = onward(g_up, "y"), onward(g_low, "y")
    out0, out1, dgate_mlp = finish(down_o, got_mlp)
    out_got = send_back([out0, out1])
    din_o = after(din_o, dgate_mlp)
    dt0, dt1, din_sums = call(
        din_kernel,
        table,
        [din_o, got_din, dmid, *tok, mod],
        [full] * 3 + [half, half, mod_spec],
        [half, half, whole((2, D))],
        [shaped((128, D), bf16)] * 2 + [shaped((2, D), f32)],
        name="norm_in_back",
    )
    din_sums, g_up, g_fc1, g_proj = cut((din_sums, g_up, g_fc1, g_proj))
    g_up, g_proj = onward(fold(g_up), "near"), onward(fold(g_proj), "far")
    g_fc1, g_fc2 = total(g_fc1), total(g_fc2, din_sums)
    g_fc2 = jnp.concatenate([g_fc2[:, :256], g_fc2[:, 256:]], axis=0)

    small = call(
        small_kernel,
        table,
        [din_sums, dgate_mlp, dmid_sums, bfc2_sum, qkv_sums, fc1_o, fc1_t],
        [whole((2, D)), whole((1, D)), sums_spec, whole((1, D)), whole((8, 512)), whole((1, 2048)), whole((1, 2048))],
        whole((16, D)),
        shaped((16, D), f32),
        name="small",
    )
    def joined(v, got):
        return jnp.concatenate([v[:-10], got[:-10], v[-10:] + got[-10:]])

    small, got, g_up, g_low, g_fc1, g_fc2 = cut((small, flip(small, "x", 2, 1), g_up, g_low, g_fc1, g_fc2))
    small = small + got
    g_up, g_low = onward(fold(g_up), "far"), onward(fold(g_low), "near")
    small, got, out_got = cut((small, flip(small, "c", 2, 1), out_got))
    small = small + got
    small, got, g_up, g_low, g_proj = cut((small, flip(small, "z", 4, 2), g_up, g_low, g_proj))
    small, dt0, dt1 = cut((joined(small, got), dt0, dt1))
    dt_got = send_back([dt0, dt1])
    g_low, g_proj = onward(fold(g_low), "far"), total(g_proj)
    out = collect(out_got, bf16)
    small, got, g_low, out, g_proj = cut((small, flip(small, "z", 4, 1), g_low, out, g_proj))
    small = joined(small, got)
    small, got, dt_got = cut((small, flip(small, "y", 2, 1), dt_got))
    small = joined(small, got)
    d_tokens = collect(dt_got, f32)
    g_qkv = call(
        assemble_kernel,
        table,
        [*g_up, *g_low],
        [whole((1, 128, 384))] * 4,
        whole((256, 384)),
        shaped((256, 384), f32),
        name="assemble",
    ).reshape(256, 2, 3 * HD)
    bias_sum = small[-10:]
    dmod_all = small[:-10].reshape(8, 6 * D)
    take = lambda v, n: lax.dynamic_slice_in_dim(v.reshape(-1), own * n, n, 0)
    out_bproj, out_bfc2 = take(bias_sum[0], 256), take(bias_sum[1], 256)
    out_bqkv = lax.dynamic_slice_in_dim(bias_sum[2:4], own * 256, 256, 1)
    out_bfc1 = take(bias_sum[4:8], 1024)
    out_bada = take(jnp.sum(dmod_all, axis=0), 1536)
    act_rel = jnp.swapaxes(flip_bits(act_abs, 1, 4, z).reshape(2, 2, 2, 256), 1, 2).reshape(8, 256)
    dmod_cols = lax.dynamic_slice_in_dim(dmod_all, (z * 2 + x) * 768, 768, 1)
    out_ada = dot(
        jnp.concatenate([act_rel] * 3), jnp.concatenate(split_three(dmod_cols)), ((0,), (0,))
    )
    dact = dot(jnp.concatenate(split_three(dmod_all)), w_ada, ((1,), (1,)))
    dact = dact[:8] + dact[8:16] + dact[16:]
    dact = jnp.swapaxes(dact.reshape(2, 2, 2, 256), 1, 2).reshape(2, 4, 256)
    dact = flip_bits(dact, 1, 4, z)
    dact = jnp.stack([dact[0], flip(dact[1], "y", 2, 1)]).reshape(2, 2, 2, 256)
    dact = jnp.where(c == 0, dact, dact[:, ::-1])
    dact = jnp.stack([dact[:, 0], flip(dact[:, 1], "c", 2, 1)], axis=1)
    dact = flip_bits(flip_bits(dact, 0, 2, y), 1, 2, c).transpose(2, 0, 1, 3).reshape(2, D)
    d_cond = jax.vjp(jax.nn.silu, conditioning.astype(f32))[1](dact)[0]
    return (
        out,
        d_tokens,
        d_cond,
        g_qkv,
        out_bqkv,
        g_proj,
        out_bproj,
        g_fc1,
        out_bfc1,
        g_fc2,
        out_bfc2,
        out_ada,
        out_bada,
    )


def solution(mesh):
    dp, tensor = mesh.shape["dp"], mesh.shape["tensor"]
    ny, nx = dp // NC, tensor // NZ
    fine = Mesh(mesh.devices.reshape(ny, NC, NZ, nx), ("y", "c", "z", "x"))
    rows, cols = ("y", "c"), ("z", "x")
    placed = (
        P(cols, rows, None),
        P(rows, None),
        P(cols, rows, None),
        P(rows, cols, None),
        P(None, rows),
        P(cols, rows),
        P(rows),
        P(rows, cols),
        P(rows),
        P(cols, rows),
        P(rows),
        P(rows, None),
        P(rows),
    )
    out_placed = (
        P(cols, rows, None),
        P(cols, rows, None),
        P(rows, None),
        P(rows, cols, None),
        P(None, rows),
        P(cols, rows),
        P(rows),
        P(rows, cols),
        P(rows),
        P(cols, rows),
        P(rows),
        P(rows, cols),
        P(rows),
    )
    body = fast_body if (ny, nx) == (2, 2) else make_body(ny, nx)
    return jax.shard_map(
        body, mesh=fine, in_specs=placed, out_specs=out_placed, check_vma=False
    )
```

```python
import functools
import math

import jax
import jax.numpy as jnp
from jax import lax
from jax.experimental import pallas as pl
from jax.experimental.pallas import tpu as pltpu
from jax.sharding import Mesh, PartitionSpec as P

HD = 64
NZ = 4
NC = 2
norm_eps = 1e-06
f32 = jnp.float32
bf16 = jnp.bfloat16


def flip_bits(array, axis, count, index):
    bit = 1
    while bit < count:
        shape = array.shape
        view = array.reshape(
            shape[:axis] + (count // (2 * bit), 2, bit) + shape[axis + 1 :]
        )
        swapped = jnp.flip(view, axis=axis + 1)
        on = ((index // bit) % 2) == 1
        array = jnp.where(on, swapped, view).reshape(shape)
        bit *= 2
    return array


def swap_with(array, axis_name, count, offset):
    return lax.ppermute(array, axis_name, [(i, i ^ offset) for i in range(count)])


def layer_stats(rows):
    center = rows - jnp.mean(rows, axis=-1, keepdims=True)
    scale = lax.rsqrt(jnp.mean(center * center, axis=-1, keepdims=True) + norm_eps)
    return center * scale, scale


def layer_back(grad, unit, scale):
    return scale * (
        grad
        - jnp.mean(grad, axis=-1, keepdims=True)
        - unit * jnp.mean(grad * unit, axis=-1, keepdims=True)
    )


def split_three(values):
    high = lax.reduce_precision(values, 8, 7)
    rest = values - high
    middle = lax.reduce_precision(rest, 8, 7)
    return [part.astype(bf16) for part in (high, middle, rest - middle)]


def dot(a, b, dims):
    return lax.dot_general(a, b, (dims, ((), ())), preferred_element_type=f32)


def attn_forward(queries, keys, values, factor):
    samples, rows, width = queries.shape
    heads = width // HD
    qh = queries.reshape(samples, rows, heads, HD)
    kh = keys.reshape(samples, keys.shape[1], heads, HD)
    vh = values.reshape(samples, keys.shape[1], heads, HD)
    scores = jnp.einsum("sqhe,skhe->shqk", qh, kh, preferred_element_type=f32) * factor
    top = jnp.max(scores, axis=-1, keepdims=True)
    exps = jnp.exp(scores - top)
    total = jnp.sum(exps, axis=-1, keepdims=True)
    probs = (exps / total).astype(bf16)
    mixed = jnp.einsum("shqk,skhe->sqhe", probs, vh, preferred_element_type=f32)
    return mixed.reshape(queries.shape).astype(bf16), (top + jnp.log(total))


def attn_backward(queries, keys, values, grads, log_norm, factor):
    samples, rows, width = queries.shape
    heads = width // HD
    qh = queries.reshape(samples, rows, heads, HD)
    gh = grads.reshape(samples, rows, heads, HD)
    kh = keys.reshape(samples, keys.shape[1], heads, HD)
    vh = values.reshape(samples, keys.shape[1], heads, HD)
    scores = jnp.einsum("sqhe,skhe->shqk", qh, kh, preferred_element_type=f32) * factor
    probs = jnp.exp(scores - log_norm)
    dprobs = jnp.einsum("sqhe,skhe->shqk", gh, vh, preferred_element_type=f32)
    delta = jnp.sum(probs * dprobs, axis=-1, keepdims=True)
    dscores = (probs * (dprobs - delta)).astype(bf16)
    dq = jnp.einsum("shqk,skhe->sqhe", dscores, kh, preferred_element_type=f32) * factor
    dk = jnp.einsum("shqk,sqhe->skhe", dscores, qh, preferred_element_type=f32) * factor
    dv = jnp.einsum("shqk,sqhe->skhe", probs.astype(bf16), gh, preferred_element_type=f32)
    return dq.reshape(queries.shape), dk.reshape(keys.shape), dv.reshape(keys.shape)


def make_body(ny, nx):
    def to_cores(k):
        return [
            (c * NZ + z, (z // 2) * NZ + c * 2 + ((z % 2) ^ k))
            for c in range(NC)
            for z in range(NZ)
        ]

    def body(
        tokens,
        conditioning,
        cotangent,
        w_qkv,
        b_qkv,
        w_proj,
        b_proj,
        w_fc1,
        b_fc1,
        w_fc2,
        b_fc2,
        w_ada,
        b_ada,
    ):
        y, c = lax.axis_index("y"), lax.axis_index("c")
        z, x = lax.axis_index("z"), lax.axis_index("x")
        z0, z1 = z % 2, z // 2
        place, ns, D = tokens.shape
        q = ns // 2
        L = 2 * place
        dp = ny * NC
        B = D // dp
        own = y * NC + c
        hpt = w_qkv.shape[1]
        HW = hpt * HD
        F = w_fc1.shape[1]
        FF = F * NZ * nx
        factor = HD ** (-0.5)

        def rel(array):
            shape = array.shape
            view = array.reshape(shape[:-1] + (ny, NC, B))
            view = flip_bits(view, len(shape) - 1, ny, y)
            view = flip_bits(view, len(shape), NC, c)
            return view.reshape(shape)

        def spread(array):
            view = array.reshape(place, 2, q, D)
            first = jnp.where(z0 == 0, view[:, 0], view[:, 1])
            second = jnp.where(z0 == 0, view[:, 1], view[:, 0])
            got = [
                lax.ppermute(piece, ("c", "z"), to_cores(k))
                for k, piece in enumerate((first, second))
            ]
            return jnp.concatenate([g.transpose(1, 0, 2) for g in got], axis=1)

        def collect(array):
            pieces = [
                array[:, k * place : (k + 1) * place].transpose(1, 0, 2) for k in range(2)
            ]
            got = [
                lax.ppermute(piece, ("c", "z"), [(b, a) for a, b in to_cores(k)])
                for k, piece in enumerate(pieces)
            ]
            first = jnp.where(z0 == 0, got[0], got[1])
            second = jnp.where(z0 == 0, got[1], got[0])
            return jnp.stack([first, second], axis=1).reshape(place, ns, D)

        def gather_x(array):
            return jnp.stack(
                [array] + [swap_with(array, "x", nx, k) for k in range(1, nx)]
            )

        def reduce_x(parts):
            total = parts[0]
            for k in range(1, nx):
                total = total + swap_with(parts[k].astype(bf16), "x", nx, k).astype(f32)
            return total

        def gather_w(shard, by_rows):
            along = 1 if by_rows else 0
            over_z = jnp.concatenate(
                [shard] + [swap_with(shard, "z", NZ, k) for k in range(1, NZ)], axis=along
            )
            over_y = jnp.stack(
                [over_z] + [swap_with(over_z, "y", ny, k) for k in range(1, ny)]
            )
            other = swap_with(over_y, "c", NC, 1)
            if by_rows:
                return jnp.stack([over_y, other], axis=1).reshape(D, shard.shape[1] * NZ)
            pieces = [p for k in range(ny) for p in (over_y[k], other[k])]
            return jnp.concatenate(pieces, axis=1)

        def reduce_w(grad, by_rows):
            if by_rows:
                view = grad.reshape(ny, NC, B, NZ, grad.shape[1] // NZ)
                part = lambda ky, kc, kz: view[ky, kc, :, kz]
            else:
                view = grad.reshape(NZ, grad.shape[0] // NZ, ny, NC, B)
                part = lambda ky, kc, kz: view[kz, :, ky, kc]
            pick = lambda kc: jnp.stack(
                [jnp.stack([part(ky, kc, kz) for kz in range(NZ)]) for ky in range(ny)]
            )
            got = swap_with(pick(1).astype(bf16), "c", NC, 1)
            over_c = pick(0) + got.astype(f32)
            over_y = over_c[0]
            for k in range(1, ny):
                over_y = over_y + swap_with(over_c[k].astype(bf16), "y", ny, k).astype(f32)
            over_z = over_y[0]
            for k in range(1, NZ):
                over_z = over_z + swap_with(over_y[k].astype(bf16), "z", NZ, k).astype(f32)
            return over_z

        cond_c = jnp.stack([conditioning, swap_with(conditioning, "c", NC, 1)])
        cond_c = flip_bits(cond_c, 0, NC, c)
        cond_all = jnp.stack([cond_c] + [swap_with(cond_c, "y", ny, k) for k in range(1, ny)])
        cond_all = flip_bits(cond_all.reshape(ny, NZ, q, D), 1, NZ, z)
        act_all = jax.nn.silu(cond_all.astype(f32)).astype(bf16)
        act_rows = lax.dynamic_slice_in_dim(act_all, own * B, B, 3)

        partial_mod = dot(act_rows[:, 0].reshape(ny * q, B), w_ada, ((1,), (0,)))
        pad = lambda v, n: lax.dynamic_update_slice_in_dim(
            jnp.zeros((n,), f32), v.astype(f32), own * v.shape[0], 0
        )
        partial_mod = partial_mod + pad(b_ada, 6 * D)
        bias_vec = jnp.concatenate(
            [pad(b_qkv[0], D), pad(b_qkv[1], D), pad(b_proj, D), pad(b_fc1, FF), pad(b_fc2, D)]
        )
        partial_mod = partial_mod.reshape(ny, q * 6 * D)
        packed_mod = jnp.concatenate(
            [partial_mod, jnp.broadcast_to(bias_vec, (ny,) + bias_vec.shape)], axis=1
        )
        total_mod = packed_mod[0]
        for k in range(1, ny):
            total_mod = total_mod + swap_with(packed_mod[k], "y", ny, k)
        total_mod = total_mod + swap_with(total_mod, "c", NC, 1)
        modulation = rel(total_mod[: q * 6 * D].reshape(q, 6, 1, D))
        biases = total_mod[q * 6 * D :]
        bias_heads = biases[: 2 * D].reshape(2, NZ, nx, HW)
        bias_heads = lax.dynamic_index_in_dim(bias_heads, x, 2, keepdims=False)
        bias_heads = flip_bits(bias_heads, 1, NZ, z).reshape(2, NZ * HW)
        bias_proj = rel(biases[2 * D : 3 * D])
        bias_fc1 = biases[3 * D : 3 * D + FF].reshape(NZ, nx, F)
        bias_fc1 = lax.dynamic_index_in_dim(bias_fc1, x, 1, keepdims=False)
        bias_fc1 = flip_bits(bias_fc1, 0, NZ, z).reshape(NZ * F)
        bias_fc2 = rel(biases[3 * D + FF :])
        shift_attn, scale_attn, gate_attn, shift_mlp, scale_mlp, gate_mlp = (
            modulation[:, i] for i in range(6)
        )

        block_in = rel(spread(tokens)).astype(f32)
        w_heads = w_qkv.reshape(B, hpt, 3, HD).transpose(0, 2, 1, 3).reshape(B, 3 * HW)
        full_qkv = gather_w(w_heads, True)
        full_proj = gather_w(w_proj, False)
        full_fc1 = gather_w(w_fc1, True)
        full_fc2 = gather_w(w_fc2, False)
        grad_top = rel(spread(cotangent)).astype(f32)

        unit_in, rstd_in = layer_stats(block_in)
        normed = (unit_in * (1.0 + scale_attn) + shift_attn).astype(bf16)
        normed_all = gather_x(normed).reshape(nx * q * L, D)
        T = nx * q * L
        packed = dot(normed_all, full_qkv, ((1,), (0,))).reshape(T, NZ, 3, HW)
        queries = (packed[:, :, 0].reshape(T, NZ * HW) + bias_heads[0]).astype(bf16)
        keys = packed[:, :, 1].reshape(T, NZ * HW).astype(bf16)
        vals = (packed[:, :, 2].reshape(T, NZ * HW) + bias_heads[1]).astype(bf16)

        def by_sample(array):
            return array.reshape(nx, q, L, -1).transpose(1, 0, 2, 3).reshape(q, nx * L, -1)

        def by_rank(array):
            return array.reshape(q, nx, L, -1).transpose(1, 0, 2, 3).reshape(T, -1)

        queries, keys, vals = by_sample(queries), by_sample(keys), by_sample(vals)
        key_vals = jnp.stack([keys, vals])
        other_kv = swap_with(key_vals, "c", NC, 1)
        keys_all = jnp.concatenate([keys, other_kv[0]], axis=1)
        vals_all = jnp.concatenate([vals, other_kv[1]], axis=1)
        mixed, log_norm = attn_forward(queries, keys_all, vals_all, factor)
        mixed_rows = by_rank(mixed)
        branch_part = dot(mixed_rows, full_proj, ((1,), (0,))).reshape(nx, q, L, D)
        branch = reduce_x(branch_part) + bias_proj
        middle = block_in + gate_attn * branch
        unit_mid, rstd_mid = layer_stats(middle)
        normed_mlp = (unit_mid * (1.0 + scale_mlp) + shift_mlp).astype(bf16)
        mlp_all = gather_x(normed_mlp).reshape(T, D)
        hidden = dot(mlp_all, full_fc1, ((1,), (0,))) + bias_fc1
        activated, gelu_pull = jax.vjp(lambda h: jax.nn.gelu(h, approximate=True), hidden)
        act_low = activated.astype(bf16)
        mlp_part = dot(act_low, full_fc2, ((1,), (0,))).reshape(nx, q, L, D)
        branch_mlp = reduce_x(mlp_part) + bias_fc2
        block_out = (middle + gate_mlp * branch_mlp).astype(bf16)
        out = collect(rel(block_out))

        dgate_mlp = jnp.sum(grad_top * branch_mlp, axis=1)
        dbranch_mlp = (gate_mlp * grad_top).astype(bf16)
        g_bfc2 = jnp.sum(dbranch_mlp, axis=(0, 1), dtype=f32)
        dmlp_all = gather_x(dbranch_mlp).reshape(T, D)
        g_fc2 = reduce_w(dot(act_low, dmlp_all, ((0,), (0,))), False)
        dactiv = dot(dmlp_all, full_fc2, ((1,), (1,)))
        dhidden = gelu_pull(dactiv)[0].astype(bf16)
        g_bfc1 = jnp.sum(dhidden, axis=0, dtype=f32)
        g_fc1 = reduce_w(dot(mlp_all, dhidden, ((0,), (0,))), True)
        dnormed_mlp = reduce_x(dot(dhidden, full_fc1, ((1,), (1,))).reshape(nx, q, L, D))
        dshift_mlp = jnp.sum(dnormed_mlp, axis=1)
        dscale_mlp = jnp.sum(dnormed_mlp * unit_mid, axis=1)
        dmiddle = grad_top + layer_back(dnormed_mlp * (1.0 + scale_mlp), unit_mid, rstd_mid)
        dgate_attn = jnp.sum(dmiddle * branch, axis=1)
        dbranch = (gate_attn * dmiddle).astype(bf16)
        g_bproj = jnp.sum(dbranch, axis=(0, 1), dtype=f32)
        dattn_all = gather_x(dbranch).reshape(T, D)
        g_proj = reduce_w(dot(mixed_rows, dattn_all, ((0,), (0,))), False)
        dmixed = by_sample(dot(dattn_all, full_proj, ((1,), (1,))).astype(bf16))
        dq, dk, dv = attn_backward(queries, keys_all, vals_all, dmixed, log_norm, factor)
        half = nx * L
        dkv = jnp.stack([dk, dv])
        got_dkv = swap_with(dkv[:, :, half:].astype(bf16), "c", NC, 1)
        dkv = (dkv[:, :, :half] + got_dkv.astype(f32)).astype(bf16)
        dq = dq.astype(bf16)
        g_bq = jnp.sum(dq, axis=(0, 1), dtype=f32)
        g_bv = jnp.sum(dkv[1], axis=(0, 1), dtype=f32)
        dpacked = jnp.stack(
            [by_rank(v).reshape(T, NZ, HW) for v in (dq, dkv[0], dkv[1])], axis=2
        ).reshape(T, NZ * 3 * HW)
        g_qkv = reduce_w(dot(normed_all, dpacked, ((0,), (0,))), True)
        g_qkv = g_qkv.reshape(B, 3, hpt, HD).transpose(0, 2, 1, 3).reshape(B, hpt, 3 * HD)
        dnormed = reduce_x(dot(dpacked, full_qkv, ((1,), (1,))).reshape(nx, q, L, D))
        dshift_attn = jnp.sum(dnormed, axis=1)
        dscale_attn = jnp.sum(dnormed * unit_in, axis=1)
        dblock = dmiddle + layer_back(dnormed * (1.0 + scale_attn), unit_in, rstd_in)
        d_tokens = collect(rel(dblock.astype(bf16))).astype(f32)

        dmod = jnp.stack(
            [dshift_attn, dscale_attn, dgate_attn, dshift_mlp, dscale_mlp, dgate_mlp], axis=1
        )
        here = (jnp.arange(nx) == x).astype(f32)[:, None]

        def head_bias(vec, width):
            vec = flip_bits(vec.reshape(NZ, 1, width), 0, NZ, z)
            return (vec * here).reshape(NZ * nx * width)

        small = jnp.concatenate(
            [
                rel(dmod).reshape(q * 6 * D),
                head_bias(g_bq, HW),
                head_bias(g_bv, HW),
                rel(g_bproj),
                head_bias(g_bfc1, F),
                rel(g_bfc2),
            ]
        )
        for k in range(1, nx):
            small_k = swap_with(small, "x", nx, k)
            total = small_k if k == 1 else total + small_k
        small = small + total
        small = small + swap_with(small, "c", NC, 1)
        cut = q * 6 * D
        over_z = [small] + [swap_with(small, "z", NZ, k) for k in range(1, NZ)]
        bias_sum = sum(v[cut:] for v in over_z)
        flat = jnp.concatenate([v[:cut] for v in over_z] + [bias_sum])
        over_y = [flat] + [swap_with(flat, "y", ny, k) for k in range(1, ny)]
        bias_sum = sum(v[NZ * cut :] for v in over_y)
        dmod_all = jnp.stack([v[: NZ * cut] for v in over_y]).reshape(ny * NZ * q, 6 * D)

        take = lambda v, n: lax.dynamic_slice_in_dim(v, own * n, n, 0)
        out_bqkv = jnp.stack([take(bias_sum[:D], B), take(bias_sum[D : 2 * D], B)])
        out_bproj = take(bias_sum[2 * D : 3 * D], B)
        out_bfc1 = take(bias_sum[3 * D : 3 * D + FF], FF // dp)
        out_bfc2 = take(bias_sum[3 * D + FF :], B)
        out_bada = take(jnp.sum(dmod_all, axis=0), 6 * D // dp)
        cols = 6 * D // (NZ * nx)
        dmod_cols = lax.dynamic_slice_in_dim(dmod_all, (z * nx + x) * cols, cols, 1)
        act_mine = act_rows.reshape(ny * NZ * q, B)
        out_ada = dot(
            jnp.concatenate([act_mine] * 3),
            jnp.concatenate(split_three(dmod_cols)),
            ((0,), (0,)),
        )
        dact = sum(
            dot(part, w_ada, ((1,), (1,))) for part in split_three(dmod_all)
        ).reshape(ny, NZ, q, B)
        over_y = jnp.stack([dact[0]] + [swap_with(dact[k], "y", ny, k) for k in range(1, ny)])
        over_y = flip_bits(over_y, 1, NZ, z)
        over_y = flip_bits(over_y.reshape(ny, NC, 2 * q, B), 1, NC, c)
        other = swap_with(over_y[:, 1], "c", NC, 1)
        dact_rows = jnp.stack([over_y[:, 0], other], axis=1)
        dact_rows = rel(dact_rows.transpose(2, 0, 1, 3).reshape(ns, D))
        silu_pull = jax.vjp(jax.nn.silu, conditioning.astype(f32))[1]
        d_cond = silu_pull(dact_rows)[0]
        return (
            out,
            d_tokens,
            d_cond,
            g_qkv,
            out_bqkv,
            g_proj,
            out_bproj,
            g_fc1,
            out_bfc1,
            g_fc2,
            out_bfc2,
            out_ada,
            out_bada,
        )

    return body


LOG2E = 1.4426950408889634


def nn(a, b):
    return lax.dot_general(a, b, (((1,), (0,)), ((), ())), preferred_element_type=f32)


def nt(a, b):
    return lax.dot_general(a, b, (((1,), (1,)), ((), ())), preferred_element_type=f32)


def lanes(ref, block, width=256):
    return ref[:, pl.ds(pl.multiple_of(block * width, width), width)]


def total_rows(array):
    return jnp.sum(array, axis=0, keepdims=True)


def whole(shape):
    zeros = (0,) * len(shape)
    return pl.BlockSpec(shape, lambda *_: zeros)


def kernel_call(body, table, operands, in_specs, out_specs, outs, steps=1, scratch=(), flops=0, name=None):
    moved = sum(o.size * o.dtype.itemsize for o in operands)
    listed = outs if isinstance(outs, list) else [outs]
    moved += sum(math.prod(o.shape) * jnp.dtype(o.dtype).itemsize for o in listed)
    return pl.pallas_call(
        body,
        grid_spec=pltpu.PrefetchScalarGridSpec(
            num_scalar_prefetch=1,
            grid=(steps,),
            in_specs=in_specs,
            out_specs=out_specs,
            scratch_shapes=list(scratch),
        ),
        out_shape=outs,
        cost_estimate=pl.CostEstimate(flops=flops // 1000, bytes_accessed=moved // 1000, transcendentals=0),
        name=name,
    )(table, *operands)


def shaped(shape, dtype):
    return jax.ShapeDtypeStruct(shape, dtype)


COLS = 512


def block_spec(rows, cols):
    return pl.BlockSpec((2, 1, rows, cols), lambda j, t: (0, j, 0, 0))


def qkv_specs():
    return [block_spec(128, 384)] * 4


def proj_specs():
    return [pl.BlockSpec((2, 1, 128, 128), lambda j, t: (0, j, 0, 3))] * 4


def halves(refs, kc, ky):
    return jnp.concatenate([refs[kc][ky, 0], refs[2 + kc][ky, 0]], axis=0)


def column_spec(width, rows=256):
    return pl.BlockSpec((rows, width), lambda j, t: (0, j))


PAIRS = [(kc, ky) for kc in range(2) for ky in range(2)]


def mod_kernel(t, act, w_ada, b_ada, b_qkv, b_proj, b_fc1, b_fc2, out):
    own = t[13]

    def placed(vec, count):
        tiled = jnp.concatenate([vec.astype(f32)] * count, axis=1)
        width = vec.shape[1]
        lane = lax.broadcasted_iota(jnp.int32, tiled.shape, 1)
        here = (lane >= own * width) & (lane < own * width + width)
        return jnp.where(here, tiled, 0.0)

    bias_ada = placed(b_ada[...], 4)
    rows = []
    for i in range(6):
        part = slice(i * 1024, (i + 1) * 1024)
        rows.append(nn(act[...], w_ada[:, part]) + bias_ada[:, part])
    tail = [placed(b_proj[...], 4), placed(b_fc2[...], 4), placed(b_qkv[0:1], 4), placed(b_qkv[1:2], 4)]
    fc1 = b_fc1[...].astype(f32)
    tail += [jnp.where(own == r, fc1, 0.0) for r in range(4)]
    tail += [jnp.zeros((1, 1024), f32)] * 2
    for ky in range(2):
        out[ky] = jnp.concatenate([r[ky : ky + 1] for r in rows] + tail, axis=0)


def norm(rows):
    center = rows - jnp.mean(rows, axis=-1, keepdims=True)
    scale = lax.rsqrt(jnp.mean(center * center, axis=-1, keepdims=True) + norm_eps)
    return center * scale, scale


def ln_kernel(t, first, second, mod, out):
    for i, ref in enumerate((first, second)):
        unit, _ = norm(ref[...].astype(f32))
        out[i * 128 : (i + 1) * 128] = (unit * (1.0 + mod[1:2]) + mod[0:1]).astype(bf16)


def dmlp_kernel(t, first, second, mod, out, sums):
    total = jnp.zeros((1, 1024), f32)
    for i, ref in enumerate((first, second)):
        grad = (mod[5:6] * ref[...].astype(f32)).astype(bf16)
        out[i * 128 : (i + 1) * 128] = grad
        total = total + total_rows(grad.astype(f32))
    sums[...] = total


def qkv_kernel(t, x, *refs):
    ws, (bias, q, kv) = refs[:4], refs[4:]
    acc = jnp.zeros((256, 384), f32)
    for kc, ky in PAIRS:
        acc = acc + nn(lanes(x, t[kc * 2 + ky]), halves(ws, kc, ky))
    q[...] = (acc[:, :128] + bias[8:9]).astype(bf16)
    kv[0] = acc[:, 128:256].astype(bf16)
    kv[1] = (acc[:, 256:] + bias[9:10]).astype(bf16)


def attn_kernel(t, q, a, b, c, d, *refs):
    mixed, lse = refs[-4:-2] if len(refs) > 2 else refs
    scale = HD**-0.5 * LOG2E
    chunks = (a, b, c, d)
    keys = jnp.concatenate([r[0] for r in chunks], axis=0)
    vals_t = jnp.concatenate([r[1] for r in chunks], axis=0).T
    lane = lax.broadcasted_iota(jnp.int32, (256, 128), 1)
    queries = q[...]
    parts = []
    for h in range(2):
        qm = jnp.where((lane // HD) == h, queries, jnp.zeros_like(queries))
        s = nt(keys, qm)
        top = jnp.max(s, axis=0, keepdims=True)
        p = jnp.exp2((s - top) * scale)
        total = jnp.sum(p, axis=0, keepdims=True)
        o = nn(vals_t, p.astype(bf16)) / total
        parts.append(o[h * HD : (h + 1) * HD])
        lse[0, h : h + 1] = top * scale + jnp.log2(total)
    rows = jnp.concatenate(parts, axis=0).T.astype(bf16)
    mixed[...] = rows
    if len(refs) > 2:
        add_projection(t, rows, refs[:4], *refs[-2:])


def attn_back_kernel(t, q, grad, mixed, lse, a, b, c, d, *refs):
    ws, (dq, near, far) = refs[:4], refs[4:]
    dmixed = jnp.zeros((256, 128), f32)
    for kc, ky in PAIRS:
        dmixed = dmixed + nt(lanes(grad, t[kc * 2 + ky]), unpack_proj(ws, kc, ky))
    factor = HD**-0.5
    scale = factor * LOG2E
    lane = lax.broadcasted_iota(jnp.int32, (256, 128), 1)
    queries, grads = q[...], dmixed.astype(bf16)
    product_t = (grads.astype(f32) * mixed[...].astype(f32)).T
    zero = jnp.zeros_like(queries)
    qms = [jnp.where((lane // HD) == h, queries, zero) for h in range(2)]
    gms = [jnp.where((lane // HD) == h, grads, zero) for h in range(2)]
    deltas = [total_rows(product_t[h * HD : (h + 1) * HD]) for h in range(2)]
    dq_t = [jnp.zeros((128, 256), f32) for _ in range(2)]
    for i, ref in enumerate((a, b, c, d)):
        key, val = ref[0], ref[1]
        key_t = key.T
        dk = jnp.zeros((256, 128), f32)
        dv = jnp.zeros((256, 128), f32)
        for h in range(2):
            p = jnp.exp2(nt(key, qms[h]) * scale - lse[0, h : h + 1])
            ds = (p * (nt(val, gms[h]) - deltas[h])).astype(bf16)
            dv = dv + nn(p.astype(bf16), gms[h])
            dk = dk + nn(ds, qms[h])
            dq_t[h] = dq_t[h] + nn(key_t, ds)
        out = (near, far)[i // 2]
        rows = slice((i % 2) * 256, (i % 2) * 256 + 256)
        out[0, rows] = (dk * factor).astype(bf16)
        out[1, rows] = dv.astype(bf16)
    both = jnp.concatenate([dq_t[h][h * HD : (h + 1) * HD] for h in range(2)], axis=0)
    dq[...] = (both * factor).T.astype(bf16)


def unpack_proj(refs, kc, ky):
    return jnp.concatenate([refs[kc][ky, 0], refs[2 + kc][ky, 0]], axis=1)


def proj_kernel(t, mixed, *refs):
    add_projection(t, mixed[...], refs[:4], *refs[4:])


def add_projection(t, rows, ws, out, acc):
    j = pl.program_id(0)

    @pl.when(j == 0)
    def _():
        acc[...] = jnp.zeros_like(acc)

    for i, (kc, ky) in enumerate(PAIRS):
        acc[i] += nn(rows, unpack_proj(ws, kc, ky))

    @pl.when(j == 3)
    def _():
        for i in range(4):
            out[:, pl.ds(pl.multiple_of(t[i] * 256, 256), 256)] = acc[i].astype(out.dtype)


def mid_kernel(t, first, second, part, got, mod, branch, middle, out):
    for i, ref in enumerate((first, second)):
        rows = slice(i * 128, (i + 1) * 128)
        br = part[rows] + got[rows].astype(f32) + mod[6:7]
        mid = ref[...].astype(f32) + mod[2:3] * br
        unit, _ = norm(mid)
        branch[rows] = br
        middle[rows] = mid
        out[rows] = (unit * (1.0 + mod[4:5]) + mod[3:4]).astype(bf16)


def fc1_kernel(t, x, wo, wt, bias, act, slope):
    j = pl.program_id(0)
    h = jnp.zeros((256, COLS), f32)
    for kc, ky in PAIRS:
        h = h + nn(lanes(x, t[kc * 2 + ky]), (wo, wt)[kc][ky, 0])
    h = h + bias[pl.ds(10 + t[8 + j], 1), :]
    root = 0.7978845608028654
    inner = jnp.tanh(root * h * (1.0 + 0.044715 * h * h))
    half = 0.5 * (1.0 + inner)
    act[...] = (h * half).astype(bf16)
    slope[...] = (half + (0.5 * root) * h * (1.0 - inner * inner) * (1.0 + 3 * 0.044715 * h * h)).astype(bf16)


def fc2_kernel(t, act, wo, wt, out, acc):
    j = pl.program_id(0)

    @pl.when(j == 0)
    def _():
        acc[...] = jnp.zeros_like(acc)

    for i, (kc, ky) in enumerate(PAIRS):
        w = (wo, wt)[kc]
        acc[i] += nn(act[:, :256], w[ky, 0, :, :256]) + nn(act[:, 256:], w[ky, 0, :, 256:])

    @pl.when(j == 3)
    def _():
        for i in range(4):
            out[:, pl.ds(pl.multiple_of(t[i] * 256, 256), 256)] = acc[i].astype(out.dtype)


def mlp_back_kernel(t, grad, slope, w2o, w2t, w1o, w1t, dh, sums, out, acc):
    j = pl.program_id(0)

    @pl.when(j == 0)
    def _():
        acc[...] = jnp.zeros_like(acc)

    left = jnp.zeros((256, 256), f32)
    right = jnp.zeros((256, 256), f32)
    for kc, ky in PAIRS:
        w, g = (w2o, w2t)[kc], lanes(grad, t[kc * 2 + ky])
        left = left + nt(g, w[ky, 0, :, :256])
        right = right + nt(g, w[ky, 0, :, 256:])
    dhidden = (jnp.concatenate([left, right], axis=1) * slope[...].astype(f32)).astype(bf16)
    dh[...] = dhidden
    sums[...] = total_rows(dhidden.astype(f32))
    for i, (kc, ky) in enumerate(PAIRS):
        acc[i] += nt(dhidden, (w1o, w1t)[kc][ky, 0])

    @pl.when(j == 3)
    def _():
        for i in range(4):
            out[:, pl.ds(pl.multiple_of(t[i] * 256, 256), 256)] = acc[i].astype(out.dtype)


def keep_rows(own, other, turned):
    @pl.when(pl.program_id(0) == 0)
    def _():
        for i in range(4):
            part = slice(i * 256, (i + 1) * 256)
            turned[part] = jnp.concatenate([own[:, part], other[:, part]], axis=0).T


def feature_rows(turned, block):
    return turned[pl.ds(pl.multiple_of(block * 256, 256), 256)]


def fc1_grads_kernel(t, xo, xt, dho, dht, keep, send, turned):
    keep_rows(xo, xt, turned)
    dh = jnp.concatenate([dho[...], dht[...]], axis=0)
    for i, (kc, ky) in enumerate(PAIRS):
        (keep, send)[kc][ky, 0] = nn(feature_rows(turned, t[i]), dh).astype(bf16)


def fc2_grads_kernel(t, acto, actt, go, gt, keep, send):
    act_t = jnp.concatenate([acto[...], actt[...]], axis=0).T
    for i, (kc, ky) in enumerate(PAIRS):
        grad = jnp.concatenate([lanes(go, t[i]), lanes(gt, t[i])], axis=0)
        fc2 = nn(act_t, grad).astype(bf16)
        (keep, send)[kc][ky, 0] = jnp.concatenate([fc2[:256], fc2[256:]], axis=1)


def proj_grads_kernel(t, mo, mt, go, gt, keep, send):
    mixed_t = jnp.concatenate([mo[...], mt[...]], axis=0).T
    for i, (kc, ky) in enumerate(PAIRS):
        grad = jnp.concatenate([lanes(go, t[i]), lanes(gt, t[i])], axis=0)
        (keep, send)[kc][ky, 0] = nn(mixed_t, grad).astype(bf16)


def qkv_grads_kernel(t, xo, xt, dpo, dpt, keep0, send0, keep1, send1, turned):
    keep_rows(xo, xt, turned)
    dpacked = jnp.concatenate([dpo[0], dpt[0]], axis=0)
    for i, (kc, ky) in enumerate(PAIRS):
        grad = nn(feature_rows(turned, t[i]), dpacked).astype(bf16)
        (keep0, send0)[kc][ky, 0] = grad[:128]
        (keep1, send1)[kc][ky, 0] = grad[128:]


def dmid_kernel(t, part, got, middle, branch, first, second, mod, dmid, out, sums):
    rows_of = []
    for i, ref in enumerate((first, second)):
        rows = slice(i * 128, (i + 1) * 128)
        dn = part[rows] + got[rows].astype(f32)
        unit, scale = norm(middle[rows])
        grad = dn * (1.0 + mod[4:5])
        back = scale * (
            grad
            - jnp.mean(grad, axis=-1, keepdims=True)
            - unit * jnp.mean(grad * unit, axis=-1, keepdims=True)
        )
        dm = ref[...].astype(f32) + back
        dbranch = (mod[2:3] * dm).astype(bf16)
        dmid[rows] = dm
        out[rows] = dbranch
        rows_of.append(
            [dn, dn * unit, dm * branch[rows], dbranch.astype(f32)]
        )
    sums[...] = jnp.concatenate(
        [total_rows(a) + total_rows(b) for a, b in zip(*rows_of)] + [jnp.zeros((4, 1024), f32)], axis=0
    )


def out_kernel(t, middle, part, got, first, second, mod, out0, out1, sums):
    total = jnp.zeros((1, 1024), f32)
    for i, (ref, out) in enumerate(((first, out0), (second, out1))):
        rows = slice(i * 128, (i + 1) * 128)
        branch = part[rows] + got[rows].astype(f32) + mod[7:8]
        out[...] = (middle[rows] + mod[5:6] * branch).astype(bf16)
        total = total + total_rows(ref[...].astype(f32) * branch)
    sums[...] = total


def qkv_back_kernel(t, dqo, dqt, n0, n1, f0, f1, *refs):
    ws, (packo, packt, sums, outo, outt, acco, acct) = refs[:4], refs[4:]
    j = pl.program_id(0)

    @pl.when(j == 0)
    def _():
        acco[...] = jnp.zeros_like(acco)
        acct[...] = jnp.zeros_like(acct)

    dkv = n0[...].astype(f32) + n1[...].astype(f32) + f0[...].astype(f32) + f1[...].astype(f32)
    dkv = dkv.astype(bf16)
    dqs = (dqo[...], dqt[...])
    packed = [
        jnp.concatenate([dqs[i], dkv[0, i * 256 : i * 256 + 256], dkv[1, i * 256 : i * 256 + 256]], axis=1)
        for i in range(2)
    ]
    packo[0] = packed[0]
    packt[0] = packed[1]
    sums[...] = jnp.concatenate(
        [
            total_rows(dqs[0].astype(f32)) + total_rows(dqs[1].astype(f32)),
            total_rows(dkv[1].astype(f32)),
            jnp.zeros((6, 128), f32),
        ],
        axis=0,
    )
    for i, (kc, ky) in enumerate(PAIRS):
        w = halves(ws, kc, ky)
        acco[i] += nt(packed[0], w)
        acct[i] += nt(packed[1], w)

    @pl.when(j == 3)
    def _():
        for i in range(4):
            where = pl.ds(pl.multiple_of(t[i] * 256, 256), 256)
            outo[:, where] = acco[i]
            outt[:, where] = acct[i].astype(bf16)


def din_kernel(t, part, got, dmid, first, second, mod, out0, out1, sums):
    rows_of = []
    for i, (ref, out) in enumerate(((first, out0), (second, out1))):
        rows = slice(i * 128, (i + 1) * 128)
        dn = part[rows] + got[rows].astype(f32)
        unit, scale = norm(ref[...].astype(f32))
        grad = dn * (1.0 + mod[1:2])
        back = scale * (
            grad
            - jnp.mean(grad, axis=-1, keepdims=True)
            - unit * jnp.mean(grad * unit, axis=-1, keepdims=True)
        )
        out[...] = (dmid[rows] + back).astype(bf16)
        rows_of.append([dn, dn * unit])
    sums[...] = jnp.concatenate([total_rows(a) + total_rows(b) for a, b in zip(*rows_of)], axis=0)


def pack_kernel(t, qkv, proj, fc2, upper, lower, side):
    for i, out in enumerate((upper, lower)):
        rows = qkv[i * 128 : (i + 1) * 128]
        parts = [rows[:, 192 * g + HD * k : 192 * g + HD * k + HD] for k in range(3) for g in range(2)]
        out[0] = jnp.concatenate(parts + [proj[:, i * 128 : (i + 1) * 128]], axis=1)
    side[0] = jnp.concatenate([fc2[:256], fc2[256:]], axis=1)


def assemble_kernel(t, up, up_got, low, low_got, out):
    for i, (own, got) in enumerate(((up, up_got), (low, low_got))):
        rows = own[0].astype(f32) + got[0].astype(f32)
        parts = [rows[:, 128 * k + HD * g : 128 * k + HD * g + HD] for g in range(2) for k in range(3)]
        out[i * 128 : (i + 1) * 128] = jnp.concatenate(parts, axis=1)


def small_kernel(t, din_sums, dgate_mlp, dmid_sums, bfc2, qkv_sums, fc1o, fc1t, out):
    out[...] = jnp.zeros_like(out)
    out[0:2] = din_sums[...]
    out[2:3] = dmid_sums[2:3]
    out[3:5] = dmid_sums[0:2]
    out[5:6] = dgate_mlp[...]
    out[6:7] = dmid_sums[3:4]
    out[7:8] = bfc2[...]
    for j in range(4):
        where = pl.ds(pl.multiple_of(t[4 + j] * 128, 128), 128)
        out[8:10, where] = qkv_sums[0:2, j * 128 : (j + 1) * 128]
        fc1 = fc1o[:, j * COLS : (j + 1) * COLS] + fc1t[:, j * COLS : (j + 1) * COLS]
        for zz in range(4):
            for xx in range(2):
                @pl.when((t[8 + j] == zz) & (t[12] == xx))
                def _(fc1=fc1, zz=zz, xx=xx):
                    out[10 + zz : 11 + zz, xx * COLS : (xx + 1) * COLS] = fc1


def fast_body(
    tokens, conditioning, cotangent, w_qkv, b_qkv, w_proj, b_proj, w_fc1, b_fc1, w_fc2, b_fc2, w_ada, b_ada
):
    y, c = lax.axis_index("y"), lax.axis_index("c")
    z, x = lax.axis_index("z"), lax.axis_index("x")
    z0, z1 = z % 2, z // 2
    D = 1024
    own = y * 2 + c
    blocks = [(y ^ ky) * 2 + (c ^ kc) for kc, ky in PAIRS]
    z_of = [z ^ k1 ^ (2 * k2) for k1 in range(2) for k2 in range(2)]
    table = jnp.stack(blocks + [zz * 2 + x for zz in z_of] + z_of + [x, own]).astype(jnp.int32)
    call = functools.partial(kernel_call)

    def flip(v, axis, count, offset):
        return lax.ppermute(v, axis, [(i, i ^ offset) for i in range(count)])

    def route(k):
        return [
            (cc * 4 + zz, (zz // 2) * 4 + cc * 2 + ((zz % 2) ^ k)) for cc in range(2) for zz in range(4)
        ]

    def spread_parts(array):
        flat = array.reshape(128, 2 * D)
        low, high = flat[:, :D], flat[:, D:]
        return jnp.where(z0 == 0, low, high), jnp.where(z0 == 0, high, low)

    def spread(array):
        return [lax.ppermute(p, ("c", "z"), route(k)) for k, p in enumerate(spread_parts(array))]

    def send_back(pieces):
        return [lax.ppermute(p, ("c", "z"), [(b, a) for a, b in route(k)]) for k, p in enumerate(pieces)]

    def collect(got, dtype, *others):
        got = lax.optimization_barrier((*got, *others))[:2]
        low = jnp.where(z0 == 0, got[0], got[1])
        high = jnp.where(z0 == 0, got[1], got[0])
        return jnp.concatenate([low, high], axis=1).astype(dtype).reshape(128, 2, D)

    def after(value, *others):
        return lax.optimization_barrier((value, *others))[0]

    STEPS = {"near": ("z", 4, 1), "far": ("z", 4, 2), "y": ("y", 2, 1)}

    cut = lax.optimization_barrier

    def widen(v, step, *others):
        v, got = lax.optimization_barrier((v, flip(v, *STEPS[step]), *others))[:2]
        return jnp.concatenate([v, got])

    def both_cores(v):
        v = v.reshape((2, 4) + v.shape[1:])
        return [v, flip(v, "c", 2, 1)]

    def cross(keep, send):
        flat = (8,) + keep.shape[2:]
        return keep.reshape(flat), flip(send.reshape(flat), "c", 2, 1)

    def fold(pair, *others):
        own, got = lax.optimization_barrier((*pair, *others))[:2]
        half = own.shape[0] // 2
        cut = lambda v, k: v[k * half : (k + 1) * half].astype(f32)
        return [(cut(own, k) + cut(got, k)).astype(bf16) for k in range(2)]

    def onward(parts, step):
        return parts[0], flip(parts[1], *STEPS[step])

    def total(pair, *others):
        own, got = lax.optimization_barrier((*pair, *others))[:2]
        v = own.astype(f32) + got.astype(f32)
        return v.reshape(v.shape[-2:])

    cond_c = jnp.stack([conditioning, flip(conditioning, "c", 2, 1)])
    cond_c = jnp.where(c == 0, cond_c, cond_c[::-1])
    cond_all = jnp.stack([cond_c, flip(cond_c, "y", 2, 1)]).reshape(2, 4, D)
    tok_parts = spread_parts(tokens)
    tok = [lax.ppermute(p, ("c", "z"), route(k)) for k, p in enumerate(tok_parts)]
    upper, lower, packed_fc2 = call(
        pack_kernel,
        table,
        [w_qkv.reshape(256, 384), w_proj, w_fc2],
        [whole((256, 384)), whole((128, 256)), whole((512, 256))],
        [whole((1, 128, COLS)), whole((1, 128, COLS)), whole((1, 256, COLS))],
        [shaped((1, 128, COLS), bf16), shaped((1, 128, COLS), bf16), shaped((1, 256, COLS), bf16)],
        name="pack",
    )
    upper = widen(upper, "far")
    upper, lower, cond_all = cut((upper, lower, cond_all))
    got_up, got_low = flip(upper, *STEPS["near"]), flip(lower, *STEPS["far"])
    act_abs = jax.nn.silu(cond_all.astype(f32)).astype(bf16)
    act_abs = lax.dynamic_slice_in_dim(act_abs, own * 256, 256, 2)
    act_here = lax.dynamic_slice_in_dim(act_abs, z, 1, 1)[:, 0]
    packed_mod = call(
        mod_kernel,
        table,
        [
            jnp.pad(act_here, ((0, 6), (0, 0))),
            w_ada,
            b_ada.reshape(1, -1),
            b_qkv,
            b_proj.reshape(1, -1),
            b_fc1.reshape(1, -1),
            b_fc2.reshape(1, -1),
        ],
        [whole((8, 256)), whole((256, 6144)), whole((1, 1536)), whole((2, 256)), whole((1, 256)), whole((1, 1024)), whole((1, 256))],
        whole((2, 16, D)),
        shaped((2, 16, D), f32),
        flops=2 * 8 * 256 * 6144,
        name="modulate",
    )
    upper, got_up, lower, got_low, tok, packed_mod, got_mod = cut(
        (upper, got_up, lower, got_low, tok, packed_mod, flip(packed_mod[1], "y", 2, 1))
    )
    upper, lower = jnp.concatenate([upper, got_up]), jnp.concatenate([lower, got_low])
    mod = packed_mod[0] + got_mod
    mod = mod + flip(mod, "c", 2, 1)
    mod_spec = whole((16, D))

    half, full = whole((128, D)), whole((256, D))
    row_b, row_f = shaped((256, D), bf16), shaped((256, D), f32)
    lower = widen(lower, "near")
    normed = call(ln_kernel, table, [*tok, after(mod, lower)], [half, half, mod_spec], full, row_b, name="norm_in")
    normed_t = flip(normed, "x", 2, 1)
    upper = widen(upper, "y")
    w1 = after(w_fc1[None], lower)
    lower, got_low, w1, got_w1, normed_t = lax.optimization_barrier(
        (lower, flip(lower, *STEPS["y"]), w1, flip(w1, *STEPS["far"]), normed_t)
    )
    lower, w1 = jnp.concatenate([lower, got_low]), jnp.concatenate([w1, got_w1])
    wa = both_cores(upper) + both_cores(after(lower, w1))

    bias_spec = pl.BlockSpec((16, 128), lambda j, t: (0, t[4 + j]))
    pair_spec = pl.BlockSpec((2, 256, 128), lambda j, t: (0, 0, j))

    def make_qkv(rows):
        return call(
            qkv_kernel,
            table,
            [rows, *wa, mod],
            [full, *qkv_specs(), bias_spec],
            [column_spec(128), pair_spec],
            [shaped((256, 512), bf16), shaped((2, 256, 512), bf16)],
            steps=4,
            flops=2 * 256 * 1024 * 1536,
            name="qkv",
        )

    q_o, kv_o = make_qkv(normed)
    far_o = flip(kv_o, "c", 2, 1)
    q_t, kv_t = make_qkv(normed_t)
    far_t = flip(kv_t, "c", 2, 1)
    chunks = [kv_o, kv_t, far_o, far_t]
    lse_spec = pl.BlockSpec((1, 2, 256), lambda j, t: (j, 0, 0))

    def attend(queries):
        return call(
            attn_kernel,
            table,
            [queries, *chunks],
            [column_spec(128)] + [pair_spec] * 4,
            [column_spec(128), lse_spec],
            [shaped((256, 512), bf16), shaped((4, 2, 256), f32)],
            steps=4,
            flops=4 * 256 * 1024 * 64 * 8 * 4,
            name="attend",
        )

    acc_d = pltpu.VMEM((4, 256, 256), f32)

    def attend_project(queries, kind):
        return call(
            attn_kernel,
            table,
            [queries, *chunks, *wa],
            [column_spec(128)] + [pair_spec] * 4 + proj_specs(),
            [column_spec(128), lse_spec, full],
            [shaped((256, 512), bf16), shaped((4, 2, 256), f32), shaped((256, D), kind)],
            steps=4,
            scratch=[acc_d],
            flops=4 * 256 * 1024 * 64 * 8 * 4,
            name="attend_project",
        )

    def project(rows, kind):
        return call(
            proj_kernel,
            table,
            [rows, *wa],
            [column_spec(128), *proj_specs()],
            full,
            shaped((256, D), kind),
            steps=4,
            scratch=[acc_d],
            flops=2 * 256 * 512 * 1024,
            name="project",
        )

    mixed_t, lse_t, part_t = attend_project(q_t, bf16)
    cot_parts = spread_parts(after(cotangent, normed))
    cot = [lax.ppermute(after(p, mixed_t), ("c", "z"), route(k)) for k, p in enumerate(cot_parts)]
    w2 = widen(after(packed_fc2, q_t), "far", mixed_t)
    got_branch = flip(part_t, "x", 2, 1)
    w1 = widen(w1, "near", mixed_t)
    q_o, part_t, w1, w2 = lax.optimization_barrier((q_o, part_t, w1, w2))
    mixed_o, lse_o = attend(q_o)
    w1, w2 = widen(w1, "y", mixed_o), widen(w2, "near", mixed_o)
    mixed_o, w1, w2, got_branch = lax.optimization_barrier((mixed_o, w1, w2, got_branch))
    part_o = project(mixed_o, f32)
    dmlp_o, bfc2_sum = call(
        dmlp_kernel,
        table,
        [*cot, after(mod, part_o)],
        [half, half, mod_spec],
        [full, whole((1, D))],
        [row_b, shaped((1, D), f32)],
        name="dbranch_mlp",
    )
    dmlp_t = flip(dmlp_o, "x", 2, 1)
    part_o = after(part_o, dmlp_o)
    w1 = both_cores(w1)
    branch, middle, normed_mlp = call(
        mid_kernel,
        table,
        [*tok, part_o, got_branch, mod],
        [half, half, full, full, mod_spec],
        [full] * 3,
        [row_f, row_f, row_b],
        name="norm_mid",
    )
    mlp_t = flip(normed_mlp, "x", 2, 1)
    wide = shaped((256, 2048), bf16)
    wide_specs = [block_spec(256, COLS)] * 2
    fc1_bias = pl.BlockSpec((16, COLS), lambda j, t: (0, t[12]))

    def up(rows):
        return call(
            fc1_kernel,
            table,
            [rows, *w1, mod],
            [full, *wide_specs, fc1_bias],
            [column_spec(COLS)] * 2,
            [wide, wide],
            steps=4,
            flops=2 * 256 * 1024 * 2048,
            name="up",
        )

    def down(act, kind):
        return call(
            fc2_kernel,
            table,
            [act, *w2],
            [column_spec(COLS), *wide_specs],
            full,
            shaped((256, D), kind),
            steps=4,
            scratch=[acc_d],
            flops=2 * 256 * 1024 * 2048,
            name="down",
        )

    def mlp_back(grad, slope, kind):
        return call(
            mlp_back_kernel,
            table,
            [grad, slope, *w2, *w1],
            [full, column_spec(COLS), *wide_specs, *wide_specs],
            [column_spec(COLS), column_spec(COLS, 1), full],
            [wide, shaped((1, 2048), f32), shaped((256, D), kind)],
            steps=4,
            scratch=[acc_d],
            flops=4 * 256 * 1024 * 2048,
            name="mlp_back",
        )

    act_o, slope_o = up(after(normed_mlp, dmlp_t))
    w2 = both_cores(widen(w2, "y", act_o, mlp_t))
    act_t, slope_t = up(after(mlp_t, act_o))
    dh_t, fc1_t, dn_t = mlp_back(dmlp_t, slope_t, bf16)
    got_dn = flip(dn_t, "x", 2, 1)
    turned = pltpu.VMEM((D, 512), bf16)
    fc2_keep, fc2_send = call(
        fc2_grads_kernel,
        table,
        [act_o, act_t, after(dmlp_o, dn_t), dmlp_t],
        [column_spec(COLS)] * 2 + [full, full],
        [block_spec(256, COLS)] * 2,
        [shaped((2, 4, 256, COLS), bf16)] * 2,
        steps=4,
        flops=4 * 256 * 1024 * 2048,
        name="fc2_grads",
    )
    g_fc2 = cross(fc2_keep, fc2_send)
    dh_o, fc1_o, dn_o = mlp_back(dmlp_o, after(slope_o, fc2_send), f32)
    g_fc2 = fold(g_fc2, dn_o)
    fc1_keep, fc1_send = call(
        fc1_grads_kernel,
        table,
        [normed_mlp, mlp_t, after(dh_o, got_dn, *g_fc2), dh_t],
        [full, full] + [column_spec(COLS)] * 2,
        [block_spec(256, COLS)] * 2,
        [shaped((2, 4, 256, COLS), bf16)] * 2,
        steps=4,
        scratch=[turned],
        flops=4 * 256 * 1024 * 2048,
        name="fc1_grads",
    )
    g_fc1 = cross(fc1_keep, fc1_send)
    g_fc2 = onward(g_fc2, "y")
    dn_o = after(dn_o, fc1_send)

    sums_spec = whole((8, D))
    dmid, dbr_o, dmid_sums = call(
        dmid_kernel,
        table,
        [dn_o, got_dn, middle, branch, *cot, mod],
        [full] * 4 + [half, half, mod_spec],
        [full, full, sums_spec],
        [row_f, row_b, shaped((8, D), f32)],
        name="norm_mid_back",
    )
    dbr_t = flip(dbr_o, "x", 2, 1)
    finish = lambda down_o, got_mlp: call(
        out_kernel,
        table,
        [middle, down_o, got_mlp, *cot, mod],
        [full] * 3 + [half, half, mod_spec],
        [half, half, whole((1, D))],
        [shaped((128, D), bf16)] * 2 + [shaped((1, D), f32)],
        name="finish",
    )

    def attend_back(queries, grad, mixed, lse):
        long_spec = pl.BlockSpec((2, 512, 128), lambda j, t: (0, 0, j))
        return call(
            attn_back_kernel,
            table,
            [queries, grad, mixed, lse, *chunks, *wa],
            [column_spec(128), full, column_spec(128), lse_spec] + [pair_spec] * 4 + proj_specs(),
            [column_spec(128), long_spec, long_spec],
            [shaped((256, 512), bf16), shaped((2, 512, 512), bf16), shaped((2, 512, 512), bf16)],
            steps=4,
            flops=10 * 256 * 1024 * 64 * 8 * 4,
            name="attend_back",
        )

    g_fc1 = fold(g_fc1, dbr_o)
    dq_o, near_o, away_o = attend_back(q_o, after(dbr_o, *g_fc1), mixed_o, lse_o)
    g_fc1 = onward(g_fc1, "y")
    back_o = flip(away_o, "c", 2, 1)
    g_fc2 = fold(g_fc2, away_o)
    dbr_t = after(dbr_t, away_o, *g_fc2)
    g_fc2 = onward(g_fc2, "near")
    p_keep, p_send = call(
        proj_grads_kernel,
        table,
        [mixed_o, mixed_t, dbr_o, dbr_t],
        [column_spec(128)] * 2 + [full, full],
        [block_spec(128, 256)] * 2,
        [shaped((2, 4, 128, 256), bf16)] * 2,
        steps=4,
        flops=4 * 256 * 512 * 1024,
        name="proj_grads",
    )
    g_proj = cross(p_keep, p_send)
    down_t = down(after(act_t, p_send), bf16)
    got_mlp = flip(down_t, "x", 2, 1)
    dbr_t = after(dbr_t, p_send, down_t)
    dq_t, near_t, away_t = attend_back(q_t, dbr_t, mixed_t, lse_t)
    back_t = flip(away_t, "c", 2, 1)
    away_t, got_mlp, g_fc1, g_fc2, g_proj = cut((away_t, got_mlp, g_fc1, g_fc2, g_proj))
    g_fc1, g_fc2, g_proj = (fold(v) for v in (g_fc1, g_fc2, g_proj))
    dq_t = after(dq_t, *g_fc1, *g_fc2, *g_proj)
    g_fc2, g_fc1, g_proj = onward(g_fc2, "far"), onward(g_fc1, "near"), onward(g_proj, "y")
    long_spec = pl.BlockSpec((2, 512, 128), lambda j, t: (0, 0, j))
    pack_spec = pl.BlockSpec((1, 256, 384), lambda j, t: (j, 0, 0))
    pack_o, pack_t, qkv_sums, din_o, din_t = call(
        qkv_back_kernel,
        table,
        [dq_o, dq_t, near_o, near_t, back_o, back_t, *wa],
        [column_spec(128)] * 2 + [long_spec] * 4 + qkv_specs(),
        [pack_spec, pack_spec, pl.BlockSpec((8, 128), lambda j, t: (0, j)), full, full],
        [shaped((4, 256, 384), bf16)] * 2 + [shaped((8, 512), f32), row_f, row_b],
        steps=4,
        scratch=[acc_d, acc_d],
        flops=4 * 256 * 1024 * 1536,
        name="qkv_back",
    )
    got_din = flip(din_t, "x", 2, 1)
    qkv_out = [shaped((2, 4, 128, 384), bf16)] * 4
    k0, s0, k1, s1 = call(
        qkv_grads_kernel,
        table,
        [normed, normed_t, after(pack_o, din_t), pack_t],
        [full, full, pack_spec, pack_spec],
        [block_spec(128, 384)] * 4,
        qkv_out,
        steps=4,
        scratch=[turned],
        flops=4 * 256 * 1024 * 1536,
        name="qkv_grads",
    )
    g_fc1 = fold(g_fc1, s0)
    k0, s0, k1, s1, got_din, g_fc1, g_fc2, g_proj = cut((k0, s0, k1, s1, got_din, g_fc1, g_fc2, g_proj))
    g_up, g_low = cross(k0, s0), cross(k1, s1)
    g_fc1, g_proj = onward(g_fc1, "far"), onward(fold(g_proj), "near")
    act_o = after(act_o, s0, s1)
    down_o, g_up, g_low, got_mlp = cut((down(act_o, f32), g_up, g_low, got_mlp))
    down_o, g_up, g_low = cut((down_o, fold(g_up), fold(g_low)))
    g_up, g_low = onward(g_up, "y"), onward(g_low, "y")
    out0, out1, dgate_mlp = finish(down_o, got_mlp)
    out_got = send_back([out0, out1])
    din_o = after(din_o, dgate_mlp)
    dt0, dt1, din_sums = call(
        din_kernel,
        table,
        [din_o, got_din, dmid, *tok, mod],
        [full] * 3 + [half, half, mod_spec],
        [half, half, whole((2, D))],
        [shaped((128, D), bf16)] * 2 + [shaped((2, D), f32)],
        name="norm_in_back",
    )
    din_sums, g_up, g_fc1, g_proj = cut((din_sums, g_up, g_fc1, g_proj))
    g_up, g_proj = onward(fold(g_up), "near"), onward(fold(g_proj), "far")
    g_fc1, g_fc2 = total(g_fc1), total(g_fc2, din_sums)
    g_fc2 = jnp.concatenate([g_fc2[:, :256], g_fc2[:, 256:]], axis=0)

    small = call(
        small_kernel,
        table,
        [din_sums, dgate_mlp, dmid_sums, bfc2_sum, qkv_sums, fc1_o, fc1_t],
        [whole((2, D)), whole((1, D)), sums_spec, whole((1, D)), whole((8, 512)), whole((1, 2048)), whole((1, 2048))],
        whole((16, D)),
        shaped((16, D), f32),
        name="small",
    )
    def joined(v, got):
        return jnp.concatenate([v[:-10], got[:-10], v[-10:] + got[-10:]])

    small, got, g_up, g_low, g_fc1, g_fc2 = cut((small, flip(small, "x", 2, 1), g_up, g_low, g_fc1, g_fc2))
    small = small + got
    g_up, g_low = onward(fold(g_up), "far"), onward(fold(g_low), "near")
    small, got, out_got = cut((small, flip(small, "c", 2, 1), out_got))
    small = small + got
    small, got, g_up, g_low, g_proj = cut((small, flip(small, "z", 4, 2), g_up, g_low, g_proj))
    small, dt0, dt1 = cut((joined(small, got), dt0, dt1))
    dt_got = send_back([dt0, dt1])
    g_low, g_proj = onward(fold(g_low), "far"), total(g_proj)
    out = collect(out_got, bf16)
    small, got, g_low, out, g_proj = cut((small, flip(small, "z", 4, 1), g_low, out, g_proj))
    small = joined(small, got)
    small, got, dt_got = cut((small, flip(small, "y", 2, 1), dt_got))
    small = joined(small, got)
    d_tokens = collect(dt_got, f32)
    g_qkv = call(
        assemble_kernel,
        table,
        [*g_up, *g_low],
        [whole((1, 128, 384))] * 4,
        whole((256, 384)),
        shaped((256, 384), f32),
        name="assemble",
    ).reshape(256, 2, 3 * HD)
    bias_sum = small[-10:]
    dmod_all = small[:-10].reshape(8, 6 * D)
    take = lambda v, n: lax.dynamic_slice_in_dim(v.reshape(-1), own * n, n, 0)
    out_bproj, out_bfc2 = take(bias_sum[0], 256), take(bias_sum[1], 256)
    out_bqkv = lax.dynamic_slice_in_dim(bias_sum[2:4], own * 256, 256, 1)
    out_bfc1 = take(bias_sum[4:8], 1024)
    out_bada = take(jnp.sum(dmod_all, axis=0), 1536)
    act_rel = jnp.swapaxes(flip_bits(act_abs, 1, 4, z).reshape(2, 2, 2, 256), 1, 2).reshape(8, 256)
    dmod_cols = lax.dynamic_slice_in_dim(dmod_all, (z * 2 + x) * 768, 768, 1)
    out_ada = dot(
        jnp.concatenate([act_rel] * 3), jnp.concatenate(split_three(dmod_cols)), ((0,), (0,))
    )
    dact = dot(jnp.concatenate(split_three(dmod_all)), w_ada, ((1,), (1,)))
    dact = dact[:8] + dact[8:16] + dact[16:]
    dact = jnp.swapaxes(dact.reshape(2, 2, 2, 256), 1, 2).reshape(2, 4, 256)
    dact = flip_bits(dact, 1, 4, z)
    dact = jnp.stack([dact[0], flip(dact[1], "y", 2, 1)]).reshape(2, 2, 2, 256)
    dact = jnp.where(c == 0, dact, dact[:, ::-1])
    dact = jnp.stack([dact[:, 0], flip(dact[:, 1], "c", 2, 1)], axis=1)
    dact = flip_bits(flip_bits(dact, 0, 2, y), 1, 2, c).transpose(2, 0, 1, 3).reshape(2, D)
    d_cond = jax.vjp(jax.nn.silu, conditioning.astype(f32))[1](dact)[0]
    return (
        out,
        d_tokens,
        d_cond,
        g_qkv,
        out_bqkv,
        g_proj,
        out_bproj,
        g_fc1,
        out_bfc1,
        g_fc2,
        out_bfc2,
        out_ada,
        out_bada,
    )


def solution(mesh):
    dp, tensor = mesh.shape["dp"], mesh.shape["tensor"]
    ny, nx = dp // NC, tensor // NZ
    fine = Mesh(mesh.devices.reshape(ny, NC, NZ, nx), ("y", "c", "z", "x"))
    rows, cols = ("y", "c"), ("z", "x")
    placed = (
        P(cols, rows, None),
        P(rows, None),
        P(cols, rows, None),
        P(rows, cols, None),
        P(None, rows),
        P(cols, rows),
        P(rows),
        P(rows, cols),
        P(rows),
        P(cols, rows),
        P(rows),
        P(rows, None),
        P(rows),
    )
    out_placed = (
        P(cols, rows, None),
        P(cols, rows, None),
        P(rows, None),
        P(rows, cols, None),
        P(None, rows),
        P(cols, rows),
        P(rows),
        P(rows, cols),
        P(rows),
        P(cols, rows),
        P(rows),
        P(rows, cols),
        P(rows),
    )
    body = fast_body if (ny, nx) == (2, 2) else make_body(ny, nx)
    return jax.shard_map(
        body, mesh=fine, in_specs=placed, out_specs=out_placed, check_vma=False
    )
```
